256 devices in a mesh: aux: 16 (over z, core), pairs: 16 (over x, y).
Axes of the slice: x: 4, y: 4, z: 8, core: 2. Of those that a mesh axis runs over, the one named last changes fastest.
Arguments:
- amplitudes: bfloat16 [32, 256, 256], P(None, 'aux', 'pairs'), may hold values from -6 to 6
- three_index: bfloat16 [448, 256, 256], P('aux'), may hold values from -0.078125 to 0.078125
- virt_energy: float32 [256], replicated, may hold values from 0.2 to 1.5
- pair_energy: float32 [32], replicated, may hold values from -1.5 to -0.3
- owner: int32 [32], replicated, may hold values from 0 to 15, as said below
- partner: int32 [32], replicated, may hold values from 0 to 31, as said below
Outputs:
- blocks: float32 [64, 256, 256], P('pairs', 'aux')
The draws below stay inside these ranges and needn't reach their ends.
Inputs may be any that keep to these rules, and one draw needn't show every extreme that they name: `owner`: no group index is named by more than 4 pairs, and one group is named by exactly 4 pairs. partner[partner[p]] == p for every pair p.
All inputs are finite; a program needn't handle non-finite values.
Results may differ from the reference program's by a relative error of at most 0.0029.
Values may be sent and summed in bfloat16 or wider, within the bound.
No kernel may reach another device: no remote copies, remote signals or barrier semaphores. Data moves between devices by JAX's collectives and lax.ppermute only.
A program may use at most 64 MiB of HBM per device.

```python
import jax
import jax.numpy as jnp
from jax import lax

V = 256
PAIR_DEV = 2
NAUX = 448
PAIRS = 32
CAP = 4
SLOTS = 64


def draw_owner(key, part):
    groups = PAIRS // PAIR_DEV
    key_busy, key_units, key_pairs = jax.random.split(jax.random.fold_in(key, 17), 3)
    busiest = jax.random.randint(key_busy, (), 0, groups)
    unit_ids = jnp.arange(PAIRS, dtype=jnp.int32)
    unit_group = unit_ids // PAIR_DEV
    unit_order = jax.random.permutation(key_units, PAIRS).astype(jnp.int32)
    guarded = (unit_ids == 0) | (unit_ids == PAIRS - 1)
    unit_score = unit_order + jnp.where(unit_group == busiest, PAIRS, 0) + jnp.where(guarded, 2 * PAIRS, 0)
    ranking = jnp.argsort(unit_score, stable=True)
    removed_units = ranking[:PAIR_DEV]
    group_ids = jnp.arange(groups, dtype=jnp.int32)
    removed = jnp.sum((unit_group[removed_units][:, None] == group_ids[None, :]).astype(jnp.int32), axis=0)
    counts = PAIR_DEV - removed + jnp.where(group_ids == busiest, PAIR_DEV, 0)
    cumulative = jnp.cumsum(counts)
    pair_rank = jax.random.permutation(key_pairs, PAIRS).astype(jnp.int32)
    return jnp.sum((cumulative[None, :] <= pair_rank[:, None]).astype(jnp.int32), axis=1).astype(jnp.int32)


def draw_partner(key, part):
    fixed_count = 2 * (PAIRS // 16)
    pair_order = jax.random.permutation(jax.random.fold_in(key, 29), PAIRS).astype(jnp.int32)
    rank_ids = jnp.arange(PAIRS, dtype=jnp.int32)
    mate_rank = jnp.where(rank_ids < fixed_count, rank_ids, fixed_count + (rank_ids - fixed_count ^ 1))
    return jnp.zeros((PAIRS,), jnp.int32).at[pair_order].set(pair_order[mate_rank]).astype(jnp.int32)


def steps_of(key, dims, pieces, smallest, largest):
    def one(dim, blocks):
        heights = jax.random.uniform(jax.random.fold_in(jax.random.fold_in(key, 6), dim), (blocks,), jnp.float32, smallest / len(pieces), largest / len(pieces))
        return jnp.repeat(jnp.exp(heights), dims[dim] // blocks).reshape((-1,) + (1,) * (len(dims) - dim - 1))

    gain = one(*pieces[0])
    for cut in pieces[1:]:
        gain = gain * one(*cut)
    return gain


def scatter_about(stream_key, dims, deviation, most, cuts=(), held_as=jnp.bfloat16):
    values = jax.random.normal(stream_key, dims, jnp.float32) * deviation
    if len(cuts) > 0:
        values = steps_of(stream_key, dims, cuts, -0.22, 0.18) * values
    return jnp.clip(values, min=-most, max=most).astype(held_as)


def setup_inputs(seed: int = 0) -> dict:
    key_of = jax.random.split(jax.random.key(seed), 7)
    amplitudes = scatter_about(key_of[0], (PAIRS, V, V), 1.0, 6.0, ((1, 16), (2, 16)))
    three_index = scatter_about(key_of[1], (NAUX, V, V), (V * 21) ** -0.5, 0.078125, ((0, 16),))
    virt_energy = jnp.clip(jax.random.uniform(key_of[2], (V,), jnp.float32, 0.2, 1.5), 0.2, 1.5)
    pair_energy = jnp.clip(jax.random.uniform(key_of[3], (PAIRS,), jnp.float32, -1.5, -0.3), -1.5, -0.3)
    owner = draw_owner(jax.random.fold_in(key_of[6], 71), 0)
    partner = draw_partner(jax.random.fold_in(key_of[6], 71), 0)
    return {"amplitudes": amplitudes, "three_index": three_index, "virt_energy": virt_energy, "pair_energy": pair_energy, "owner": owner, "partner": partner}


def reference(amplitudes, three_index, virt_energy, pair_energy, owner, partner):
    pair_ids = jnp.arange(PAIRS, dtype=jnp.int32)
    earlier = (owner[None, :] == owner[:, None]) & (pair_ids[None, :] < pair_ids[:, None])
    slot_rank = jnp.sum(earlier.astype(jnp.int32), axis=1).astype(jnp.int32)
    position = (owner * CAP + slot_rank).astype(jnp.int32)
    three_float = three_index.astype(jnp.float32)

    def ladder_one(amp_tile):
        half_product = jnp.einsum("cd,qbd->qcb", amp_tile.astype(jnp.float32), three_float)
        rounded = lax.optimization_barrier(half_product.astype(jnp.bfloat16))
        return jnp.einsum("qac,qcb->ab", three_float, rounded.astype(jnp.float32))

    ladder = lax.map(ladder_one, amplitudes)
    divisor = virt_energy[None, :, None] + virt_energy[None, None, :] - pair_energy[:, None, None]
    scaled = ladder / divisor
    combined = scaled + jnp.swapaxes(scaled[partner], 1, 2)
    blocks = jnp.zeros((SLOTS, V, V), jnp.float32).at[position].set(combined)
    return blocks
```

```python
import jax
import jax.numpy as jnp
from jax import lax
from jax.experimental import pallas as pl
from jax.experimental.pallas import tpu as pltpu
from jax.sharding import PartitionSpec as P


def ladder_kernel(same_ref, pair_e_ref, amp_ref, b_ref, row_e_ref, col_e_ref, out_ref, amp_t, acc):
    step = pl.program_id(0)
    virt = b_ref.shape[1]
    count = b_ref.shape[0]

    @pl.when(step == 0)
    def _():
        for s in range(2):
            amp_t[:, s * virt : (s + 1) * virt] = amp_ref[s].T
        acc[...] = jnp.zeros_like(acc)

    rows = b_ref[...].reshape(count * virt, virt)
    half = jnp.dot(rows, amp_t[...], preferred_element_type=jnp.float32).astype(jnp.bfloat16)
    for s in range(2):
        total = acc[s]
        for k in range(count):
            total += lax.dot_general(
                half[k * virt : (k + 1) * virt, s * virt : (s + 1) * virt],
                b_ref[k],
                (((1,), (1,)), ((), ())),
                preferred_element_type=jnp.float32,
            )
        acc[s] = total

    @pl.when(step == pl.num_programs(0) - 1)
    def _():
        sums = row_e_ref[...] + col_e_ref[...]
        first = acc[0] / (sums - pair_e_ref[0])
        second = acc[1] / (sums - pair_e_ref[1])
        same = same_ref[0] > 0
        first_n = first.T
        second_n = second.T
        blocks = (
            first_n + jnp.where(same, first, second),
            second_n + jnp.where(same, second, first),
        )
        for s in range(2):
            out_ref[:, s] = blocks[s].astype(jnp.bfloat16).reshape(out_ref.shape[0], out_ref.shape[2], virt)


def ladder(same, pair_e, amp, three_index, virt_energy, aux):
    naux, virt, _ = three_index.shape
    count = 4
    smem = pl.BlockSpec(memory_space=pltpu.SMEM)
    return pl.pallas_call(
        ladder_kernel,
        grid=(naux // count,),
        in_specs=[
            smem,
            smem,
            pl.BlockSpec((2, virt, virt), lambda i: (0, 0, 0)),
            pl.BlockSpec((count, virt, virt), lambda i: (i, 0, 0)),
            pl.BlockSpec((virt, 1), lambda i: (0, 0)),
            pl.BlockSpec((1, virt), lambda i: (0, 0)),
        ],
        out_specs=pl.BlockSpec((aux, 2, virt // aux, virt), lambda i: (0, 0, 0, 0)),
        out_shape=jax.ShapeDtypeStruct((aux, 2, virt // aux, virt), jnp.bfloat16),
        scratch_shapes=[
            pltpu.VMEM((virt, 2 * virt), jnp.bfloat16),
            pltpu.VMEM((2, virt, virt), jnp.float32),
        ],
        name="ladder",
    )(same, pair_e, amp, three_index, virt_energy[:, None], virt_energy[None, :])


def per_device(amplitudes, three_index, virt_energy, pair_energy, owner, partner):
    aux = lax.axis_size("aux")
    groups = lax.axis_size("pairs")
    my_group = lax.axis_index("pairs")
    pairs_all = owner.shape[0]
    rows, cols = amplitudes.shape[1:]
    virt = three_index.shape[1]
    capacity = 2 * (pairs_all // groups)
    ids = jnp.arange(pairs_all, dtype=jnp.int32)
    before = ids[None, :] < ids[:, None]
    leads = partner > ids
    fixed = partner == ids
    low = jnp.minimum(ids, partner)
    lead_rank = jnp.sum((leads[None, :] & (ids[None, :] < low[:, None])).astype(jnp.int32), axis=1)
    fixed_rank = jnp.sum((fixed[None, :] & before).astype(jnp.int32), axis=1)
    leaders = jnp.sum(leads.astype(jnp.int32))
    place = jnp.where(fixed, 2 * leaders + fixed_rank, 2 * lead_rank + (ids > partner))
    pick = place[None, :] == ids[:, None]
    outgoing = jnp.dot(
        pick.astype(jnp.bfloat16),
        amplitudes.reshape(pairs_all, rows * cols),
        preferred_element_type=jnp.float32,
    ).astype(jnp.bfloat16)
    outgoing = jnp.broadcast_to(
        outgoing.reshape(1, groups, 2, rows * cols), (aux, groups, 2, rows * cols)
    ).reshape(aux * groups, 2, rows * cols)
    arrived = lax.all_to_all(outgoing, ("aux", "pairs"), split_axis=0, concat_axis=0, tiled=True)
    amp = arrived.reshape(aux, groups, 2, rows, cols).transpose(2, 0, 3, 1, 4).reshape(2, virt, virt)
    mine = pick & (ids[:, None] // 2 == my_group)
    pair_e = jnp.sum(jnp.where(mine, pair_energy[None, :], 0.0), axis=1).reshape(groups, 2).sum(axis=0)
    same = (my_group >= leaders).astype(jnp.int32).reshape(1)
    partial = ladder(same, pair_e, amp, three_index, virt_energy, aux)
    shares = lax.all_to_all(partial, "aux", split_axis=0, concat_axis=0, tiled=True)
    done = jnp.sum(shares.astype(jnp.float32), axis=0).astype(jnp.bfloat16)
    spread = jnp.broadcast_to(done[None], (groups,) + done.shape)
    found = lax.all_to_all(spread, "pairs", split_axis=0, concat_axis=0, tiled=True)
    found = found.reshape(pairs_all, rows * virt)
    earlier = (owner[None, :] == owner[:, None]) & before
    position = owner * capacity + jnp.sum(earlier.astype(jnp.int32), axis=1)
    own_ids = my_group * capacity + jnp.arange(capacity, dtype=jnp.int32)
    own_link = (position[None, :] == own_ids[:, None])
    own_place = jnp.sum(jnp.where(own_link, place[None, :] + 1, 0), axis=1) - 1
    take = (own_place[:, None] == ids[None, :]).astype(jnp.bfloat16)
    return jnp.dot(take, found, preferred_element_type=jnp.float32).reshape(capacity, rows, virt)


def solution(mesh):
    placed = (P(None, "aux", "pairs"), P("aux", None, None), P(), P(), P(), P())
    return jax.shard_map(
        per_device, mesh=mesh, in_specs=placed, out_specs=P("pairs", "aux", None), check_vma=False
    )
```

```python
import jax
import jax.numpy as jnp
from jax import lax
from jax.experimental import pallas as pl
from jax.experimental.pallas import tpu as pltpu
from jax.sharding import Mesh
from jax.sharding import PartitionSpec as P

BF16 = jnp.bfloat16
F32 = jnp.float32
NT = (((1,), (1,)), ((), ()))
VMEM_SPEC = pl.BlockSpec(memory_space=pltpu.VMEM)


def in_vmem(x):
    return pltpu.with_memory_space_constraint(x, pltpu.VMEM)


def iota(shape, dim):
    return lax.broadcasted_iota(jnp.int32, shape, dim)


def swap_matrix(side):
    full = side * side
    turned = (iota((full, full), 0) % side) * side + iota((full, full), 0) // side
    return jnp.where(turned == iota((full, full), 1), 1.0, 0.0).astype(BF16)


def plan_kernel(group_ref, amp_ref, partner_ref, owner_ref, energy_ref, out_ref, take_ref, info_ref, *, side, capacity):
    count = partner_ref.shape[1]
    square = (count, count)
    group = group_ref[...]
    row = iota(square, 0)
    col = iota(square, 1)
    diagonal = row == col
    partner = jnp.broadcast_to(partner_ref[...], square)
    owner = jnp.broadcast_to(owner_ref[...], square)

    def down(x):
        return jnp.sum(jnp.where(diagonal, x, 0), axis=1, keepdims=True)

    leads = (partner > col).astype(jnp.int32)
    fixed = (partner == col).astype(jnp.int32)
    low = jnp.minimum(partner, col)
    lead_rank = jnp.sum(jnp.where(row < low, down(leads), 0), axis=0, keepdims=True)
    fixed_rank = jnp.sum(jnp.where(row < col, down(fixed), 0), axis=0, keepdims=True)
    leaders = jnp.sum(leads[:1], axis=1, keepdims=True)
    late = (col[:1] > partner[:1]).astype(jnp.int32)
    place = jnp.where(fixed[:1] > 0, 2 * leaders + fixed_rank, 2 * lead_rank + late)
    pick = jnp.where(jnp.broadcast_to(place, square) == row, 1.0, 0.0).astype(BF16)
    tiles = lax.dot_general(pick, amp_ref[...], NT, preferred_element_type=F32).astype(BF16)
    out_ref[...] = jnp.dot(tiles, swap_matrix(side), preferred_element_type=F32).astype(BF16)
    slot_rank = jnp.sum(((down(owner) == owner) & (row < col)).astype(jnp.int32), axis=0, keepdims=True)
    position = owner_ref[...] * capacity + slot_rank
    small = (8, count)
    wanted = iota(small, 0) + capacity * jnp.broadcast_to(group[:1, :count], small)
    mine = jnp.where(jnp.broadcast_to(position, small) == wanted, 1.0, 0.0).astype(BF16)
    take_ref[...] = lax.dot_general(mine, pick, NT, preferred_element_type=F32).astype(BF16)
    slots = iota(small, 0) + 2 * jnp.broadcast_to(group[:1, :count], small)
    chosen = jnp.where(jnp.broadcast_to(place, small) == slots, jnp.broadcast_to(energy_ref[...], small), 0.0)
    energies = jnp.broadcast_to(jnp.sum(chosen, axis=1, keepdims=True), (8, 128))
    same = jnp.where(group >= jnp.broadcast_to(leaders, (8, 128)), 1.0, 0.0)
    info_ref[...] = jnp.where(iota((8, 128), 0) == 2, same, energies)


def plan(amplitudes, partner, owner, pair_energy, group, capacity):
    count, side, _ = amplitudes.shape
    amp = jnp.transpose(amplitudes, (1, 2, 0)).reshape(side * side, count)
    return pl.pallas_call(
        lambda *refs: plan_kernel(*refs, side=side, capacity=capacity),
        in_specs=[VMEM_SPEC] * 5,
        out_specs=[VMEM_SPEC] * 3,
        out_shape=[
            jax.ShapeDtypeStruct((count, side * side), BF16),
            jax.ShapeDtypeStruct((8, count), BF16),
            jax.ShapeDtypeStruct((8, 128), F32),
        ],
        compiler_params=pltpu.CompilerParams(vmem_limit_bytes=8 << 20),
        name="plan",
    )(
        jnp.full((8, 128), group, jnp.int32),
        amp,
        partner.reshape(1, count),
        owner.reshape(1, count),
        pair_energy.reshape(1, count),
    )


def ladder_kernel(core_ref, info_ref, virt_ref, own_ref, other_ref, b_ref, out_ref, turned, *, side):
    virt = b_ref.shape[1]
    naux = b_ref.shape[0]
    half_lanes = virt // 2
    per_vector = half_lanes // side
    first_core = jnp.broadcast_to(core_ref[:1, :] == 0, (side, half_lanes))

    def piece(slot, z, core, half):
        rows = pl.ds(z * side, side)
        lanes = pl.ds(half * half_lanes, half_lanes)
        own = own_ref[slot, rows, lanes].astype(F32)
        other = other_ref[slot, rows, lanes].astype(F32)
        return jnp.where(first_core, own, other) if core == 0 else jnp.where(first_core, other, own)

    order = [(slot, half, high) for slot in range(2) for half in range(2) for high in range(2)]
    vectors = []
    for low in range(per_vector):
        z_low, core = low // 2, low % 2
        vectors.append(
            jnp.concatenate(
                [piece(slot, high * (per_vector // 2) + z_low, core, half) for slot, half, high in order], axis=0
            )
        )
    lane_group = iota(vectors[0].shape, 1) // side
    step = 1
    while step < per_vector:
        keep = (lane_group & step) == 0
        shift = step * side
        for i in range(per_vector):
            if i & step:
                continue
            j = i | step
            a, b = vectors[i], vectors[j]
            vectors[i] = jnp.where(keep, a, pltpu.roll(b, shift, 1))
            vectors[j] = jnp.where(keep, pltpu.roll(a, half_lanes - shift, 1), b)
        step *= 2
    for s_low in range(per_vector):
        vector = vectors[s_low].astype(BF16)
        for k, (slot, half, high) in enumerate(order):
            rows = pl.ds((half * per_vector + s_low) * side, side)
            lanes = pl.ds(slot * virt + high * half_lanes, half_lanes)
            turned[rows, lanes] = vector[k * side : (k + 1) * side]
    amp_t = jnp.dot(swap_matrix(side), turned[...], preferred_element_type=F32).astype(BF16)

    half = jnp.dot(
        b_ref[...].reshape(naux * virt, virt), amp_t, preferred_element_type=F32
    ).astype(BF16)
    totals = []
    for slot in range(2):
        total = jnp.zeros((virt, virt), F32)
        for q in range(naux):
            total += lax.dot_general(
                half[q * virt : (q + 1) * virt, slot * virt : (slot + 1) * virt],
                b_ref[q],
                NT,
                preferred_element_type=F32,
            )
        totals.append(total)

    rows_of = jnp.broadcast_to(virt_ref[...], (virt, virt))
    sums = rows_of + rows_of.T
    info = info_ref[...]
    first = totals[0] / (sums - info[0:1, 0:1])
    second = totals[1] / (sums - info[1:2, 0:1])
    same = jnp.broadcast_to(info[2:3, 0:1] > 0.5, (virt, virt))
    blocks = (first.T + jnp.where(same, first, second), second.T + jnp.where(same, second, first))
    share = out_ref.shape[2]
    for slot in range(2):
        out_ref[:, slot] = blocks[slot].astype(BF16).reshape(virt // share, share, virt)


def ladder(core, info, virt_energy, own, other, three_index, aux, side):
    virt = three_index.shape[1]
    return pl.pallas_call(
        lambda *refs: ladder_kernel(*refs, side=side),
        in_specs=[VMEM_SPEC] * 6,
        out_specs=VMEM_SPEC,
        out_shape=jax.ShapeDtypeStruct((aux, 2, virt // aux, virt), BF16),
        scratch_shapes=[pltpu.VMEM((virt, 2 * virt), BF16)],
        compiler_params=pltpu.CompilerParams(vmem_limit_bytes=40 << 20),
        name="ladder",
    )(
        jnp.full((8, 128), core, jnp.int32),
        info,
        virt_energy.reshape(1, virt),
        own,
        other,
        in_vmem(three_index),
    )


def gather_kernel(shares_ref, out_ref):
    total = shares_ref[0].astype(F32)
    for k in range(1, shares_ref.shape[0]):
        total += shares_ref[k].astype(F32)
    done = total.astype(BF16)
    for k in range(out_ref.shape[0]):
        out_ref[k] = done


def gather(shares, groups):
    return pl.pallas_call(
        gather_kernel,
        in_specs=[VMEM_SPEC],
        out_specs=VMEM_SPEC,
        out_shape=jax.ShapeDtypeStruct((groups,) + shares.shape[1:], BF16),
        compiler_params=pltpu.CompilerParams(vmem_limit_bytes=8 << 20),
        name="gather",
    )(shares)


def per_device(amplitudes, three_index, virt_energy, pair_energy, owner, partner):
    aux_axes = ("z", "core")
    aux = lax.axis_size(aux_axes)
    depth = lax.axis_size("z")
    groups = lax.axis_size("pairs")
    pairs_all, side, _ = amplitudes.shape
    virt = three_index.shape[1]
    capacity = 2 * (pairs_all // groups)
    tiles, take, info = plan(amplitudes, partner, owner, pair_energy, lax.axis_index("pairs"), capacity)
    outgoing = jnp.broadcast_to(
        tiles.reshape(1, groups, 2, side * side), (depth, groups, 2, side * side)
    ).reshape(depth * groups, 2, side * side)
    arrived = lax.all_to_all(outgoing, ("z", "pairs"), split_axis=0, concat_axis=0, tiled=True)
    own = jnp.transpose(arrived, (1, 0, 2))
    other = lax.ppermute(own, "core", [(0, 1), (1, 0)])
    partial = ladder(lax.axis_index("core"), info, virt_energy, own, other, three_index, aux, side)
    shares = lax.all_to_all(partial, aux_axes, split_axis=0, concat_axis=0, tiled=True)
    spread = gather(shares, groups)
    found = lax.all_to_all(spread, "pairs", split_axis=0, concat_axis=0, tiled=True)
    found = found.reshape(pairs_all, side * virt)
    return jnp.dot(take[:capacity], found, preferred_element_type=F32).reshape(capacity, side, virt)


def solution(mesh):
    groups = mesh.shape["pairs"]
    devices = mesh.devices.reshape(mesh.shape["aux"] // 2, 2, groups)
    split = Mesh(devices, ("z", "core", "pairs"))
    aux = ("z", "core")
    placed = (P(None, aux, "pairs"), P(aux, None, None), P(), P(), P(), P())
    return jax.shard_map(
        per_device, mesh=split, in_specs=placed, out_specs=P("pairs", aux, None), check_vma=False
    )
```

```python
import jax
import jax.numpy as jnp
from jax import lax
from jax.experimental import pallas as pl
from jax.experimental.pallas import tpu as pltpu
from jax.sharding import Mesh
from jax.sharding import PartitionSpec as P

BF16 = jnp.bfloat16
F32 = jnp.float32
NT = (((1,), (1,)), ((), ()))
HEAD = 8
HEAD_PARTS = 2
REST_PARTS = 4
VMEM_SPEC = pl.BlockSpec(memory_space=pltpu.VMEM)
HBM_SPEC = pl.BlockSpec(memory_space=pltpu.HBM)


def in_hbm(x):
    return pltpu.with_memory_space_constraint(x, pltpu.HBM)


def iota(shape, dim):
    return lax.broadcasted_iota(jnp.int32, shape, dim)


def swap_matrix(side):
    full = side * side
    turned = (iota((full, full), 0) % side) * side + iota((full, full), 0) // side
    return jnp.where(turned == iota((full, full), 1), 1.0, 0.0).astype(BF16)


def plan_kernel(
    group_ref,
    amp_hbm,
    partner_hbm,
    owner_hbm,
    energy_hbm,
    virt_hbm,
    three_hbm,
    out_ref,
    info_ref,
    virt_ref,
    head_ref,
    amp_ref,
    partner_ref,
    owner_ref,
    energy_ref,
    sems,
    *,
    side,
    capacity,
):
    sources = (partner_hbm, owner_hbm, amp_hbm, energy_hbm, virt_hbm)
    targets = (partner_ref, owner_ref, amp_ref, energy_ref, virt_ref)
    copies = [pltpu.make_async_copy(a, b, sems.at[i]) for i, (a, b) in enumerate(zip(sources, targets))]
    part = head_ref.shape[0] // HEAD_PARTS
    for i in range(HEAD_PARTS):
        rows = pl.ds(i * part, part)
        copies.append(pltpu.make_async_copy(three_hbm.at[rows], head_ref.at[rows], sems.at[len(sources) + i]))
    for copy in copies:
        copy.start()
    count = partner_ref.shape[1]
    square = (count, count)
    group = group_ref[...]
    row = iota(square, 0)
    col = iota(square, 1)
    diagonal = row == col
    swap = swap_matrix(side)
    copies[0].wait()
    copies[1].wait()
    partner = jnp.broadcast_to(partner_ref[...], square)
    owner = jnp.broadcast_to(owner_ref[...], square)

    def down(x):
        return jnp.sum(jnp.where(diagonal, x, 0), axis=1, keepdims=True)

    leads = (partner > col).astype(jnp.int32)
    fixed = (partner == col).astype(jnp.int32)
    low = jnp.minimum(partner, col)
    lead_rank = jnp.sum(jnp.where(row < low, down(leads), 0), axis=0, keepdims=True)
    fixed_rank = jnp.sum(jnp.where(row < col, down(fixed), 0), axis=0, keepdims=True)
    leaders = jnp.sum(leads[:1], axis=1, keepdims=True)
    late = (col[:1] > partner[:1]).astype(jnp.int32)
    place = jnp.where(fixed[:1] > 0, 2 * leaders + fixed_rank, 2 * lead_rank + late)
    pick = jnp.where(jnp.broadcast_to(place, square) == row, 1.0, 0.0).astype(BF16)
    copies[2].wait()
    tiles = lax.dot_general(pick, amp_ref[...], NT, preferred_element_type=F32).astype(BF16)
    out_ref[...] = jnp.dot(tiles, swap, preferred_element_type=F32).astype(BF16)
    slot_rank = jnp.sum(((down(owner) == owner) & (row < col)).astype(jnp.int32), axis=0, keepdims=True)
    position = owner_ref[...] * capacity + slot_rank
    small = (8, count)
    wide = (8, 128)
    my_group = jnp.broadcast_to(group[:1, :count], small)
    mine = jnp.broadcast_to(position, small) == iota(small, 0) + capacity * my_group
    found = jnp.sum(jnp.where(mine, jnp.broadcast_to(place + 1, small), 0), axis=1, keepdims=True)
    copies[3].wait()
    copies[4].wait()
    slots = iota(small, 0) + 2 * my_group
    chosen = jnp.where(jnp.broadcast_to(place, small) == slots, jnp.broadcast_to(energy_ref[...], small), 0.0)
    energies = jnp.broadcast_to(jnp.sum(chosen, axis=1, keepdims=True), wide)
    same = jnp.where(group >= jnp.broadcast_to(leaders, wide), 1.0, 0.0)
    info_ref[0] = jnp.where(iota(wide, 0) == 2, same, energies)
    info_ref[1] = jnp.broadcast_to(found, wide).astype(F32)
    for copy in copies[len(sources) :]:
        copy.wait()


def plan(amplitudes, partner, owner, pair_energy, virt_energy, three_index, group, capacity):
    count, side, _ = amplitudes.shape
    virt = virt_energy.shape[0]
    amp = jnp.transpose(amplitudes, (1, 2, 0)).reshape(side * side, count)
    return pl.pallas_call(
        lambda *refs: plan_kernel(*refs, side=side, capacity=capacity),
        in_specs=[VMEM_SPEC] + [HBM_SPEC] * 6,
        out_specs=[VMEM_SPEC] * 4,
        out_shape=[
            jax.ShapeDtypeStruct((count, side * side), BF16),
            jax.ShapeDtypeStruct((2, 8, 128), F32),
            jax.ShapeDtypeStruct((1, virt), F32),
            jax.ShapeDtypeStruct((HEAD,) + three_index.shape[1:], BF16),
        ],
        scratch_shapes=[
            pltpu.VMEM((side * side, count), BF16),
            pltpu.VMEM((1, count), jnp.int32),
            pltpu.VMEM((1, count), jnp.int32),
            pltpu.VMEM((1, count), F32),
            pltpu.SemaphoreType.DMA((5 + HEAD_PARTS,)),
        ],
        compiler_params=pltpu.CompilerParams(vmem_limit_bytes=8 << 20),
        name="plan",
    )(
        jnp.full((8, 128), group, jnp.int32),
        in_hbm(amp),
        in_hbm(partner.reshape(1, count)),
        in_hbm(owner.reshape(1, count)),
        in_hbm(pair_energy.reshape(1, count)),
        in_hbm(virt_energy.reshape(1, virt)),
        in_hbm(three_index),
    )


def ladder_kernel(core_ref, info_ref, virt_ref, own_ref, other_ref, head_ref, three_hbm, keep_ref, send_ref, turned, rest_ref, sems, *, side):
    virt = head_ref.shape[1]
    head = head_ref.shape[0]
    part = rest_ref.shape[0] // REST_PARTS
    copies = []
    for i in range(REST_PARTS):
        source = three_hbm.at[pl.ds(head + i * part, part)]
        copies.append(pltpu.make_async_copy(source, rest_ref.at[pl.ds(i * part, part)], sems.at[i]))
        copies[-1].start()
    half_lanes = virt // 2
    per_vector = half_lanes // side
    first_core = jnp.broadcast_to(core_ref[:1, :] == 0, (side, half_lanes))

    def piece(slot, z, core, half):
        rows = pl.ds(z * side, side)
        lanes = pl.ds(half * half_lanes, half_lanes)
        own = own_ref[slot, rows, lanes].astype(F32)
        other = other_ref[slot, rows, lanes].astype(F32)
        return jnp.where(first_core, own, other) if core == 0 else jnp.where(first_core, other, own)

    order = [(slot, half, high) for slot in range(2) for half in range(2) for high in range(2)]
    vectors = []
    for low in range(per_vector):
        z_low, core = low // 2, low % 2
        vectors.append(
            jnp.concatenate(
                [piece(slot, high * (per_vector // 2) + z_low, core, half) for slot, half, high in order], axis=0
            )
        )
    lane_group = iota(vectors[0].shape, 1) // side
    step = 1
    while step < per_vector:
        keep = (lane_group & step) == 0
        shift = step * side
        for i in range(per_vector):
            if i & step:
                continue
            j = i | step
            a, b = vectors[i], vectors[j]
            vectors[i] = jnp.where(keep, a, pltpu.roll(b, shift, 1))
            vectors[j] = jnp.where(keep, pltpu.roll(a, half_lanes - shift, 1), b)
        step *= 2
    for s_low in range(per_vector):
        vector = vectors[s_low].astype(BF16)
        for k, (slot, half, high) in enumerate(order):
            rows = pl.ds((half * per_vector + s_low) * side, side)
            lanes = pl.ds(slot * virt + high * half_lanes, half_lanes)
            turned[rows, lanes] = vector[k * side : (k + 1) * side]
    amp_t = jnp.dot(swap_matrix(side), turned[...], preferred_element_type=F32).astype(BF16)

    totals = [jnp.zeros((virt, virt), F32)] * 2
    for i in range(REST_PARTS + 1):
        if i == 0:
            block_ref = head_ref
        else:
            copies[i - 1].wait()
            block_ref = rest_ref.at[pl.ds((i - 1) * part, part)]
        count = block_ref.shape[0]
        rows = block_ref[...].reshape(count * virt, virt)
        half = jnp.dot(rows, amp_t, preferred_element_type=F32).astype(BF16)
        for slot in range(2):
            for q in range(count):
                totals[slot] = totals[slot] + lax.dot_general(
                    half[q * virt : (q + 1) * virt, slot * virt : (slot + 1) * virt],
                    block_ref[q],
                    NT,
                    preferred_element_type=F32,
                )

    rows_of = jnp.broadcast_to(virt_ref[...], (virt, virt))
    sums = rows_of + rows_of.T
    info = info_ref[0]
    first = totals[0] / (sums - info[0:1, 0:1])
    second = totals[1] / (sums - info[1:2, 0:1])
    same = jnp.broadcast_to(info[2:3, 0:1] > 0.5, (virt, virt))
    blocks = (first.T + jnp.where(same, first, second), second.T + jnp.where(same, second, first))
    on_first = jnp.broadcast_to(core_ref[:1, :1] == 0, (virt, virt))
    keep_ref[...] = jnp.where(on_first, blocks[0], blocks[1])
    send_ref[...] = jnp.where(on_first, blocks[1], blocks[0])


def ladder(core, info, virt_row, own, other, head, three_index, side):
    naux, virt, _ = three_index.shape
    return pl.pallas_call(
        lambda *refs: ladder_kernel(*refs, side=side),
        in_specs=[VMEM_SPEC] * 6 + [HBM_SPEC],
        out_specs=[VMEM_SPEC] * 2,
        out_shape=[jax.ShapeDtypeStruct((virt, virt), F32)] * 2,
        scratch_shapes=[
            pltpu.VMEM((virt, 2 * virt), BF16),
            pltpu.VMEM((naux - HEAD, virt, virt), BF16),
            pltpu.SemaphoreType.DMA((REST_PARTS,)),
        ],
        compiler_params=pltpu.CompilerParams(vmem_limit_bytes=40 << 20),
        name="ladder",
    )(
        jnp.full((8, 128), core, jnp.int32),
        info,
        virt_row,
        own,
        other,
        head,
        in_hbm(three_index),
    )


def merge_kernel(kept_ref, came_ref, out_ref):
    out_ref[...] = (kept_ref[...] + came_ref[...]).astype(BF16).reshape(out_ref.shape)


def merge(kept, came, aux):
    virt = kept.shape[0]
    return pl.pallas_call(
        merge_kernel,
        in_specs=[VMEM_SPEC] * 2,
        out_specs=VMEM_SPEC,
        out_shape=jax.ShapeDtypeStruct((aux, virt // aux, virt), BF16),
        compiler_params=pltpu.CompilerParams(vmem_limit_bytes=8 << 20),
        name="merge",
    )(kept, came)


def gather_kernel(shares_ref, out_ref):
    for core in range(2):
        total = shares_ref[core].astype(F32)
        for k in range(core + 2, shares_ref.shape[0], 2):
            total += shares_ref[k].astype(F32)
        done = total.astype(BF16)
        for k in range(out_ref.shape[0]):
            out_ref[k, core] = done


def gather(shares, groups):
    return pl.pallas_call(
        gather_kernel,
        in_specs=[VMEM_SPEC],
        out_specs=VMEM_SPEC,
        out_shape=jax.ShapeDtypeStruct((groups, 2) + shares.shape[1:], BF16),
        compiler_params=pltpu.CompilerParams(vmem_limit_bytes=8 << 20),
        name="gather",
    )(shares)


def select_kernel(info_ref, found_ref, out_ref):
    for k in range(out_ref.shape[0]):
        index = info_ref[1, k, 0].astype(jnp.int32)
        block = found_ref[jnp.maximum(index - 1, 0)].astype(F32)
        out_ref[k] = jnp.where(index > 0, block, 0.0)


def select(info, found, capacity):
    return pl.pallas_call(
        select_kernel,
        in_specs=[VMEM_SPEC] * 2,
        out_specs=VMEM_SPEC,
        out_shape=jax.ShapeDtypeStruct((capacity,) + found.shape[1:], F32),
        compiler_params=pltpu.CompilerParams(vmem_limit_bytes=8 << 20),
        name="select",
    )(info, found)


def per_device(amplitudes, three_index, virt_energy, pair_energy, owner, partner):
    aux_axes = ("z", "core")
    swap = [(0, 1), (1, 0)]
    aux = lax.axis_size(aux_axes)
    depth = lax.axis_size("z")
    groups = lax.axis_size("pairs")
    core = lax.axis_index("core")
    pairs_all, side, _ = amplitudes.shape
    virt = three_index.shape[1]
    capacity = 2 * (pairs_all // groups)
    tiles, info, virt_row, head = plan(
        amplitudes, partner, owner, pair_energy, virt_energy, three_index, lax.axis_index("pairs"), capacity
    )
    outgoing = jnp.broadcast_to(
        tiles.reshape(1, groups, 2, side * side), (depth, groups, 2, side * side)
    ).reshape(depth * groups, 2, side * side)
    arrived = lax.all_to_all(outgoing, ("z", "pairs"), split_axis=0, concat_axis=0, tiled=True)
    own = jnp.transpose(arrived, (1, 0, 2))
    other = lax.ppermute(own, "core", swap)
    keep, send = ladder(core, info, virt_row, own, other, head, three_index, side)
    partial = merge(keep, lax.ppermute(send, "core", swap), aux)
    shares = lax.all_to_all(partial, aux_axes, split_axis=0, concat_axis=0, tiled=True)
    spread = gather(shares, groups)
    found = lax.all_to_all(spread, "pairs", split_axis=0, concat_axis=0, tiled=True)
    return select(info, found.reshape(pairs_all, side, virt), capacity)


def solution(mesh):
    groups = mesh.shape["pairs"]
    devices = mesh.devices.reshape(mesh.shape["aux"] // 2, 2, groups)
    split = Mesh(devices, ("z", "core", "pairs"))
    aux = ("z", "core")
    placed = (P(None, aux, "pairs"), P(aux, None, None), P(), P(), P(), P())
    return jax.shard_map(
        per_device, mesh=split, in_specs=placed, out_specs=P("pairs", aux, None), check_vma=False
    )
```

```python
import jax
import jax.numpy as jnp
from jax import lax
from jax.experimental import pallas as pl
from jax.experimental.pallas import tpu as pltpu
from jax.sharding import Mesh
from jax.sharding import PartitionSpec as P

BF16 = jnp.bfloat16
F32 = jnp.float32
NT = (((1,), (1,)), ((), ()))
PARTS = 7
VMEM_SPEC = pl.BlockSpec(memory_space=pltpu.VMEM)
HBM_SPEC = pl.BlockSpec(memory_space=pltpu.HBM)


def in_hbm(x):
    return pltpu.with_memory_space_constraint(x, pltpu.HBM)


def iota(shape, dim):
    return lax.broadcasted_iota(jnp.int32, shape, dim)


def swap_matrix(side):
    full = side * side
    turned = (iota((full, full), 0) % side) * side + iota((full, full), 0) // side
    return jnp.where(turned == iota((full, full), 1), 1.0, 0.0).astype(BF16)


def plan_kernel(
    group_ref,
    amp_hbm,
    partner_hbm,
    owner_hbm,
    energy_hbm,
    virt_hbm,
    out_ref,
    info_ref,
    virt_ref,
    amp_ref,
    partner_ref,
    owner_ref,
    energy_ref,
    sems,
    *,
    side,
    capacity,
):
    sources = (partner_hbm, owner_hbm, amp_hbm, energy_hbm, virt_hbm)
    targets = (partner_ref, owner_ref, amp_ref, energy_ref, virt_ref)
    copies = [pltpu.make_async_copy(a, b, sems.at[i]) for i, (a, b) in enumerate(zip(sources, targets))]
    for copy in copies:
        copy.start()
    count = partner_ref.shape[1]
    square = (count, count)
    group = group_ref[...]
    row = iota(square, 0)
    col = iota(square, 1)
    diagonal = row == col
    swap = swap_matrix(side)
    copies[0].wait()
    copies[1].wait()
    partner = jnp.broadcast_to(partner_ref[...], square)
    owner = jnp.broadcast_to(owner_ref[...], square)

    def down(x):
        return jnp.sum(jnp.where(diagonal, x, 0), axis=1, keepdims=True)

    leads = (partner > col).astype(jnp.int32)
    fixed = (partner == col).astype(jnp.int32)
    low = jnp.minimum(partner, col)
    lead_rank = jnp.sum(jnp.where(row < low, down(leads), 0), axis=0, keepdims=True)
    fixed_rank = jnp.sum(jnp.where(row < col, down(fixed), 0), axis=0, keepdims=True)
    leaders = jnp.sum(leads[:1], axis=1, keepdims=True)
    late = (col[:1] > partner[:1]).astype(jnp.int32)
    place = jnp.where(fixed[:1] > 0, 2 * leaders + fixed_rank, 2 * lead_rank + late)
    pick = jnp.where(jnp.broadcast_to(place, square) == row, 1.0, 0.0).astype(BF16)
    copies[2].wait()
    tiles = lax.dot_general(pick, amp_ref[...], NT, preferred_element_type=F32).astype(BF16)
    out_ref[...] = jnp.dot(tiles, swap, preferred_element_type=F32).astype(BF16)
    slot_rank = jnp.sum(((down(owner) == owner) & (row < col)).astype(jnp.int32), axis=0, keepdims=True)
    position = owner_ref[...] * capacity + slot_rank
    small = (8, count)
    wide = (8, 128)
    my_group = jnp.broadcast_to(group[:1, :count], small)
    mine = jnp.broadcast_to(position, small) == iota(small, 0) + capacity * my_group
    found = jnp.sum(jnp.where(mine, jnp.broadcast_to(place + 1, small), 0), axis=1, keepdims=True)
    copies[3].wait()
    copies[4].wait()
    slots = iota(small, 0) + 2 * my_group
    chosen = jnp.where(jnp.broadcast_to(place, small) == slots, jnp.broadcast_to(energy_ref[...], small), 0.0)
    energies = jnp.broadcast_to(jnp.sum(chosen, axis=1, keepdims=True), wide)
    same = jnp.where(group >= jnp.broadcast_to(leaders, wide), 1.0, 0.0)
    info_ref[0] = jnp.where(iota(wide, 0) == 2, same, energies)
    info_ref[1] = jnp.broadcast_to(found, wide).astype(F32)


def plan(amplitudes, partner, owner, pair_energy, virt_energy, group, capacity):
    count, side, _ = amplitudes.shape
    virt = virt_energy.shape[0]
    amp = jnp.transpose(amplitudes, (1, 2, 0)).reshape(side * side, count)
    return pl.pallas_call(
        lambda *refs: plan_kernel(*refs, side=side, capacity=capacity),
        in_specs=[VMEM_SPEC] + [HBM_SPEC] * 5,
        out_specs=[VMEM_SPEC] * 3,
        out_shape=[
            jax.ShapeDtypeStruct((count, side * side), BF16),
            jax.ShapeDtypeStruct((2, 8, 128), F32),
            jax.ShapeDtypeStruct((1, virt), F32),
        ],
        scratch_shapes=[
            pltpu.VMEM((side * side, count), BF16),
            pltpu.VMEM((1, count), jnp.int32),
            pltpu.VMEM((1, count), jnp.int32),
            pltpu.VMEM((1, count), F32),
            pltpu.SemaphoreType.DMA((5,)),
        ],
        compiler_params=pltpu.CompilerParams(vmem_limit_bytes=8 << 20),
        name="plan",
    )(
        jnp.full((8, 128), group, jnp.int32),
        in_hbm(amp),
        in_hbm(partner.reshape(1, count)),
        in_hbm(owner.reshape(1, count)),
        in_hbm(pair_energy.reshape(1, count)),
        in_hbm(virt_energy.reshape(1, virt)),
    )


def prep_kernel(info_ref, virt_ref, three_hbm, three_ref, scale_ref, sems):
    part = three_ref.shape[0] // PARTS
    copies = []
    for i in range(PARTS):
        rows = pl.ds(i * part, part)
        copies.append(pltpu.make_async_copy(three_hbm.at[rows], three_ref.at[rows], sems.at[i]))
        copies[-1].start()
    virt = virt_ref.shape[1]
    rows_of = jnp.broadcast_to(virt_ref[...], (virt, virt))
    sums = rows_of + rows_of.T
    info = info_ref[0]
    for slot in range(2):
        scale_ref[slot] = 1.0 / (sums - info[slot : slot + 1, 0:1])
    for copy in copies:
        copy.wait()


def prep(info, virt_row, three_index):
    virt = three_index.shape[1]
    return pl.pallas_call(
        prep_kernel,
        in_specs=[VMEM_SPEC] * 2 + [HBM_SPEC],
        out_specs=[VMEM_SPEC] * 2,
        out_shape=[
            jax.ShapeDtypeStruct(three_index.shape, BF16),
            jax.ShapeDtypeStruct((2, virt, virt), F32),
        ],
        scratch_shapes=[pltpu.SemaphoreType.DMA((PARTS,))],
        compiler_params=pltpu.CompilerParams(vmem_limit_bytes=8 << 20),
        cost_estimate=pl.CostEstimate(flops=0, bytes_accessed=2 * three_index.size, transcendentals=0),
        name="prep",
    )(info, virt_row, in_hbm(three_index))


def ladder_kernel(core_ref, info_ref, scale_ref, own_ref, other_ref, b_ref, keep_ref, send_ref, turned, *, side):
    naux, virt, _ = b_ref.shape
    half_lanes = virt // 2
    per_vector = half_lanes // side
    first_core = jnp.broadcast_to(core_ref[:1, :] == 0, (side, half_lanes))

    def piece(slot, z, core, half):
        rows = pl.ds(z * side, side)
        lanes = pl.ds(half * half_lanes, half_lanes)
        own = own_ref[slot, rows, lanes].astype(F32)
        other = other_ref[slot, rows, lanes].astype(F32)
        return jnp.where(first_core, own, other) if core == 0 else jnp.where(first_core, other, own)

    order = [(slot, half, high) for slot in range(2) for half in range(2) for high in range(2)]
    vectors = []
    for low in range(per_vector):
        z_low, core = low // 2, low % 2
        vectors.append(
            jnp.concatenate(
                [piece(slot, high * (per_vector // 2) + z_low, core, half) for slot, half, high in order], axis=0
            )
        )
    lane_group = iota(vectors[0].shape, 1) // side
    step = 1
    while step < per_vector:
        keep = (lane_group & step) == 0
        shift = step * side
        for i in range(per_vector):
            if i & step:
                continue
            j = i | step
            a, b = vectors[i], vectors[j]
            vectors[i] = jnp.where(keep, a, pltpu.roll(b, shift, 1))
            vectors[j] = jnp.where(keep, pltpu.roll(a, half_lanes - shift, 1), b)
        step *= 2
    for s_low in range(per_vector):
        vector = vectors[s_low].astype(BF16)
        for k, (slot, half, high) in enumerate(order):
            rows = pl.ds((half * per_vector + s_low) * side, side)
            lanes = pl.ds(slot * virt + high * half_lanes, half_lanes)
            turned[rows, lanes] = vector[k * side : (k + 1) * side]
    amp_t = jnp.dot(swap_matrix(side), turned[...], preferred_element_type=F32).astype(BF16)

    rows = b_ref[...].reshape(naux * virt, virt)
    half = jnp.dot(rows, amp_t, preferred_element_type=F32).astype(BF16)
    totals = []
    for slot in range(2):
        total = jnp.zeros((virt, virt), F32)
        for q in range(naux):
            total += lax.dot_general(
                half[q * virt : (q + 1) * virt, slot * virt : (slot + 1) * virt],
                b_ref[q],
                NT,
                preferred_element_type=F32,
            )
        totals.append(total)

    info = info_ref[0]
    first = totals[0] * scale_ref[0]
    second = totals[1] * scale_ref[1]
    same = jnp.broadcast_to(info[2:3, 0:1] > 0.5, (virt, virt))
    blocks = (first.T + jnp.where(same, first, second), second.T + jnp.where(same, second, first))
    on_first = jnp.broadcast_to(core_ref[:1, :1] == 0, (virt, virt))
    keep_ref[...] = jnp.where(on_first, blocks[0], blocks[1])
    send_ref[...] = jnp.where(on_first, blocks[1], blocks[0])


def ladder(core, info, scale, own, other, three, side):
    _, virt, _ = three.shape
    return pl.pallas_call(
        lambda *refs: ladder_kernel(*refs, side=side),
        in_specs=[VMEM_SPEC] * 6,
        out_specs=[VMEM_SPEC] * 2,
        out_shape=[jax.ShapeDtypeStruct((virt, virt), F32)] * 2,
        scratch_shapes=[pltpu.VMEM((virt, 2 * virt), BF16)],
        compiler_params=pltpu.CompilerParams(vmem_limit_bytes=40 << 20),
        name="ladder",
    )(
        jnp.full((8, 128), core, jnp.int32),
        info,
        scale,
        own,
        other,
        three,
    )


def merge_kernel(kept_ref, came_ref, out_ref):
    out_ref[...] = (kept_ref[...] + came_ref[...]).astype(BF16).reshape(out_ref.shape)


def merge(kept, came, aux):
    virt = kept.shape[0]
    return pl.pallas_call(
        merge_kernel,
        in_specs=[VMEM_SPEC] * 2,
        out_specs=VMEM_SPEC,
        out_shape=jax.ShapeDtypeStruct((aux, virt // aux, virt), BF16),
        compiler_params=pltpu.CompilerParams(vmem_limit_bytes=8 << 20),
        name="merge",
    )(kept, came)


def gather_kernel(shares_ref, out_ref):
    for core in range(2):
        total = shares_ref[core].astype(F32)
        for k in range(core + 2, shares_ref.shape[0], 2):
            total += shares_ref[k].astype(F32)
        done = total.astype(BF16)
        for k in range(out_ref.shape[0]):
            out_ref[k, core] = done


def gather(shares, groups):
    return pl.pallas_call(
        gather_kernel,
        in_specs=[VMEM_SPEC],
        out_specs=VMEM_SPEC,
        out_shape=jax.ShapeDtypeStruct((groups, 2) + shares.shape[1:], BF16),
        compiler_params=pltpu.CompilerParams(vmem_limit_bytes=8 << 20),
        name="gather",
    )(shares)


def select_kernel(info_ref, found_ref, out_ref):
    for k in range(out_ref.shape[0]):
        index = info_ref[1, k, 0].astype(jnp.int32)
        block = found_ref[jnp.maximum(index - 1, 0)].astype(F32)
        out_ref[k] = jnp.where(index > 0, block, 0.0)


def select(info, found, capacity):
    return pl.pallas_call(
        select_kernel,
        in_specs=[VMEM_SPEC] * 2,
        out_specs=VMEM_SPEC,
        out_shape=jax.ShapeDtypeStruct((capacity,) + found.shape[1:], F32),
        compiler_params=pltpu.CompilerParams(vmem_limit_bytes=8 << 20),
        name="select",
    )(info, found)


def per_device(amplitudes, three_index, virt_energy, pair_energy, owner, partner):
    aux_axes = ("z", "core")
    swap = [(0, 1), (1, 0)]
    aux = lax.axis_size(aux_axes)
    depth = lax.axis_size("z")
    groups = lax.axis_size("pairs")
    core = lax.axis_index("core")
    pairs_all, side, _ = amplitudes.shape
    virt = three_index.shape[1]
    capacity = 2 * (pairs_all // groups)
    tiles, info, virt_row = plan(
        amplitudes, partner, owner, pair_energy, virt_energy, lax.axis_index("pairs"), capacity
    )
    outgoing = jnp.broadcast_to(
        tiles.reshape(1, groups, 2, side * side), (depth, groups, 2, side * side)
    ).reshape(depth * groups, 2, side * side)
    arrived = lax.all_to_all(outgoing, ("z", "pairs"), split_axis=0, concat_axis=0, tiled=True)
    three, scale = prep(info, virt_row, three_index)
    own = jnp.transpose(arrived, (1, 0, 2))
    other = lax.ppermute(own, "core", swap)
    keep, send = ladder(core, info, scale, own, other, three, side)
    partial = merge(keep, lax.ppermute(send, "core", swap), aux)
    shares = lax.all_to_all(partial, aux_axes, split_axis=0, concat_axis=0, tiled=True)
    spread = gather(shares, groups)
    found = lax.all_to_all(spread, "pairs", split_axis=0, concat_axis=0, tiled=True)
    return select(info, found.reshape(pairs_all, side, virt), capacity)


def solution(mesh):
    groups = mesh.shape["pairs"]
    devices = mesh.devices.reshape(mesh.shape["aux"] // 2, 2, groups)
    split = Mesh(devices, ("z", "core", "pairs"))
    aux = ("z", "core")
    placed = (P(None, aux, "pairs"), P(aux, None, None), P(), P(), P(), P())
    return jax.shard_map(
        per_device, mesh=split, in_specs=placed, out_specs=P("pairs", aux, None), check_vma=False
    )
```

```python
import jax
import jax.numpy as jnp
from jax import lax
from jax.experimental import pallas as pl
from jax.experimental.pallas import tpu as pltpu
from jax.sharding import Mesh
from jax.sharding import PartitionSpec as P


BF16 = jnp.bfloat16
F32 = jnp.float32
NT = (((1,), (1,)), ((), ()))
HEAD = 8
HEAD_PARTS = 2
OWN_PARTS = 4
OTHER_PARTS = 4
VMEM_SPEC = pl.BlockSpec(memory_space=pltpu.VMEM)
HBM_SPEC = pl.BlockSpec(memory_space=pltpu.HBM)


def in_hbm(x):
    return pltpu.with_memory_space_constraint(x, pltpu.HBM)


def iota(shape, dim):
    return lax.broadcasted_iota(jnp.int32, shape, dim)


def swap_matrix(side):
    full = side * side
    turned = (iota((full, full), 0) % side) * side + iota((full, full), 0) // side
    return jnp.where(turned == iota((full, full), 1), 1.0, 0.0).astype(BF16)


def plan_kernel(
    group_ref,
    core_ref,
    amp_hbm,
    partner_hbm,
    owner_hbm,
    energy_hbm,
    virt_hbm,
    three_hbm,
    pick_ref,
    info_ref,
    virt_ref,
    amp_ref,
    head_ref,
    partner_ref,
    owner_ref,
    energy_ref,
    sems,
    *,
    capacity,
):
    sources = (partner_hbm, owner_hbm, energy_hbm, virt_hbm, amp_hbm)
    targets = (partner_ref, owner_ref, energy_ref, virt_ref, amp_ref)
    copies = [pltpu.make_async_copy(a, b, sems.at[i]) for i, (a, b) in enumerate(zip(sources, targets))]
    part = head_ref.shape[0] // HEAD_PARTS
    for i in range(HEAD_PARTS):
        rows = pl.ds(i * part, part)
        copies.append(pltpu.make_async_copy(three_hbm.at[rows], head_ref.at[rows], sems.at[len(sources) + i]))
    for copy in copies:
        copy.start()
    count = partner_ref.shape[1]
    square = (count, count)
    group = group_ref[...]
    core = core_ref[...]
    row = iota(square, 0)
    col = iota(square, 1)
    diagonal = row == col
    for copy in copies[:3]:
        copy.wait()
    partner = jnp.broadcast_to(partner_ref[...], square)
    owner = jnp.broadcast_to(owner_ref[...], square)

    def down(x):
        return jnp.sum(jnp.where(diagonal, x, 0), axis=1, keepdims=True)

    leads = (partner > col).astype(jnp.int32)
    fixed = (partner == col).astype(jnp.int32)
    low = jnp.minimum(partner, col)
    lead_rank = jnp.sum(jnp.where(row < low, down(leads), 0), axis=0, keepdims=True)
    fixed_rank = jnp.sum(jnp.where(row < col, down(fixed), 0), axis=0, keepdims=True)
    leaders = jnp.sum(leads[:1], axis=1, keepdims=True)
    late = (col[:1] > partner[:1]).astype(jnp.int32)
    place = jnp.where(fixed[:1] > 0, 2 * leaders + fixed_rank, 2 * lead_rank + late)
    slot = row - row % 2 + jnp.broadcast_to(core[:1, :count], square)
    hit = jnp.broadcast_to(place, square) == slot
    for which in range(2):
        pick_ref[which] = jnp.where(hit & (row % 2 == which), 1.0, 0.0).astype(BF16)
    slot_rank = jnp.sum(((down(owner) == owner) & (row < col)).astype(jnp.int32), axis=0, keepdims=True)
    position = owner_ref[...] * capacity + slot_rank
    small = (8, count)
    wide = (8, 128)
    my_group = jnp.broadcast_to(group[:1, :count], small)
    my_core = jnp.broadcast_to(core[:1, :count], small)
    mine = jnp.broadcast_to(position, small) == iota(small, 0) + capacity * my_group
    found = jnp.sum(jnp.where(mine, jnp.broadcast_to(place + 1, small), 0), axis=1, keepdims=True)
    chosen = jnp.broadcast_to(place, small) == 2 * my_group + my_core
    energy = jnp.sum(jnp.where(chosen, jnp.broadcast_to(energy_ref[...], small), 0.0), axis=1, keepdims=True)
    same = jnp.where(group >= jnp.broadcast_to(leaders, wide), 1.0, 0.0)
    info_ref[0] = jnp.where(iota(wide, 0) == 2, same, jnp.broadcast_to(energy, wide))
    info_ref[1] = jnp.broadcast_to(found, wide).astype(F32)
    for copy in copies[3:]:
        copy.wait()


def plan(amp, partner, owner, pair_energy, virt_energy, three_index, group, core, capacity):
    count = partner.shape[0]
    virt = virt_energy.shape[0]
    return pl.pallas_call(
        lambda *refs: plan_kernel(*refs, capacity=capacity),
        in_specs=[VMEM_SPEC] * 2 + [HBM_SPEC] * 6,
        out_specs=[VMEM_SPEC] * 5,
        out_shape=[
            jax.ShapeDtypeStruct((2, count, count), BF16),
            jax.ShapeDtypeStruct((2, 8, 128), F32),
            jax.ShapeDtypeStruct((1, virt), F32),
            jax.ShapeDtypeStruct(amp.shape, BF16),
            jax.ShapeDtypeStruct((HEAD,) + three_index.shape[1:], BF16),
        ],
        scratch_shapes=[
            pltpu.VMEM((1, count), jnp.int32),
            pltpu.VMEM((1, count), jnp.int32),
            pltpu.VMEM((1, count), F32),
            pltpu.SemaphoreType.DMA((5 + HEAD_PARTS,)),
        ],
        compiler_params=pltpu.CompilerParams(vmem_limit_bytes=8 << 20),
        cost_estimate=pl.CostEstimate(flops=0, bytes_accessed=2 << 20, transcendentals=0),
        name="plan",
    )(
        jnp.full((8, 128), group, jnp.int32),
        jnp.full((8, 128), core, jnp.int32),
        in_hbm(amp),
        in_hbm(partner.reshape(1, count)),
        in_hbm(owner.reshape(1, count)),
        in_hbm(pair_energy.reshape(1, count)),
        in_hbm(virt_energy.reshape(1, virt)),
        in_hbm(three_index),
    )


def pack_kernel(pick_ref, own_ref, other_ref, out_ref, *, side):
    tiles = lax.dot_general(pick_ref[0], own_ref[...], NT, preferred_element_type=F32)
    tiles += lax.dot_general(pick_ref[1], other_ref[...], NT, preferred_element_type=F32)
    out_ref[...] = jnp.dot(tiles.astype(BF16), swap_matrix(side), preferred_element_type=F32).astype(BF16)


def pack(pick, own, other, side):
    return pl.pallas_call(
        lambda *refs: pack_kernel(*refs, side=side),
        in_specs=[VMEM_SPEC] * 3,
        out_specs=VMEM_SPEC,
        out_shape=jax.ShapeDtypeStruct((pick.shape[1], own.shape[0]), BF16),
        compiler_params=pltpu.CompilerParams(vmem_limit_bytes=8 << 20),
        name="pack",
    )(pick, own, other)


def ladder_kernel(
    core_ref, info_ref, virt_ref, tiles_ref, head_ref, own_hbm, other_hbm, out_ref, turned, own_ref, other_ref, sems, *, side
):
    head, virt, _ = head_ref.shape
    copies = []
    blocks = [head_ref]
    for source, target, skip, parts in ((own_hbm, own_ref, head, OWN_PARTS), (other_hbm, other_ref, 0, OTHER_PARTS)):
        part = target.shape[0] // parts
        for i in range(parts):
            block = target.at[pl.ds(i * part, part)]
            copy = pltpu.make_async_copy(source.at[pl.ds(skip + i * part, part)], block, sems.at[len(copies)])
            copy.start()
            copies.append(copy)
            blocks.append(block)
    half_lanes = virt // 2
    per_vector = half_lanes // side
    first_core = jnp.broadcast_to(core_ref[:1, :] == 0, (side, half_lanes))

    def piece(z, core, half):
        rows = pl.ds(z * side, side)
        lanes = pl.ds(half * half_lanes, half_lanes)
        own = tiles_ref[0, rows, lanes]
        other = tiles_ref[1, rows, lanes]
        return jnp.where(first_core, own, other) if core == 0 else jnp.where(first_core, other, own)

    order = [(half, high) for half in range(2) for high in range(2)]
    vectors = []
    for low in range(per_vector):
        z_low, core = low // 2, low % 2
        vectors.append(
            jnp.concatenate([piece(high * (per_vector // 2) + z_low, core, half) for half, high in order], axis=0)
        )
    lane_group = iota(vectors[0].shape, 1) // side
    step = 1
    while step < per_vector:
        keep = (lane_group & step) == 0
        shift = step * side
        for i in range(per_vector):
            if i & step:
                continue
            j = i | step
            a, b = vectors[i], vectors[j]
            vectors[i] = jnp.where(keep, a, pltpu.roll(b, shift, 1))
            vectors[j] = jnp.where(keep, pltpu.roll(a, half_lanes - shift, 1), b)
        step *= 2
    for s_low in range(per_vector):
        for k, (half, high) in enumerate(order):
            rows = pl.ds((half * per_vector + s_low) * side, side)
            lanes = pl.ds(high * half_lanes, half_lanes)
            turned[rows, lanes] = vectors[s_low][k * side : (k + 1) * side]
    amp_t = jnp.dot(swap_matrix(side), turned[...], preferred_element_type=F32).astype(BF16)

    total = jnp.zeros((virt, virt), F32)
    for i, block in enumerate(blocks):
        if i > 0:
            copies[i - 1].wait()
        count = block.shape[0]
        rows = block[...].reshape(count * virt, virt)
        product = jnp.dot(rows, amp_t, preferred_element_type=F32).astype(BF16)
        for q in range(count):
            total += lax.dot_general(
                product[q * virt : (q + 1) * virt], block[q], NT, preferred_element_type=F32
            )

    rows_of = jnp.broadcast_to(virt_ref[...], (virt, virt))
    out_ref[...] = total / (rows_of + rows_of.T - info_ref[0, 0:1, 0:1])


def ladder(core, info, virt_row, tiles, head, three_index, three_other, side):
    naux, virt, _ = three_index.shape
    return pl.pallas_call(
        lambda *refs: ladder_kernel(*refs, side=side),
        in_specs=[VMEM_SPEC] * 5 + [HBM_SPEC] * 2,
        out_specs=VMEM_SPEC,
        out_shape=jax.ShapeDtypeStruct((virt, virt), F32),
        scratch_shapes=[
            pltpu.VMEM((virt, virt), BF16),
            pltpu.VMEM((naux - HEAD, virt, virt), BF16),
            pltpu.VMEM((naux, virt, virt), BF16),
            pltpu.SemaphoreType.DMA((OWN_PARTS + OTHER_PARTS,)),
        ],
        compiler_params=pltpu.CompilerParams(vmem_limit_bytes=40 << 20),
        name="ladder",
    )(
        jnp.full((8, 128), core, jnp.int32),
        info,
        virt_row,
        tiles,
        head,
        in_hbm(three_index),
        in_hbm(three_other),
    )


def merge_kernel(info_ref, own_ref, other_ref, out_ref):
    own = own_ref[...]
    same = jnp.broadcast_to(info_ref[0, 2:3, 0:1] > 0.5, own.shape)
    total = own.T + jnp.where(same, own, other_ref[...])
    out_ref[...] = total.astype(BF16).reshape(out_ref.shape)


def merge(info, own, other, aux):
    virt = own.shape[0]
    return pl.pallas_call(
        merge_kernel,
        in_specs=[VMEM_SPEC] * 3,
        out_specs=VMEM_SPEC,
        out_shape=jax.ShapeDtypeStruct((aux, virt // aux, virt), BF16),
        compiler_params=pltpu.CompilerParams(vmem_limit_bytes=8 << 20),
        name="merge",
    )(info, own, other)


def gather_kernel(shares_ref, out_ref):
    for core in range(2):
        total = shares_ref[core].astype(F32)
        for k in range(core + 2, shares_ref.shape[0], 2):
            total += shares_ref[k].astype(F32)
        done = total.astype(BF16)
        for k in range(out_ref.shape[0]):
            out_ref[k, core] = done


def gather(shares, groups):
    return pl.pallas_call(
        gather_kernel,
        in_specs=[VMEM_SPEC],
        out_specs=VMEM_SPEC,
        out_shape=jax.ShapeDtypeStruct((groups, 2) + shares.shape[1:], BF16),
        compiler_params=pltpu.CompilerParams(vmem_limit_bytes=8 << 20),
        name="gather",
    )(shares)


def select_kernel(info_ref, found_ref, out_ref):
    for k in range(out_ref.shape[0]):
        index = info_ref[1, k, 0].astype(jnp.int32)
        block = found_ref[jnp.maximum(index - 1, 0)].astype(F32)
        out_ref[k] = jnp.where(index > 0, block, 0.0)


def select(info, found, capacity):
    return pl.pallas_call(
        select_kernel,
        in_specs=[VMEM_SPEC] * 2,
        out_specs=VMEM_SPEC,
        out_shape=jax.ShapeDtypeStruct((capacity,) + found.shape[1:], F32),
        compiler_params=pltpu.CompilerParams(vmem_limit_bytes=8 << 20),
        name="select",
    )(info, found)


def per_device(amplitudes, three_index, virt_energy, pair_energy, owner, partner):
    aux_axes = ("z", "core")
    swap = [(0, 1), (1, 0)]
    aux = lax.axis_size(aux_axes)
    depth = lax.axis_size("z")
    groups = lax.axis_size("pairs")
    core = lax.axis_index("core")
    pairs_all, side, _ = amplitudes.shape
    virt = three_index.shape[1]
    capacity = 2 * (pairs_all // groups)
    amp = jnp.transpose(amplitudes, (1, 2, 0)).reshape(side * side, pairs_all)
    amp_other = lax.ppermute(amp, "core", swap)
    pick, info, virt_row, amp_own, head = plan(
        amp, partner, owner, pair_energy, virt_energy, three_index, lax.axis_index("pairs"), core, capacity
    )
    three_late, amp_other = lax.optimization_barrier((three_index, amp_other))
    three_other = lax.ppermute(three_late, "core", swap)
    tiles = pack(pick, amp_own, amp_other, side)
    outgoing = jnp.broadcast_to(
        tiles.reshape(1, groups, 2, side * side), (depth, groups, 2, side * side)
    ).reshape(depth * groups, 2, side * side)
    arrived = lax.all_to_all(outgoing, ("z", "pairs"), split_axis=0, concat_axis=0, tiled=True)
    arrived = jnp.transpose(arrived, (1, 0, 2))
    turned = ladder(core, info, virt_row, arrived, head, three_index, three_other, side)
    partial = merge(info, turned, lax.ppermute(turned, "core", swap), aux)
    shares = lax.all_to_all(partial, aux_axes, split_axis=0, concat_axis=0, tiled=True)
    spread = gather(shares, groups)
    found = lax.all_to_all(spread, "pairs", split_axis=0, concat_axis=0, tiled=True)
    return select(info, found.reshape(pairs_all, side, virt), capacity)


def solution(mesh):
    groups = mesh.shape["pairs"]
    devices = mesh.devices.reshape(mesh.shape["aux"] // 2, 2, groups)
    split = Mesh(devices, ("z", "core", "pairs"))
    aux = ("z", "core")
    placed = (P(None, aux, "pairs"), P(aux, None, None), P(), P(), P(), P())
    return jax.shard_map(
        per_device, mesh=split, in_specs=placed, out_specs=P("pairs", aux, None), check_vma=False
    )
```

```python
import jax
import jax.numpy as jnp
from jax import lax
from jax.experimental import pallas as pl
from jax.experimental.pallas import tpu as pltpu
from jax.sharding import Mesh
from jax.sharding import PartitionSpec as P


BF16 = jnp.bfloat16
F32 = jnp.float32
NT = (((1,), (1,)), ((), ()))
HEAD = 14
HEAD_PARTS = 2
OWN_PARTS = 1
OTHER_PARTS = 1
VMEM_SPEC = pl.BlockSpec(memory_space=pltpu.VMEM)
HBM_SPEC = pl.BlockSpec(memory_space=pltpu.HBM)


def in_hbm(x):
    return pltpu.with_memory_space_constraint(x, pltpu.HBM)


def iota(shape, dim):
    return lax.broadcasted_iota(jnp.int32, shape, dim)


def swap_matrix(side):
    full = side * side
    turned = (iota((full, full), 0) % side) * side + iota((full, full), 0) // side
    return jnp.where(turned == iota((full, full), 1), 1.0, 0.0).astype(BF16)


def plan_kernel(
    group_ref,
    core_ref,
    amp_hbm,
    partner_hbm,
    owner_hbm,
    energy_hbm,
    virt_hbm,
    three_hbm,
    pick_ref,
    info_ref,
    virt_ref,
    amp_ref,
    head_ref,
    partner_ref,
    owner_ref,
    energy_ref,
    sems,
    *,
    capacity,
):
    sources = (partner_hbm, owner_hbm, energy_hbm, virt_hbm, amp_hbm)
    targets = (partner_ref, owner_ref, energy_ref, virt_ref, amp_ref)
    copies = [pltpu.make_async_copy(a, b, sems.at[i]) for i, (a, b) in enumerate(zip(sources, targets))]
    part = head_ref.shape[0] // HEAD_PARTS
    for i in range(HEAD_PARTS):
        rows = pl.ds(i * part, part)
        copies.append(pltpu.make_async_copy(three_hbm.at[rows], head_ref.at[rows], sems.at[len(sources) + i]))
    for copy in copies:
        copy.start()
    count = partner_ref.shape[1]
    square = (count, count)
    group = group_ref[...]
    core = core_ref[...]
    row = iota(square, 0)
    col = iota(square, 1)
    diagonal = row == col
    for copy in copies[:3]:
        copy.wait()
    partner = jnp.broadcast_to(partner_ref[...], square)
    owner = jnp.broadcast_to(owner_ref[...], square)

    def down(x):
        return jnp.sum(jnp.where(diagonal, x, 0), axis=1, keepdims=True)

    leads = (partner > col).astype(jnp.int32)
    fixed = (partner == col).astype(jnp.int32)
    low = jnp.minimum(partner, col)
    lead_rank = jnp.sum(jnp.where(row < low, down(leads), 0), axis=0, keepdims=True)
    fixed_rank = jnp.sum(jnp.where(row < col, down(fixed), 0), axis=0, keepdims=True)
    leaders = jnp.sum(leads[:1], axis=1, keepdims=True)
    late = (col[:1] > partner[:1]).astype(jnp.int32)
    place = jnp.where(fixed[:1] > 0, 2 * leaders + fixed_rank, 2 * lead_rank + late)
    slot = row - row % 2 + jnp.broadcast_to(core[:1, :count], square)
    hit = jnp.broadcast_to(place, square) == slot
    for which in range(2):
        pick_ref[which] = jnp.where(hit & (row % 2 == which), 1.0, 0.0).astype(BF16)
    slot_rank = jnp.sum(((down(owner) == owner) & (row < col)).astype(jnp.int32), axis=0, keepdims=True)
    position = owner_ref[...] * capacity + slot_rank
    small = (8, count)
    wide = (8, 128)
    my_group = jnp.broadcast_to(group[:1, :count], small)
    my_core = jnp.broadcast_to(core[:1, :count], small)
    mine = jnp.broadcast_to(position, small) == iota(small, 0) + capacity * my_group
    found = jnp.sum(jnp.where(mine, jnp.broadcast_to(place + 1, small), 0), axis=1, keepdims=True)
    chosen = jnp.broadcast_to(place, small) == 2 * my_group + my_core
    energy = jnp.sum(jnp.where(chosen, jnp.broadcast_to(energy_ref[...], small), 0.0), axis=1, keepdims=True)
    same = jnp.where(group >= jnp.broadcast_to(leaders, wide), 1.0, 0.0)
    info_ref[0] = jnp.where(iota(wide, 0) == 2, same, jnp.broadcast_to(energy, wide))
    info_ref[1] = jnp.broadcast_to(found, wide).astype(F32)
    for copy in copies[3:]:
        copy.wait()


def plan(amp, partner, owner, pair_energy, virt_energy, three_index, group, core, capacity):
    count = partner.shape[0]
    virt = virt_energy.shape[0]
    return pl.pallas_call(
        lambda *refs: plan_kernel(*refs, capacity=capacity),
        in_specs=[VMEM_SPEC] * 2 + [HBM_SPEC] * 6,
        out_specs=[VMEM_SPEC] * 5,
        out_shape=[
            jax.ShapeDtypeStruct((2, count, count), BF16),
            jax.ShapeDtypeStruct((2, 8, 128), F32),
            jax.ShapeDtypeStruct((1, virt), F32),
            jax.ShapeDtypeStruct(amp.shape, BF16),
            jax.ShapeDtypeStruct((HEAD,) + three_index.shape[1:], BF16),
        ],
        scratch_shapes=[
            pltpu.VMEM((1, count), jnp.int32),
            pltpu.VMEM((1, count), jnp.int32),
            pltpu.VMEM((1, count), F32),
            pltpu.SemaphoreType.DMA((5 + HEAD_PARTS,)),
        ],
        compiler_params=pltpu.CompilerParams(vmem_limit_bytes=8 << 20),
        cost_estimate=pl.CostEstimate(flops=0, bytes_accessed=2 << 20, transcendentals=0),
        name="plan",
    )(
        jnp.full((8, 128), group, jnp.int32),
        jnp.full((8, 128), core, jnp.int32),
        in_hbm(amp),
        in_hbm(partner.reshape(1, count)),
        in_hbm(owner.reshape(1, count)),
        in_hbm(pair_energy.reshape(1, count)),
        in_hbm(virt_energy.reshape(1, virt)),
        in_hbm(three_index),
    )


def pack_kernel(pick_ref, own_ref, other_ref, out_ref, *, side):
    tiles = lax.dot_general(pick_ref[0], own_ref[...], NT, preferred_element_type=F32)
    tiles += lax.dot_general(pick_ref[1], other_ref[...], NT, preferred_element_type=F32)
    out_ref[...] = jnp.dot(tiles.astype(BF16), swap_matrix(side), preferred_element_type=F32).astype(BF16)


def pack(pick, own, other, side):
    return pl.pallas_call(
        lambda *refs: pack_kernel(*refs, side=side),
        in_specs=[VMEM_SPEC] * 3,
        out_specs=VMEM_SPEC,
        out_shape=jax.ShapeDtypeStruct((pick.shape[1], own.shape[0]), BF16),
        compiler_params=pltpu.CompilerParams(vmem_limit_bytes=8 << 20),
        name="pack",
    )(pick, own, other)


def ladder_kernel(
    core_ref, info_ref, virt_ref, tiles_ref, head_ref, own_hbm, other_hbm, out_ref, turned, own_ref, other_ref, sems, *, side
):
    head, virt, _ = head_ref.shape
    copies = []
    blocks = [head_ref]
    for source, target, skip, parts in ((own_hbm, own_ref, head, OWN_PARTS), (other_hbm, other_ref, 0, OTHER_PARTS)):
        part = target.shape[0] // parts
        for i in range(parts):
            block = target.at[pl.ds(i * part, part)]
            copy = pltpu.make_async_copy(source.at[pl.ds(skip + i * part, part)], block, sems.at[len(copies)])
            copy.start()
            copies.append(copy)
            blocks.append(block)
    half_lanes = virt // 2
    per_vector = half_lanes // side
    first_core = jnp.broadcast_to(core_ref[:1, :] == 0, (side, half_lanes))

    def piece(z, core, half):
        rows = pl.ds(z * side, side)
        lanes = pl.ds(half * half_lanes, half_lanes)
        own = tiles_ref[0, rows, lanes]
        other = tiles_ref[1, rows, lanes]
        return jnp.where(first_core, own, other) if core == 0 else jnp.where(first_core, other, own)

    order = [(half, high) for half in range(2) for high in range(2)]
    vectors = []
    for low in range(per_vector):
        z_low, core = low // 2, low % 2
        vectors.append(
            jnp.concatenate([piece(high * (per_vector // 2) + z_low, core, half) for half, high in order], axis=0)
        )
    lane_group = iota(vectors[0].shape, 1) // side
    step = 1
    while step < per_vector:
        keep = (lane_group & step) == 0
        shift = step * side
        for i in range(per_vector):
            if i & step:
                continue
            j = i | step
            a, b = vectors[i], vectors[j]
            vectors[i] = jnp.where(keep, a, pltpu.roll(b, shift, 1))
            vectors[j] = jnp.where(keep, pltpu.roll(a, half_lanes - shift, 1), b)
        step *= 2
    for s_low in range(per_vector):
        for k, (half, high) in enumerate(order):
            rows = pl.ds((half * per_vector + s_low) * side, side)
            lanes = pl.ds(high * half_lanes, half_lanes)
            turned[rows, lanes] = vectors[s_low][k * side : (k + 1) * side]
    amp_t = jnp.dot(swap_matrix(side), turned[...], preferred_element_type=F32).astype(BF16)

    total = jnp.zeros((virt, virt), F32)
    for i, block in enumerate(blocks):
        if i > 0:
            copies[i - 1].wait()
        count = block.shape[0]
        rows = block[...].reshape(count * virt, virt)
        product = jnp.dot(rows, amp_t, preferred_element_type=F32).astype(BF16)
        for q in range(count):
            total += lax.dot_general(
                product[q * virt : (q + 1) * virt], block[q], NT, preferred_element_type=F32
            )

    rows_of = jnp.broadcast_to(virt_ref[...], (virt, virt))
    out_ref[...] = total / (rows_of + rows_of.T - info_ref[0, 0:1, 0:1])


def ladder(core, info, virt_row, tiles, head, three_index, three_other, side):
    naux, virt, _ = three_index.shape
    return pl.pallas_call(
        lambda *refs: ladder_kernel(*refs, side=side),
        in_specs=[VMEM_SPEC] * 5 + [HBM_SPEC] * 2,
        out_specs=VMEM_SPEC,
        out_shape=jax.ShapeDtypeStruct((virt, virt), F32),
        scratch_shapes=[
            pltpu.VMEM((virt, virt), BF16),
            pltpu.VMEM((naux - HEAD, virt, virt), BF16),
            pltpu.VMEM((naux, virt, virt), BF16),
            pltpu.SemaphoreType.DMA((OWN_PARTS + OTHER_PARTS,)),
        ],
        compiler_params=pltpu.CompilerParams(vmem_limit_bytes=40 << 20),
        name="ladder",
    )(
        jnp.full((8, 128), core, jnp.int32),
        info,
        virt_row,
        tiles,
        head,
        in_hbm(three_index),
        in_hbm(three_other),
    )


def merge_kernel(info_ref, own_ref, other_ref, out_ref):
    own = own_ref[...]
    same = jnp.broadcast_to(info_ref[0, 2:3, 0:1] > 0.5, own.shape)
    total = own.T + jnp.where(same, own, other_ref[...])
    out_ref[...] = total.astype(BF16).reshape(out_ref.shape)


def merge(info, own, other, aux):
    virt = own.shape[0]
    return pl.pallas_call(
        merge_kernel,
        in_specs=[VMEM_SPEC] * 3,
        out_specs=VMEM_SPEC,
        out_shape=jax.ShapeDtypeStruct((aux, virt // aux, virt), BF16),
        compiler_params=pltpu.CompilerParams(vmem_limit_bytes=8 << 20),
        name="merge",
    )(info, own, other)


def gather_kernel(shares_ref, out_ref):
    for core in range(2):
        total = shares_ref[core].astype(F32)
        for k in range(core + 2, shares_ref.shape[0], 2):
            total += shares_ref[k].astype(F32)
        done = total.astype(BF16)
        for k in range(out_ref.shape[0]):
            out_ref[k, core] = done


def gather(shares, groups):
    return pl.pallas_call(
        gather_kernel,
        in_specs=[VMEM_SPEC],
        out_specs=VMEM_SPEC,
        out_shape=jax.ShapeDtypeStruct((groups, 2) + shares.shape[1:], BF16),
        compiler_params=pltpu.CompilerParams(vmem_limit_bytes=8 << 20),
        name="gather",
    )(shares)


def select_kernel(info_ref, found_ref, out_ref):
    for k in range(out_ref.shape[0]):
        index = info_ref[1, k, 0].astype(jnp.int32)
        block = found_ref[jnp.maximum(index - 1, 0)].astype(F32)
        out_ref[k] = jnp.where(index > 0, block, 0.0)


def select(info, found, capacity):
    return pl.pallas_call(
        select_kernel,
        in_specs=[VMEM_SPEC] * 2,
        out_specs=VMEM_SPEC,
        out_shape=jax.ShapeDtypeStruct((capacity,) + found.shape[1:], F32),
        compiler_params=pltpu.CompilerParams(vmem_limit_bytes=8 << 20),
        name="select",
    )(info, found)


def per_device(amplitudes, three_index, virt_energy, pair_energy, owner, partner):
    aux_axes = ("z", "core")
    swap = [(0, 1), (1, 0)]
    aux = lax.axis_size(aux_axes)
    depth = lax.axis_size("z")
    groups = lax.axis_size("pairs")
    core = lax.axis_index("core")
    pairs_all, side, _ = amplitudes.shape
    virt = three_index.shape[1]
    capacity = 2 * (pairs_all // groups)
    amp = jnp.transpose(amplitudes, (1, 2, 0)).reshape(side * side, pairs_all)
    amp_other = lax.ppermute(amp, "core", swap)
    three_other = lax.ppermute(three_index, "core", swap)
    pick, info, virt_row, amp_own, head = plan(
        amp, partner, owner, pair_energy, virt_energy, three_index, lax.axis_index("pairs"), core, capacity
    )
    tiles = pack(pick, amp_own, amp_other, side)
    outgoing = jnp.broadcast_to(
        tiles.reshape(1, groups, 2, side * side), (depth, groups, 2, side * side)
    ).reshape(depth * groups, 2, side * side)
    arrived = lax.all_to_all(outgoing, ("z", "pairs"), split_axis=0, concat_axis=0, tiled=True)
    arrived = jnp.transpose(arrived, (1, 0, 2))
    turned = ladder(core, info, virt_row, arrived, head, three_index, three_other, side)
    partial = merge(info, turned, lax.ppermute(turned, "core", swap), aux)
    shares = lax.all_to_all(partial, aux_axes, split_axis=0, concat_axis=0, tiled=True)
    spread = gather(shares, groups)
    found = lax.all_to_all(spread, "pairs", split_axis=0, concat_axis=0, tiled=True)
    return select(info, found.reshape(pairs_all, side, virt), capacity)


def solution(mesh):
    groups = mesh.shape["pairs"]
    devices = mesh.devices.reshape(mesh.shape["aux"] // 2, 2, groups)
    split = Mesh(devices, ("z", "core", "pairs"))
    aux = ("z", "core")
    placed = (P(None, aux, "pairs"), P(aux, None, None), P(), P(), P(), P())
    return jax.shard_map(
        per_device, mesh=split, in_specs=placed, out_specs=P("pairs", aux, None), check_vma=False
    )
```

```python
import jax
import jax.numpy as jnp
from jax import lax
from jax.experimental import pallas as pl
from jax.experimental.pallas import tpu as pltpu
from jax.sharding import Mesh
from jax.sharding import PartitionSpec as P


BF16 = jnp.bfloat16
F32 = jnp.float32
NT = (((1,), (1,)), ((), ()))
NEAR_HEAD = 14
FAR_HEAD = 8
VMEM_SPEC = pl.BlockSpec(memory_space=pltpu.VMEM)
HBM_SPEC = pl.BlockSpec(memory_space=pltpu.HBM)
SMEM_SPEC = pl.BlockSpec(memory_space=pltpu.SMEM)


def in_hbm(x):
    return pltpu.with_memory_space_constraint(x, pltpu.HBM)


def iota(shape, dim):
    return lax.broadcasted_iota(jnp.int32, shape, dim)


def swap_matrix(side):
    full = side * side
    turned = (iota((full, full), 0) % side) * side + iota((full, full), 0) // side
    return jnp.where(turned == iota((full, full), 1), 1.0, 0.0).astype(BF16)


def order_of(partner, row, col):
    leads = (partner > col).astype(jnp.int32)
    fixed = (partner == col).astype(jnp.int32)
    low = jnp.minimum(partner, col)
    diagonal = row == col

    def down(x):
        return jnp.sum(jnp.where(diagonal, x, 0), axis=1, keepdims=True)

    lead_rank = jnp.sum(jnp.where(row < low, down(leads), 0), axis=0, keepdims=True)
    fixed_rank = jnp.sum(jnp.where(row < col, down(fixed), 0), axis=0, keepdims=True)
    leaders = jnp.sum(leads[:1], axis=1, keepdims=True)
    late = (col[:1] > partner[:1]).astype(jnp.int32)
    place = jnp.where(fixed[:1] > 0, 2 * leaders + fixed_rank, 2 * lead_rank + late)
    return place, leaders, down


def plan_kernel(
    near_ref, core_ref, amp_hbm, partner_hbm, three_hbm, pick_ref, amp_ref, own_ref, partner_ref, sems
):
    near = near_ref[0] > 0
    kept = own_ref.shape[0]
    copies = [
        pltpu.make_async_copy(partner_hbm, partner_ref, sems.at[0]),
        pltpu.make_async_copy(amp_hbm, amp_ref, sems.at[1]),
    ]
    head = pl.ds(0, FAR_HEAD)
    tail = pl.ds(FAR_HEAD, kept - FAR_HEAD)
    copies.append(pltpu.make_async_copy(three_hbm.at[head], own_ref.at[head], sems.at[2]))
    rest = pltpu.make_async_copy(three_hbm.at[tail], own_ref.at[tail], sems.at[3])
    for copy in copies:
        copy.start()

    @pl.when(near)
    def _():
        rest.start()

    count = partner_ref.shape[1]
    square = (count, count)
    row = iota(square, 0)
    col = iota(square, 1)
    slot = row - row % 2 + jnp.broadcast_to(core_ref[:1, :count], square)
    copies[0].wait()
    partner = jnp.broadcast_to(partner_ref[...], square)
    place, _, _ = order_of(partner, row, col)
    hit = jnp.broadcast_to(place, square) == slot
    for which in range(2):
        pick_ref[which] = jnp.where(hit & (row % 2 == which), 1.0, 0.0).astype(BF16)
    for copy in copies[1:]:
        copy.wait()

    @pl.when(near)
    def _():
        rest.wait()


def plan(near, core, amp, partner, three_index):
    count = partner.shape[0]
    return pl.pallas_call(
        plan_kernel,
        in_specs=[SMEM_SPEC, VMEM_SPEC] + [HBM_SPEC] * 3,
        out_specs=[VMEM_SPEC] * 3,
        out_shape=[
            jax.ShapeDtypeStruct((2, count, count), BF16),
            jax.ShapeDtypeStruct(amp.shape, BF16),
            jax.ShapeDtypeStruct((NEAR_HEAD,) + three_index.shape[1:], BF16),
        ],
        scratch_shapes=[pltpu.VMEM((1, count), jnp.int32), pltpu.SemaphoreType.DMA((4,))],
        compiler_params=pltpu.CompilerParams(vmem_limit_bytes=8 << 20),
        cost_estimate=pl.CostEstimate(flops=0, bytes_accessed=2 << 20, transcendentals=0),
        name="plan",
    )(
        near,
        jnp.full((8, 128), core, jnp.int32),
        in_hbm(amp),
        in_hbm(partner.reshape(1, count)),
        in_hbm(three_index),
    )


def book_kernel(
    group_ref, partner_hbm, owner_hbm, energy_hbm, virt_hbm, info_ref, sums_ref, partner_ref, owner_ref, energy_ref, virt_ref, sems, *, capacity
):
    sources = (partner_hbm, owner_hbm, energy_hbm, virt_hbm)
    targets = (partner_ref, owner_ref, energy_ref, virt_ref)
    copies = [pltpu.make_async_copy(a, b, sems.at[i]) for i, (a, b) in enumerate(zip(sources, targets))]
    for copy in copies:
        copy.start()
    count = partner_ref.shape[1]
    virt = virt_ref.shape[1]
    square = (count, count)
    small = (8, count)
    wide = (8, 128)
    group = group_ref[...]
    row = iota(square, 0)
    col = iota(square, 1)
    for copy in copies:
        copy.wait()
    partner = jnp.broadcast_to(partner_ref[...], square)
    owner = jnp.broadcast_to(owner_ref[...], square)
    place, leaders, down = order_of(partner, row, col)
    slot_rank = jnp.sum(((down(owner) == owner) & (row < col)).astype(jnp.int32), axis=0, keepdims=True)
    position = owner_ref[...] * capacity + slot_rank
    my_group = jnp.broadcast_to(group[:1, :count], small)
    mine = jnp.broadcast_to(position, small) == iota(small, 0) + capacity * my_group
    found = jnp.sum(jnp.where(mine, jnp.broadcast_to(place + 1, small), 0), axis=1, keepdims=True)
    chosen = jnp.broadcast_to(place, small) == iota(small, 0) + 2 * my_group
    energy = jnp.sum(jnp.where(chosen, jnp.broadcast_to(energy_ref[...], small), 0.0), axis=1, keepdims=True)
    same = jnp.where(group >= jnp.broadcast_to(leaders, wide), 1.0, 0.0)
    info_ref[0] = jnp.where(iota(wide, 0) == 2, same, jnp.broadcast_to(energy, wide))
    info_ref[1] = jnp.broadcast_to(found, wide).astype(F32)
    rows_of = jnp.broadcast_to(virt_ref[...], (virt, virt))
    sums = rows_of + rows_of.T
    for slot in range(2):
        sums_ref[slot] = 1.0 / (sums - info_ref[0, slot : slot + 1, 0:1])


def book(group, partner, owner, pair_energy, virt_energy, capacity):
    count = partner.shape[0]
    virt = virt_energy.shape[0]
    return pl.pallas_call(
        lambda *refs: book_kernel(*refs, capacity=capacity),
        in_specs=[VMEM_SPEC] + [HBM_SPEC] * 4,
        out_specs=[VMEM_SPEC] * 2,
        out_shape=[
            jax.ShapeDtypeStruct((2, 8, 128), F32),
            jax.ShapeDtypeStruct((2, virt, virt), F32),
        ],
        scratch_shapes=[
            pltpu.VMEM((1, count), jnp.int32),
            pltpu.VMEM((1, count), jnp.int32),
            pltpu.VMEM((1, count), F32),
            pltpu.VMEM((1, virt), F32),
            pltpu.SemaphoreType.DMA((4,)),
        ],
        compiler_params=pltpu.CompilerParams(vmem_limit_bytes=8 << 20),
        cost_estimate=pl.CostEstimate(flops=0, bytes_accessed=1 << 20, transcendentals=0),
        name="book",
    )(
        jnp.full((8, 128), group, jnp.int32),
        in_hbm(partner.reshape(1, count)),
        in_hbm(owner.reshape(1, count)),
        in_hbm(pair_energy.reshape(1, count)),
        in_hbm(virt_energy.reshape(1, virt)),
    )


def pack_kernel(pick_ref, own_ref, other_ref, out_ref, *, side):
    tiles = lax.dot_general(pick_ref[0], own_ref[...], NT, preferred_element_type=F32)
    tiles += lax.dot_general(pick_ref[1], other_ref[...], NT, preferred_element_type=F32)
    out_ref[...] = jnp.dot(tiles.astype(BF16), swap_matrix(side), preferred_element_type=F32).astype(BF16)


def pack(pick, own, other, side):
    return pl.pallas_call(
        lambda *refs: pack_kernel(*refs, side=side),
        in_specs=[VMEM_SPEC] * 3,
        out_specs=VMEM_SPEC,
        out_shape=jax.ShapeDtypeStruct((pick.shape[1], own.shape[0]), BF16),
        compiler_params=pltpu.CompilerParams(vmem_limit_bytes=8 << 20),
        name="pack",
    )(pick, own, other)


def ladder_kernel(
    near_ref, core_ref, tiles_ref, own_ref, own_hbm, other_hbm, out_ref, turned, rest_ref, other_ref, sems, *, side
):
    near = near_ref[0] > 0
    naux, virt, _ = other_ref.shape
    skipped = NEAR_HEAD - FAR_HEAD
    tail = pl.ds(skipped, naux - NEAR_HEAD)
    middle = pltpu.make_async_copy(own_hbm.at[pl.ds(FAR_HEAD, skipped)], rest_ref.at[pl.ds(0, skipped)], sems.at[0])
    rest = pltpu.make_async_copy(own_hbm.at[pl.ds(NEAR_HEAD, naux - NEAR_HEAD)], rest_ref.at[tail], sems.at[1])
    fetch = pltpu.make_async_copy(other_hbm, other_ref, sems.at[2])

    @pl.when(jnp.logical_not(near))
    def _():
        middle.start()

    rest.start()
    fetch.start()
    half_lanes = virt // 2
    per_vector = half_lanes // side
    first_core = jnp.broadcast_to(core_ref[:1, :] == 0, (side, half_lanes))

    def piece(z, core, half):
        rows = pl.ds(z * side, side)
        lanes = pl.ds(half * half_lanes, half_lanes)
        own = tiles_ref[0, rows, lanes]
        other = tiles_ref[1, rows, lanes]
        return jnp.where(first_core, own, other) if core == 0 else jnp.where(first_core, other, own)

    order = [(half, high) for half in range(2) for high in range(2)]
    vectors = []
    for low in range(per_vector):
        z_low, core = low // 2, low % 2
        vectors.append(
            jnp.concatenate([piece(high * (per_vector // 2) + z_low, core, half) for half, high in order], axis=0)
        )
    lane_group = iota(vectors[0].shape, 1) // side
    step = 1
    while step < per_vector:
        keep = (lane_group & step) == 0
        shift = step * side
        for i in range(per_vector):
            if i & step:
                continue
            j = i | step
            a, b = vectors[i], vectors[j]
            vectors[i] = jnp.where(keep, a, pltpu.roll(b, shift, 1))
            vectors[j] = jnp.where(keep, pltpu.roll(a, half_lanes - shift, 1), b)
        step *= 2
    for s_low in range(per_vector):
        for k, (half, high) in enumerate(order):
            rows = pl.ds((half * per_vector + s_low) * side, side)
            lanes = pl.ds(high * half_lanes, half_lanes)
            turned[rows, lanes] = vectors[s_low][k * side : (k + 1) * side]
    amp_t = jnp.dot(swap_matrix(side), turned[...], preferred_element_type=F32).astype(BF16)

    def run(blocks):
        total = jnp.zeros((virt, virt), F32)
        for block, copies in blocks:
            for copy in copies:
                copy.wait()
            count = block.shape[0]
            rows = block[...].reshape(count * virt, virt)
            product = jnp.dot(rows, amp_t, preferred_element_type=F32).astype(BF16)
            for q in range(count):
                total += lax.dot_general(
                    product[q * virt : (q + 1) * virt], block[q], NT, preferred_element_type=F32
                )
        out_ref[...] = total

    @pl.when(near)
    def _():
        run(((own_ref, ()), (rest_ref.at[tail], (rest,)), (other_ref, (fetch,))))

    @pl.when(jnp.logical_not(near))
    def _():
        run(((own_ref.at[pl.ds(0, FAR_HEAD)], ()), (rest_ref, (middle, rest)), (other_ref, (fetch,))))


def ladder(near, core, tiles, own, three_index, three_other, side):
    naux, virt, _ = three_index.shape
    return pl.pallas_call(
        lambda *refs: ladder_kernel(*refs, side=side),
        in_specs=[SMEM_SPEC] + [VMEM_SPEC] * 3 + [HBM_SPEC] * 2,
        out_specs=VMEM_SPEC,
        out_shape=jax.ShapeDtypeStruct((virt, virt), F32),
        scratch_shapes=[
            pltpu.VMEM((virt, virt), BF16),
            pltpu.VMEM((naux - FAR_HEAD, virt, virt), BF16),
            pltpu.VMEM((naux, virt, virt), BF16),
            pltpu.SemaphoreType.DMA((3,)),
        ],
        compiler_params=pltpu.CompilerParams(vmem_limit_bytes=40 << 20),
        name="ladder",
    )(
        near,
        jnp.full((8, 128), core, jnp.int32),
        tiles,
        own,
        in_hbm(three_index),
        in_hbm(three_other),
    )


def merge_kernel(core_ref, info_ref, scale_ref, own_ref, other_ref, out_ref):
    on_first = jnp.broadcast_to(core_ref[:1, :1] == 0, own_ref.shape)
    own_scale = jnp.where(on_first, scale_ref[0], scale_ref[1])
    other_scale = jnp.where(on_first, scale_ref[1], scale_ref[0])
    own = own_ref[...] * own_scale
    other = other_ref[...] * other_scale
    same = jnp.broadcast_to(info_ref[0, 2:3, 0:1] > 0.5, own.shape)
    total = own.T + jnp.where(same, own, other)
    out_ref[...] = total.astype(BF16).reshape(out_ref.shape)


def merge(core, info, scale, own, other, aux):
    virt = own.shape[0]
    return pl.pallas_call(
        merge_kernel,
        in_specs=[VMEM_SPEC] * 5,
        out_specs=VMEM_SPEC,
        out_shape=jax.ShapeDtypeStruct((aux, virt // aux, virt), BF16),
        compiler_params=pltpu.CompilerParams(vmem_limit_bytes=8 << 20),
        name="merge",
    )(jnp.full((8, 128), core, jnp.int32), info, scale, own, other)


def gather_kernel(shares_ref, out_ref):
    for core in range(2):
        total = shares_ref[core].astype(F32)
        for k in range(core + 2, shares_ref.shape[0], 2):
            total += shares_ref[k].astype(F32)
        done = total.astype(BF16)
        for k in range(out_ref.shape[0]):
            out_ref[k, core] = done


def gather(shares, groups):
    return pl.pallas_call(
        gather_kernel,
        in_specs=[VMEM_SPEC],
        out_specs=VMEM_SPEC,
        out_shape=jax.ShapeDtypeStruct((groups, 2) + shares.shape[1:], BF16),
        compiler_params=pltpu.CompilerParams(vmem_limit_bytes=8 << 20),
        name="gather",
    )(shares)


def select_kernel(info_ref, found_ref, out_ref):
    for k in range(out_ref.shape[0]):
        index = info_ref[1, k, 0].astype(jnp.int32)
        block = found_ref[jnp.maximum(index - 1, 0)].astype(F32)
        out_ref[k] = jnp.where(index > 0, block, 0.0)


def select(info, found, capacity):
    return pl.pallas_call(
        select_kernel,
        in_specs=[VMEM_SPEC] * 2,
        out_specs=VMEM_SPEC,
        out_shape=jax.ShapeDtypeStruct((capacity,) + found.shape[1:], F32),
        compiler_params=pltpu.CompilerParams(vmem_limit_bytes=8 << 20),
        name="select",
    )(info, found)


def per_device(amplitudes, three_index, virt_energy, pair_energy, owner, partner):
    aux_axes = ("z", "core")
    swap = [(0, 1), (1, 0)]
    aux = lax.axis_size(aux_axes)
    depth = lax.axis_size("z")
    groups = lax.axis_size("pairs")
    core = lax.axis_index("core")
    pairs_all, side, _ = amplitudes.shape
    virt = three_index.shape[1]
    capacity = 2 * (pairs_all // groups)
    near = (lax.axis_index("z") < depth // 2).astype(jnp.int32).reshape(1)
    amp = jnp.transpose(amplitudes, (1, 2, 0)).reshape(side * side, pairs_all)
    amp_other = lax.ppermute(amp, "core", swap)
    three_other = lax.ppermute(three_index, "core", swap)
    pick, amp_own, own = plan(near, core, amp, partner, three_index)
    tiles = pack(pick, amp_own, amp_other, side)
    outgoing = jnp.broadcast_to(
        tiles.reshape(1, groups, 2, side * side), (depth, groups, 2, side * side)
    ).reshape(depth * groups, 2, side * side)
    arrived = lax.all_to_all(outgoing, ("z", "pairs"), split_axis=0, concat_axis=0, tiled=True)
    arrived = jnp.transpose(arrived, (1, 0, 2))
    turned = ladder(near, core, arrived, own, three_index, three_other, side)
    traded = lax.ppermute(turned, "core", swap)
    info, scale = book(lax.axis_index("pairs"), partner, owner, pair_energy, virt_energy, capacity)
    partial = merge(core, info, scale, turned, traded, aux)
    shares = lax.all_to_all(partial, aux_axes, split_axis=0, concat_axis=0, tiled=True)
    spread = gather(shares, groups)
    found = lax.all_to_all(spread, "pairs", split_axis=0, concat_axis=0, tiled=True)
    return select(info, found.reshape(pairs_all, side, virt), capacity)


def solution(mesh):
    groups = mesh.shape["pairs"]
    devices = mesh.devices.reshape(mesh.shape["aux"] // 2, 2, groups)
    split = Mesh(devices, ("z", "core", "pairs"))
    aux = ("z", "core")
    placed = (P(None, aux, "pairs"), P(aux, None, None), P(), P(), P(), P())
    return jax.shard_map(
        per_device, mesh=split, in_specs=placed, out_specs=P("pairs", aux, None), check_vma=False
    )
```

```python
import jax
import jax.numpy as jnp
from jax import lax
from jax.experimental import pallas as pl
from jax.experimental.pallas import tpu as pltpu
from jax.sharding import Mesh
from jax.sharding import PartitionSpec as P


BF16 = jnp.bfloat16
F32 = jnp.float32
NT = (((1,), (1,)), ((), ()))
NEAR_HEAD = 20
FAR_HEAD = 8
VMEM_SPEC = pl.BlockSpec(memory_space=pltpu.VMEM)
HBM_SPEC = pl.BlockSpec(memory_space=pltpu.HBM)
SMEM_SPEC = pl.BlockSpec(memory_space=pltpu.SMEM)


def in_hbm(x):
    return pltpu.with_memory_space_constraint(x, pltpu.HBM)


def iota(shape, dim):
    return lax.broadcasted_iota(jnp.int32, shape, dim)


def swap_matrix(side):
    full = side * side
    turned = (iota((full, full), 0) % side) * side + iota((full, full), 0) // side
    return jnp.where(turned == iota((full, full), 1), 1.0, 0.0).astype(BF16)


def plan_kernel(
    near_ref,
    group_ref,
    amp_hbm,
    partner_hbm,
    owner_hbm,
    energy_hbm,
    virt_hbm,
    three_hbm,
    out_ref,
    info_ref,
    virt_ref,
    head_ref,
    amp_ref,
    partner_ref,
    owner_ref,
    energy_ref,
    sems,
    *,
    side,
    capacity,
):
    sources = (partner_hbm, owner_hbm, amp_hbm, energy_hbm, virt_hbm)
    targets = (partner_ref, owner_ref, amp_ref, energy_ref, virt_ref)
    copies = [pltpu.make_async_copy(a, b, sems.at[i]) for i, (a, b) in enumerate(zip(sources, targets))]
    first = pl.ds(0, FAR_HEAD)
    tail = pl.ds(FAR_HEAD, head_ref.shape[0] - FAR_HEAD)
    copies.append(pltpu.make_async_copy(three_hbm.at[first], head_ref.at[first], sems.at[5]))
    rest = pltpu.make_async_copy(three_hbm.at[tail], head_ref.at[tail], sems.at[6])
    near = near_ref[0] > 0
    for copy in copies:
        copy.start()

    @pl.when(near)
    def _():
        rest.start()

    count = partner_ref.shape[1]
    square = (count, count)
    group = group_ref[...]
    row = iota(square, 0)
    col = iota(square, 1)
    diagonal = row == col
    swap = swap_matrix(side)
    copies[0].wait()
    copies[1].wait()
    partner = jnp.broadcast_to(partner_ref[...], square)
    owner = jnp.broadcast_to(owner_ref[...], square)

    def down(x):
        return jnp.sum(jnp.where(diagonal, x, 0), axis=1, keepdims=True)

    leads = (partner > col).astype(jnp.int32)
    fixed = (partner == col).astype(jnp.int32)
    low = jnp.minimum(partner, col)
    lead_rank = jnp.sum(jnp.where(row < low, down(leads), 0), axis=0, keepdims=True)
    fixed_rank = jnp.sum(jnp.where(row < col, down(fixed), 0), axis=0, keepdims=True)
    leaders = jnp.sum(leads[:1], axis=1, keepdims=True)
    late = (col[:1] > partner[:1]).astype(jnp.int32)
    place = jnp.where(fixed[:1] > 0, 2 * leaders + fixed_rank, 2 * lead_rank + late)
    pick = jnp.where(jnp.broadcast_to(place, square) == row, 1.0, 0.0).astype(BF16)
    copies[2].wait()
    tiles = lax.dot_general(pick, amp_ref[...], NT, preferred_element_type=F32).astype(BF16)
    out_ref[...] = jnp.dot(tiles, swap, preferred_element_type=F32).astype(BF16)
    slot_rank = jnp.sum(((down(owner) == owner) & (row < col)).astype(jnp.int32), axis=0, keepdims=True)
    position = owner_ref[...] * capacity + slot_rank
    small = (8, count)
    wide = (8, 128)
    my_group = jnp.broadcast_to(group[:1, :count], small)
    mine = jnp.broadcast_to(position, small) == iota(small, 0) + capacity * my_group
    found = jnp.sum(jnp.where(mine, jnp.broadcast_to(place + 1, small), 0), axis=1, keepdims=True)
    copies[3].wait()
    copies[4].wait()
    slots = iota(small, 0) + 2 * my_group
    chosen = jnp.where(jnp.broadcast_to(place, small) == slots, jnp.broadcast_to(energy_ref[...], small), 0.0)
    energies = jnp.broadcast_to(jnp.sum(chosen, axis=1, keepdims=True), wide)
    same = jnp.where(group >= jnp.broadcast_to(leaders, wide), 1.0, 0.0)
    info_ref[0] = jnp.where(iota(wide, 0) == 2, same, energies)
    info_ref[1] = jnp.broadcast_to(found, wide).astype(F32)
    copies[5].wait()

    @pl.when(near)
    def _():
        rest.wait()


def plan(near, amplitudes, partner, owner, pair_energy, virt_energy, three_index, group, capacity):
    count, side, _ = amplitudes.shape
    virt = virt_energy.shape[0]
    amp = jnp.transpose(amplitudes, (1, 2, 0)).reshape(side * side, count)
    return pl.pallas_call(
        lambda *refs: plan_kernel(*refs, side=side, capacity=capacity),
        in_specs=[SMEM_SPEC, VMEM_SPEC] + [HBM_SPEC] * 6,
        out_specs=[VMEM_SPEC] * 4,
        out_shape=[
            jax.ShapeDtypeStruct((count, side * side), BF16),
            jax.ShapeDtypeStruct((2, 8, 128), F32),
            jax.ShapeDtypeStruct((1, virt), F32),
            jax.ShapeDtypeStruct((NEAR_HEAD,) + three_index.shape[1:], BF16),
        ],
        scratch_shapes=[
            pltpu.VMEM((side * side, count), BF16),
            pltpu.VMEM((1, count), jnp.int32),
            pltpu.VMEM((1, count), jnp.int32),
            pltpu.VMEM((1, count), F32),
            pltpu.SemaphoreType.DMA((7,)),
        ],
        compiler_params=pltpu.CompilerParams(vmem_limit_bytes=8 << 20),
        name="plan",
    )(
        near,
        jnp.full((8, 128), group, jnp.int32),
        in_hbm(amp),
        in_hbm(partner.reshape(1, count)),
        in_hbm(owner.reshape(1, count)),
        in_hbm(pair_energy.reshape(1, count)),
        in_hbm(virt_energy.reshape(1, virt)),
        in_hbm(three_index),
    )


def half_columns(tiles_ref, turned, even, side, virt):
    lanes_of = virt // 2
    groups = lanes_of // side
    low = [i // 2 + (groups // 2) * (i % 2) for i in range(groups)]
    high = [low[(i - 1) % groups] for i in range(groups)]
    order = [(slot, half) for slot in range(2) for half in range(2)]

    def piece(slot, half, i):
        lanes = pl.ds(half * lanes_of, lanes_of)
        a = tiles_ref[slot, pl.ds(low[i] * side, side), lanes]
        b = tiles_ref[slot, pl.ds(high[i] * side, side), lanes]
        return jnp.where(even, a, b)

    vectors = [jnp.concatenate([piece(slot, half, i) for slot, half in order], axis=0) for i in range(groups)]
    lane_group = iota(vectors[0].shape, 1) // side
    step = 1
    while step < groups:
        keep = (lane_group & step) == 0
        shift = step * side
        for i in range(groups):
            if i & step:
                continue
            j = i | step
            a, b = vectors[i], vectors[j]
            vectors[i] = jnp.where(keep, a, pltpu.roll(b, shift, 1))
            vectors[j] = jnp.where(keep, pltpu.roll(a, lanes_of - shift, 1), b)
        step *= 2
    for i in range(groups):
        for k, (slot, half) in enumerate(order):
            rows = pl.ds((half * groups + i) * side, side)
            turned[rows, pl.ds(slot * lanes_of, lanes_of)] = vectors[i][k * side : (k + 1) * side]
    return jnp.dot(swap_matrix(side), turned[...], preferred_element_type=F32).astype(BF16)


def half_ladder(total, block, amp_t, plain, side):
    count, virt, _ = block.shape
    lanes_of = virt // 2
    product = jnp.dot(block[...].reshape(count * virt, virt), amp_t, preferred_element_type=F32).astype(BF16)

    def gathered(q):
        return jnp.where(plain, block[q, :, :lanes_of], pltpu.roll(block[q, :, lanes_of:], side, 1))

    for q in range(0, count, 2):
        left = []
        for slot in range(2):
            lanes = slice(slot * lanes_of, (slot + 1) * lanes_of)
            left.append(
                jnp.concatenate(
                    [product[q * virt : (q + 1) * virt, lanes], product[(q + 1) * virt : (q + 2) * virt, lanes]], axis=1
                )
            )
        right = jnp.concatenate([gathered(q), gathered(q + 1)], axis=1)
        total += lax.dot_general(jnp.concatenate(left, axis=0), right, NT, preferred_element_type=F32)
    return total


def masks(core_ref, which, side, virt):
    lanes_of = virt // 2
    parity = jnp.bitwise_xor(core_ref[:1, :], which)
    even = jnp.broadcast_to(parity == 0, (side, lanes_of))
    shape = (virt, lanes_of)
    plain = (iota(shape, 1) // side) % 2 == jnp.broadcast_to(parity, shape)
    return even, plain


def own_kernel(near_ref, core_ref, tiles_ref, head_ref, three_hbm, total_ref, rest_ref, turned, sems, *, side):
    near = near_ref[0] > 0
    far_rest, virt, _ = rest_ref.shape
    skipped = NEAR_HEAD - FAR_HEAD
    tail = pl.ds(skipped, far_rest - skipped)
    middle = pltpu.make_async_copy(three_hbm.at[pl.ds(FAR_HEAD, skipped)], rest_ref.at[pl.ds(0, skipped)], sems.at[0])
    last = pltpu.make_async_copy(three_hbm.at[pl.ds(NEAR_HEAD, far_rest - skipped)], rest_ref.at[tail], sems.at[1])

    @pl.when(jnp.logical_not(near))
    def _():
        middle.start()

    last.start()
    even, plain = masks(core_ref, 0, side, virt)
    amp_t = half_columns(tiles_ref, turned, even, side, virt)
    zero = jnp.zeros((2 * virt, virt), F32)

    @pl.when(near)
    def _():
        total = half_ladder(zero, head_ref, amp_t, plain, side)
        last.wait()
        total_ref[...] = half_ladder(total, rest_ref.at[tail], amp_t, plain, side)

    @pl.when(jnp.logical_not(near))
    def _():
        total = half_ladder(zero, head_ref.at[pl.ds(0, FAR_HEAD)], amp_t, plain, side)
        middle.wait()
        last.wait()
        total_ref[...] = half_ladder(total, rest_ref, amp_t, plain, side)


def own_half(near, core, tiles, head, three_index, side):
    naux, virt, _ = three_index.shape
    return pl.pallas_call(
        lambda *refs: own_kernel(*refs, side=side),
        in_specs=[SMEM_SPEC] + [VMEM_SPEC] * 3 + [HBM_SPEC],
        out_specs=[VMEM_SPEC] * 2,
        out_shape=[
            jax.ShapeDtypeStruct((2 * virt, virt), F32),
            jax.ShapeDtypeStruct((naux - FAR_HEAD, virt, virt), BF16),
        ],
        scratch_shapes=[pltpu.VMEM((virt, virt), BF16), pltpu.SemaphoreType.DMA((2,))],
        compiler_params=pltpu.CompilerParams(vmem_limit_bytes=24 << 20),
        cost_estimate=pl.CostEstimate(flops=1 << 30, bytes_accessed=4 << 20, transcendentals=0),
        name="own",
    )(near, jnp.full((8, 128), core, jnp.int32), tiles, head, in_hbm(three_index))


def other_kernel(
    near_ref, core_ref, info_ref, virt_ref, tiles_ref, head_ref, rest_ref, total_ref, keep_ref, send_ref, turned, sum_ref, *, side
):
    near = near_ref[0] > 0
    far_rest, virt, _ = rest_ref.shape
    skipped = NEAR_HEAD - FAR_HEAD
    even, plain = masks(core_ref, 1, side, virt)
    amp_t = half_columns(tiles_ref, turned, even, side, virt)

    @pl.when(near)
    def _():
        total = half_ladder(total_ref[...], head_ref, amp_t, plain, side)
        sum_ref[...] = half_ladder(total, rest_ref.at[pl.ds(skipped, far_rest - skipped)], amp_t, plain, side)

    @pl.when(jnp.logical_not(near))
    def _():
        total = half_ladder(total_ref[...], head_ref.at[pl.ds(0, FAR_HEAD)], amp_t, plain, side)
        sum_ref[...] = half_ladder(total, rest_ref, amp_t, plain, side)

    rows_of = jnp.broadcast_to(virt_ref[...], (virt, virt))
    sums = rows_of + rows_of.T
    info = info_ref[0]
    first = sum_ref[:virt, :] / (sums - info[0:1, 0:1])
    second = sum_ref[virt:, :] / (sums - info[1:2, 0:1])
    same = jnp.broadcast_to(info[2:3, 0:1] > 0.5, (virt, virt))
    blocks = (first.T + jnp.where(same, first, second), second.T + jnp.where(same, second, first))
    on_first = jnp.broadcast_to(core_ref[:1, :1] == 0, (virt, virt))
    keep_ref[...] = jnp.where(on_first, blocks[0], blocks[1])
    send_ref[...] = jnp.where(on_first, blocks[1], blocks[0])


def other_half(near, core, info, virt_row, tiles, head, rest, total, side):
    virt = head.shape[1]
    return pl.pallas_call(
        lambda *refs: other_kernel(*refs, side=side),
        in_specs=[SMEM_SPEC] + [VMEM_SPEC] * 7,
        out_specs=[VMEM_SPEC] * 2,
        out_shape=[jax.ShapeDtypeStruct((virt, virt), F32)] * 2,
        scratch_shapes=[pltpu.VMEM((virt, virt), BF16), pltpu.VMEM((2 * virt, virt), F32)],
        compiler_params=pltpu.CompilerParams(vmem_limit_bytes=24 << 20),
        name="other",
    )(near, jnp.full((8, 128), core, jnp.int32), info, virt_row, tiles, head, rest, total)


def merge_kernel(kept_ref, came_ref, out_ref):
    out_ref[...] = (kept_ref[...] + came_ref[...]).astype(BF16).reshape(out_ref.shape)


def merge(kept, came, aux):
    virt = kept.shape[0]
    return pl.pallas_call(
        merge_kernel,
        in_specs=[VMEM_SPEC] * 2,
        out_specs=VMEM_SPEC,
        out_shape=jax.ShapeDtypeStruct((aux, virt // aux, virt), BF16),
        compiler_params=pltpu.CompilerParams(vmem_limit_bytes=8 << 20),
        name="merge",
    )(kept, came)


def gather_kernel(shares_ref, out_ref):
    for core in range(2):
        total = shares_ref[core].astype(F32)
        for k in range(core + 2, shares_ref.shape[0], 2):
            total += shares_ref[k].astype(F32)
        done = total.astype(BF16)
        for k in range(out_ref.shape[0]):
            out_ref[k, core] = done


def gather(shares, groups):
    return pl.pallas_call(
        gather_kernel,
        in_specs=[VMEM_SPEC],
        out_specs=VMEM_SPEC,
        out_shape=jax.ShapeDtypeStruct((groups, 2) + shares.shape[1:], BF16),
        compiler_params=pltpu.CompilerParams(vmem_limit_bytes=8 << 20),
        name="gather",
    )(shares)


def select_kernel(info_ref, found_ref, out_ref):
    for k in range(out_ref.shape[0]):
        index = info_ref[1, k, 0].astype(jnp.int32)
        block = found_ref[jnp.maximum(index - 1, 0)].astype(F32)
        out_ref[k] = jnp.where(index > 0, block, 0.0)


def select(info, found, capacity):
    return pl.pallas_call(
        select_kernel,
        in_specs=[VMEM_SPEC] * 2,
        out_specs=VMEM_SPEC,
        out_shape=jax.ShapeDtypeStruct((capacity,) + found.shape[1:], F32),
        compiler_params=pltpu.CompilerParams(vmem_limit_bytes=8 << 20),
        name="select",
    )(info, found)


def per_device(amplitudes, three_index, virt_energy, pair_energy, owner, partner):
    aux_axes = ("z", "core")
    swap = [(0, 1), (1, 0)]
    aux = lax.axis_size(aux_axes)
    depth = lax.axis_size("z")
    groups = lax.axis_size("pairs")
    core = lax.axis_index("core")
    pairs_all, side, _ = amplitudes.shape
    virt = three_index.shape[1]
    capacity = 2 * (pairs_all // groups)
    near = (lax.axis_index("z") < depth // 2).astype(jnp.int32).reshape(1)
    tiles, info, virt_row, head = plan(
        near, amplitudes, partner, owner, pair_energy, virt_energy, three_index, lax.axis_index("pairs"), capacity
    )
    outgoing = jnp.broadcast_to(
        tiles.reshape(1, groups, 2, side * side), (depth, groups, 2, side * side)
    ).reshape(depth * groups, 2, side * side)
    arrived = lax.all_to_all(outgoing, ("z", "pairs"), split_axis=0, concat_axis=0, tiled=True)
    own = jnp.transpose(arrived, (1, 0, 2))
    other = lax.ppermute(own, "core", swap)
    total, rest = own_half(near, core, own, head, three_index, side)
    keep, send = other_half(near, core, info, virt_row, other, head, rest, total, side)
    partial = merge(keep, lax.ppermute(send, "core", swap), aux)
    shares = lax.all_to_all(partial, aux_axes, split_axis=0, concat_axis=0, tiled=True)
    spread = gather(shares, groups)
    found = lax.all_to_all(spread, "pairs", split_axis=0, concat_axis=0, tiled=True)
    return select(info, found.reshape(pairs_all, side, virt), capacity)


def solution(mesh):
    groups = mesh.shape["pairs"]
    devices = mesh.devices.reshape(mesh.shape["aux"] // 2, 2, groups)
    split = Mesh(devices, ("z", "core", "pairs"))
    aux = ("z", "core")
    placed = (P(None, aux, "pairs"), P(aux, None, None), P(), P(), P(), P())
    return jax.shard_map(
        per_device, mesh=split, in_specs=placed, out_specs=P("pairs", aux, None), check_vma=False
    )
```

```python
import jax
import jax.numpy as jnp
from jax import lax
from jax.experimental import pallas as pl
from jax.experimental.pallas import tpu as pltpu
from jax.sharding import Mesh
from jax.sharding import PartitionSpec as P


BF16 = jnp.bfloat16
F32 = jnp.float32
NT = (((1,), (1,)), ((), ()))
NEAR_HEAD = 20
FAR_MIDDLE = 14
FAR_HEAD = 6
VMEM_SPEC = pl.BlockSpec(memory_space=pltpu.VMEM)
HBM_SPEC = pl.BlockSpec(memory_space=pltpu.HBM)
SMEM_SPEC = pl.BlockSpec(memory_space=pltpu.SMEM)


def in_hbm(x):
    return pltpu.with_memory_space_constraint(x, pltpu.HBM)


def iota(shape, dim):
    return lax.broadcasted_iota(jnp.int32, shape, dim)


def swap_matrix(side):
    full = side * side
    turned = (iota((full, full), 0) % side) * side + iota((full, full), 0) // side
    return jnp.where(turned == iota((full, full), 1), 1.0, 0.0).astype(BF16)


def order_of(partner, row, col):
    leads = (partner > col).astype(jnp.int32)
    fixed = (partner == col).astype(jnp.int32)
    low = jnp.minimum(partner, col)
    diagonal = row == col

    def down(x):
        return jnp.sum(jnp.where(diagonal, x, 0), axis=1, keepdims=True)

    lead_rank = jnp.sum(jnp.where(row < low, down(leads), 0), axis=0, keepdims=True)
    fixed_rank = jnp.sum(jnp.where(row < col, down(fixed), 0), axis=0, keepdims=True)
    leaders = jnp.sum(leads[:1], axis=1, keepdims=True)
    late = (col[:1] > partner[:1]).astype(jnp.int32)
    place = jnp.where(fixed[:1] > 0, 2 * leaders + fixed_rank, 2 * lead_rank + late)
    return place, leaders, down


def plan_kernel(
    near_ref, core_ref, amp_hbm, partner_hbm, three_hbm, pick_ref, amp_ref, own_ref, partner_ref, sems
):
    near = near_ref[0] > 0
    kept = own_ref.shape[0]
    copies = [
        pltpu.make_async_copy(partner_hbm, partner_ref, sems.at[0]),
        pltpu.make_async_copy(amp_hbm, amp_ref, sems.at[1]),
    ]
    head = pl.ds(0, FAR_HEAD)
    tail = pl.ds(FAR_HEAD, kept - FAR_HEAD)
    copies.append(pltpu.make_async_copy(three_hbm.at[head], own_ref.at[head], sems.at[2]))
    rest = pltpu.make_async_copy(three_hbm.at[tail], own_ref.at[tail], sems.at[3])
    for copy in copies:
        copy.start()

    @pl.when(near)
    def _():
        rest.start()

    count = partner_ref.shape[1]
    square = (count, count)
    row = iota(square, 0)
    col = iota(square, 1)
    slot = row - row % 2 + jnp.broadcast_to(core_ref[:1, :count], square)
    copies[0].wait()
    partner = jnp.broadcast_to(partner_ref[...], square)
    place, _, _ = order_of(partner, row, col)
    hit = jnp.broadcast_to(place, square) == slot
    for which in range(2):
        pick_ref[which] = jnp.where(hit & (row % 2 == which), 1.0, 0.0).astype(BF16)
    for copy in copies[1:]:
        copy.wait()

    @pl.when(near)
    def _():
        rest.wait()


def plan(near, core, amp, partner, three_index):
    count = partner.shape[0]
    return pl.pallas_call(
        plan_kernel,
        in_specs=[SMEM_SPEC, VMEM_SPEC] + [HBM_SPEC] * 3,
        out_specs=[VMEM_SPEC] * 3,
        out_shape=[
            jax.ShapeDtypeStruct((2, count, count), BF16),
            jax.ShapeDtypeStruct(amp.shape, BF16),
            jax.ShapeDtypeStruct((NEAR_HEAD,) + three_index.shape[1:], BF16),
        ],
        scratch_shapes=[pltpu.VMEM((1, count), jnp.int32), pltpu.SemaphoreType.DMA((4,))],
        compiler_params=pltpu.CompilerParams(vmem_limit_bytes=8 << 20),
        cost_estimate=pl.CostEstimate(flops=0, bytes_accessed=2 << 20, transcendentals=0),
        name="plan",
    )(
        near,
        jnp.full((8, 128), core, jnp.int32),
        in_hbm(amp),
        in_hbm(partner.reshape(1, count)),
        in_hbm(three_index),
    )


def book_kernel(
    group_ref, core_ref, own_ref, partner_hbm, owner_hbm, energy_hbm, virt_hbm, info_ref, base_ref, factor_ref, partner_ref, owner_ref, energy_ref, virt_ref, sems, *, capacity
):
    sources = (partner_hbm, owner_hbm, energy_hbm, virt_hbm)
    targets = (partner_ref, owner_ref, energy_ref, virt_ref)
    copies = [pltpu.make_async_copy(a, b, sems.at[i]) for i, (a, b) in enumerate(zip(sources, targets))]
    for copy in copies:
        copy.start()
    count = partner_ref.shape[1]
    virt = virt_ref.shape[1]
    square = (count, count)
    small = (8, count)
    wide = (8, 128)
    group = group_ref[...]
    row = iota(square, 0)
    col = iota(square, 1)
    for copy in copies:
        copy.wait()
    partner = jnp.broadcast_to(partner_ref[...], square)
    owner = jnp.broadcast_to(owner_ref[...], square)
    place, leaders, down = order_of(partner, row, col)
    slot_rank = jnp.sum(((down(owner) == owner) & (row < col)).astype(jnp.int32), axis=0, keepdims=True)
    position = owner_ref[...] * capacity + slot_rank
    my_group = jnp.broadcast_to(group[:1, :count], small)
    mine = jnp.broadcast_to(position, small) == iota(small, 0) + capacity * my_group
    found = jnp.sum(jnp.where(mine, jnp.broadcast_to(place + 1, small), 0), axis=1, keepdims=True)
    chosen = jnp.broadcast_to(place, small) == iota(small, 0) + 2 * my_group
    energy = jnp.sum(jnp.where(chosen, jnp.broadcast_to(energy_ref[...], small), 0.0), axis=1, keepdims=True)
    same = jnp.where(group >= jnp.broadcast_to(leaders, wide), 1.0, 0.0)
    info_ref[0] = jnp.where(iota(wide, 0) == 2, same, jnp.broadcast_to(energy, wide))
    info_ref[1] = jnp.broadcast_to(found, wide).astype(F32)
    rows_of = jnp.broadcast_to(virt_ref[...], (virt, virt))
    sums = rows_of + rows_of.T
    on_first = jnp.broadcast_to(core_ref[:1, :1] == 0, (1, 1))
    first, second = info_ref[0, 0:1, 0:1], info_ref[0, 1:2, 0:1]
    alone = jnp.broadcast_to(info_ref[0, 2:3, 0:1] > 0.5, own_ref.shape)
    own = own_ref[...] / (sums - jnp.where(on_first, first, second))
    base_ref[...] = own.T + jnp.where(alone, own, 0.0)
    factor_ref[...] = jnp.where(alone, 0.0, 1.0 / (sums - jnp.where(on_first, second, first)))


def book(group, core, own, partner, owner, pair_energy, virt_energy, capacity):
    count = partner.shape[0]
    virt = virt_energy.shape[0]
    return pl.pallas_call(
        lambda *refs: book_kernel(*refs, capacity=capacity),
        in_specs=[VMEM_SPEC] * 3 + [HBM_SPEC] * 4,
        out_specs=[VMEM_SPEC] * 3,
        out_shape=[
            jax.ShapeDtypeStruct((2, 8, 128), F32),
            jax.ShapeDtypeStruct((virt, virt), F32),
            jax.ShapeDtypeStruct((virt, virt), F32),
        ],
        scratch_shapes=[
            pltpu.VMEM((1, count), jnp.int32),
            pltpu.VMEM((1, count), jnp.int32),
            pltpu.VMEM((1, count), F32),
            pltpu.VMEM((1, virt), F32),
            pltpu.SemaphoreType.DMA((4,)),
        ],
        compiler_params=pltpu.CompilerParams(vmem_limit_bytes=8 << 20),
        cost_estimate=pl.CostEstimate(flops=0, bytes_accessed=1 << 20, transcendentals=0),
        name="book",
    )(
        jnp.full((8, 128), group, jnp.int32),
        jnp.full((8, 128), core, jnp.int32),
        own,
        in_hbm(partner.reshape(1, count)),
        in_hbm(owner.reshape(1, count)),
        in_hbm(pair_energy.reshape(1, count)),
        in_hbm(virt_energy.reshape(1, virt)),
    )


def pack_kernel(pick_ref, own_ref, other_ref, out_ref, *, side):
    tiles = lax.dot_general(pick_ref[0], own_ref[...], NT, preferred_element_type=F32)
    tiles += lax.dot_general(pick_ref[1], other_ref[...], NT, preferred_element_type=F32)
    out_ref[...] = jnp.dot(tiles.astype(BF16), swap_matrix(side), preferred_element_type=F32).astype(BF16)


def pack(pick, own, other, side):
    return pl.pallas_call(
        lambda *refs: pack_kernel(*refs, side=side),
        in_specs=[VMEM_SPEC] * 3,
        out_specs=VMEM_SPEC,
        out_shape=jax.ShapeDtypeStruct((pick.shape[1], own.shape[0]), BF16),
        compiler_params=pltpu.CompilerParams(vmem_limit_bytes=8 << 20),
        name="pack",
    )(pick, own, other)


def ladder_kernel(
    near_ref, core_ref, tiles_ref, own_ref, own_hbm, other_hbm, out_ref, turned, rest_ref, other_ref, sems, *, side
):
    near = near_ref[0] > 0
    naux, virt, _ = other_ref.shape
    edges = (FAR_HEAD, FAR_MIDDLE, NEAR_HEAD, naux)
    spans = []
    copies = []
    for i in range(3):
        size = edges[i + 1] - edges[i]
        spans.append(rest_ref.at[pl.ds(edges[i] - FAR_HEAD, size)])
        copies.append(pltpu.make_async_copy(own_hbm.at[pl.ds(edges[i], size)], spans[i], sems.at[i]))
    fetch = pltpu.make_async_copy(other_hbm, other_ref, sems.at[3])

    @pl.when(jnp.logical_not(near))
    def _():
        copies[0].start()
        copies[1].start()

    copies[2].start()
    fetch.start()
    half_lanes = virt // 2
    per_vector = half_lanes // side
    first_core = jnp.broadcast_to(core_ref[:1, :] == 0, (side, half_lanes))

    def piece(z, core, half):
        rows = pl.ds(z * side, side)
        lanes = pl.ds(half * half_lanes, half_lanes)
        own = tiles_ref[0, rows, lanes]
        other = tiles_ref[1, rows, lanes]
        return jnp.where(first_core, own, other) if core == 0 else jnp.where(first_core, other, own)

    order = [(half, high) for half in range(2) for high in range(2)]
    vectors = []
    for low in range(per_vector):
        z_low, core = low // 2, low % 2
        vectors.append(
            jnp.concatenate([piece(high * (per_vector // 2) + z_low, core, half) for half, high in order], axis=0)
        )
    lane_group = iota(vectors[0].shape, 1) // side
    step = 1
    while step < per_vector:
        keep = (lane_group & step) == 0
        shift = step * side
        for i in range(per_vector):
            if i & step:
                continue
            j = i | step
            a, b = vectors[i], vectors[j]
            vectors[i] = jnp.where(keep, a, pltpu.roll(b, shift, 1))
            vectors[j] = jnp.where(keep, pltpu.roll(a, half_lanes - shift, 1), b)
        step *= 2
    for s_low in range(per_vector):
        for k, (half, high) in enumerate(order):
            rows = pl.ds((half * per_vector + s_low) * side, side)
            lanes = pl.ds(high * half_lanes, half_lanes)
            turned[rows, lanes] = vectors[s_low][k * side : (k + 1) * side]
    amp_t = jnp.dot(swap_matrix(side), turned[...], preferred_element_type=F32).astype(BF16)

    def run(blocks):
        total = jnp.zeros((virt, virt), F32)
        for block, copies in blocks:
            for copy in copies:
                copy.wait()
            count = block.shape[0]
            rows = block[...].reshape(count * virt, virt)
            product = jnp.dot(rows, amp_t, preferred_element_type=F32).astype(BF16)
            for q in range(count):
                total += lax.dot_general(
                    product[q * virt : (q + 1) * virt], block[q], NT, preferred_element_type=F32
                )
        out_ref[...] = total

    @pl.when(near)
    def _():
        run(((own_ref, ()), (spans[2], copies[2:]), (other_ref, (fetch,))))

    @pl.when(jnp.logical_not(near))
    def _():
        late = rest_ref.at[pl.ds(FAR_MIDDLE - FAR_HEAD, naux - FAR_MIDDLE)]
        run(
            (
                (own_ref.at[pl.ds(0, FAR_HEAD)], ()),
                (spans[0], copies[:1]),
                (late, copies[1:]),
                (other_ref, (fetch,)),
            )
        )


def ladder(near, core, tiles, own, three_index, three_other, side):
    naux, virt, _ = three_index.shape
    return pl.pallas_call(
        lambda *refs: ladder_kernel(*refs, side=side),
        in_specs=[SMEM_SPEC] + [VMEM_SPEC] * 3 + [HBM_SPEC] * 2,
        out_specs=VMEM_SPEC,
        out_shape=jax.ShapeDtypeStruct((virt, virt), F32),
        scratch_shapes=[
            pltpu.VMEM((virt, virt), BF16),
            pltpu.VMEM((naux - FAR_HEAD, virt, virt), BF16),
            pltpu.VMEM((naux, virt, virt), BF16),
            pltpu.SemaphoreType.DMA((4,)),
        ],
        compiler_params=pltpu.CompilerParams(vmem_limit_bytes=40 << 20),
        name="ladder",
    )(
        near,
        jnp.full((8, 128), core, jnp.int32),
        tiles,
        own,
        in_hbm(three_index),
        in_hbm(three_other),
    )


def merge_kernel(base_ref, factor_ref, other_ref, out_ref):
    total = base_ref[...] + other_ref[...] * factor_ref[...]
    out_ref[...] = total.astype(BF16).reshape(out_ref.shape)


def merge(base, factor, other, aux):
    virt = base.shape[0]
    return pl.pallas_call(
        merge_kernel,
        in_specs=[VMEM_SPEC] * 3,
        out_specs=VMEM_SPEC,
        out_shape=jax.ShapeDtypeStruct((aux, virt // aux, virt), BF16),
        compiler_params=pltpu.CompilerParams(vmem_limit_bytes=8 << 20),
        name="merge",
    )(base, factor, other)


def gather_kernel(shares_ref, out_ref):
    for core in range(2):
        total = shares_ref[core].astype(F32)
        for k in range(core + 2, shares_ref.shape[0], 2):
            total += shares_ref[k].astype(F32)
        done = total.astype(BF16)
        for k in range(out_ref.shape[0]):
            out_ref[k, core] = done


def gather(shares, groups):
    return pl.pallas_call(
        gather_kernel,
        in_specs=[VMEM_SPEC],
        out_specs=VMEM_SPEC,
        out_shape=jax.ShapeDtypeStruct((groups, 2) + shares.shape[1:], BF16),
        compiler_params=pltpu.CompilerParams(vmem_limit_bytes=8 << 20),
        name="gather",
    )(shares)


def select_kernel(info_ref, found_ref, out_ref):
    for k in range(out_ref.shape[0]):
        index = info_ref[1, k, 0].astype(jnp.int32)
        block = found_ref[jnp.maximum(index - 1, 0)].astype(F32)
        out_ref[k] = jnp.where(index > 0, block, 0.0)


def select(info, found, capacity):
    return pl.pallas_call(
        select_kernel,
        in_specs=[VMEM_SPEC] * 2,
        out_specs=VMEM_SPEC,
        out_shape=jax.ShapeDtypeStruct((capacity,) + found.shape[1:], F32),
        compiler_params=pltpu.CompilerParams(vmem_limit_bytes=8 << 20),
        name="select",
    )(info, found)


def per_device(amplitudes, three_index, virt_energy, pair_energy, owner, partner):
    aux_axes = ("z", "core")
    swap = [(0, 1), (1, 0)]
    aux = lax.axis_size(aux_axes)
    depth = lax.axis_size("z")
    groups = lax.axis_size("pairs")
    core = lax.axis_index("core")
    pairs_all, side, _ = amplitudes.shape
    virt = three_index.shape[1]
    capacity = 2 * (pairs_all // groups)
    near = (lax.axis_index("z") < depth // 2).astype(jnp.int32).reshape(1)
    amp = jnp.transpose(amplitudes, (1, 2, 0)).reshape(side * side, pairs_all)
    amp_other = lax.ppermute(amp, "core", swap)
    three_other = lax.ppermute(three_index, "core", swap)
    pick, amp_own, own = plan(near, core, amp, partner, three_index)
    tiles = pack(pick, amp_own, amp_other, side)
    outgoing = jnp.broadcast_to(
        tiles.reshape(1, groups, 2, side * side), (depth, groups, 2, side * side)
    ).reshape(depth * groups, 2, side * side)
    arrived = lax.all_to_all(outgoing, ("z", "pairs"), split_axis=0, concat_axis=0, tiled=True)
    arrived = jnp.transpose(arrived, (1, 0, 2))
    turned = ladder(near, core, arrived, own, three_index, three_other, side)
    traded = lax.ppermute(turned, "core", swap)
    info, base, factor = book(lax.axis_index("pairs"), core, turned, partner, owner, pair_energy, virt_energy, capacity)
    partial = merge(base, factor, traded, aux)
    shares = lax.all_to_all(partial, aux_axes, split_axis=0, concat_axis=0, tiled=True)
    spread = gather(shares, groups)
    found = lax.all_to_all(spread, "pairs", split_axis=0, concat_axis=0, tiled=True)
    return select(info, found.reshape(pairs_all, side, virt), capacity)


def solution(mesh):
    groups = mesh.shape["pairs"]
    devices = mesh.devices.reshape(mesh.shape["aux"] // 2, 2, groups)
    split = Mesh(devices, ("z", "core", "pairs"))
    aux = ("z", "core")
    placed = (P(None, aux, "pairs"), P(aux, None, None), P(), P(), P(), P())
    return jax.shard_map(
        per_device, mesh=split, in_specs=placed, out_specs=P("pairs", aux, None), check_vma=False
    )
```

```python
import jax
import jax.numpy as jnp
from jax import lax
from jax.experimental import pallas as pl
from jax.experimental.pallas import tpu as pltpu
from jax.sharding import Mesh
from jax.sharding import PartitionSpec as P


BF16 = jnp.bfloat16
F32 = jnp.float32
NT = (((1,), (1,)), ((), ()))
NEAR_HEAD = 14
FAR_HEAD = 8
VMEM_SPEC = pl.BlockSpec(memory_space=pltpu.VMEM)
HBM_SPEC = pl.BlockSpec(memory_space=pltpu.HBM)
SMEM_SPEC = pl.BlockSpec(memory_space=pltpu.SMEM)


def in_hbm(x):
    return pltpu.with_memory_space_constraint(x, pltpu.HBM)


def iota(shape, dim):
    return lax.broadcasted_iota(jnp.int32, shape, dim)


def swap_matrix(side):
    full = side * side
    turned = (iota((full, full), 0) % side) * side + iota((full, full), 0) // side
    return jnp.where(turned == iota((full, full), 1), 1.0, 0.0).astype(BF16)


def order_of(partner, row, col):
    leads = (partner > col).astype(jnp.int32)
    fixed = (partner == col).astype(jnp.int32)
    low = jnp.minimum(partner, col)
    diagonal = row == col

    def down(x):
        return jnp.sum(jnp.where(diagonal, x, 0), axis=1, keepdims=True)

    lead_rank = jnp.sum(jnp.where(row < low, down(leads), 0), axis=0, keepdims=True)
    fixed_rank = jnp.sum(jnp.where(row < col, down(fixed), 0), axis=0, keepdims=True)
    leaders = jnp.sum(leads[:1], axis=1, keepdims=True)
    late = (col[:1] > partner[:1]).astype(jnp.int32)
    place = jnp.where(fixed[:1] > 0, 2 * leaders + fixed_rank, 2 * lead_rank + late)
    return place, leaders, down


def plan_kernel(
    near_ref, core_ref, amp_hbm, partner_hbm, three_hbm, pick_ref, amp_ref, own_ref, partner_ref, sems
):
    near = near_ref[0] > 0
    kept = own_ref.shape[0]
    copies = [
        pltpu.make_async_copy(partner_hbm, partner_ref, sems.at[0]),
        pltpu.make_async_copy(amp_hbm, amp_ref, sems.at[1]),
    ]
    head = pl.ds(0, FAR_HEAD)
    tail = pl.ds(FAR_HEAD, kept - FAR_HEAD)
    copies.append(pltpu.make_async_copy(three_hbm.at[head], own_ref.at[head], sems.at[2]))
    rest = pltpu.make_async_copy(three_hbm.at[tail], own_ref.at[tail], sems.at[3])
    for copy in copies:
        copy.start()

    @pl.when(near)
    def _():
        rest.start()

    count = partner_ref.shape[1]
    square = (count, count)
    row = iota(square, 0)
    col = iota(square, 1)
    slot = row - row % 2 + jnp.broadcast_to(core_ref[:1, :count], square)
    copies[0].wait()
    partner = jnp.broadcast_to(partner_ref[...], square)
    place, _, _ = order_of(partner, row, col)
    hit = jnp.broadcast_to(place, square) == slot
    for which in range(2):
        pick_ref[which] = jnp.where(hit & (row % 2 == which), 1.0, 0.0).astype(BF16)
    for copy in copies[1:]:
        copy.wait()

    @pl.when(near)
    def _():
        rest.wait()


def plan(near, core, amp, partner, three_index):
    count = partner.shape[0]
    return pl.pallas_call(
        plan_kernel,
        in_specs=[SMEM_SPEC, VMEM_SPEC] + [HBM_SPEC] * 3,
        out_specs=[VMEM_SPEC] * 3,
        out_shape=[
            jax.ShapeDtypeStruct((2, count, count), BF16),
            jax.ShapeDtypeStruct(amp.shape, BF16),
            jax.ShapeDtypeStruct((NEAR_HEAD,) + three_index.shape[1:], BF16),
        ],
        scratch_shapes=[pltpu.VMEM((1, count), jnp.int32), pltpu.SemaphoreType.DMA((4,))],
        compiler_params=pltpu.CompilerParams(vmem_limit_bytes=8 << 20),
        cost_estimate=pl.CostEstimate(flops=0, bytes_accessed=2 << 20, transcendentals=0),
        name="plan",
    )(
        near,
        jnp.full((8, 128), core, jnp.int32),
        in_hbm(amp),
        in_hbm(partner.reshape(1, count)),
        in_hbm(three_index),
    )


def book_kernel(
    group_ref, core_ref, own_ref, partner_hbm, owner_hbm, energy_hbm, virt_hbm, info_ref, base_ref, factor_ref, partner_ref, owner_ref, energy_ref, virt_ref, sems, *, capacity
):
    sources = (partner_hbm, owner_hbm, energy_hbm, virt_hbm)
    targets = (partner_ref, owner_ref, energy_ref, virt_ref)
    copies = [pltpu.make_async_copy(a, b, sems.at[i]) for i, (a, b) in enumerate(zip(sources, targets))]
    for copy in copies:
        copy.start()
    count = partner_ref.shape[1]
    virt = virt_ref.shape[1]
    square = (count, count)
    small = (8, count)
    wide = (8, 128)
    group = group_ref[...]
    row = iota(square, 0)
    col = iota(square, 1)
    for copy in copies:
        copy.wait()
    partner = jnp.broadcast_to(partner_ref[...], square)
    owner = jnp.broadcast_to(owner_ref[...], square)
    place, leaders, down = order_of(partner, row, col)
    slot_rank = jnp.sum(((down(owner) == owner) & (row < col)).astype(jnp.int32), axis=0, keepdims=True)
    position = owner_ref[...] * capacity + slot_rank
    my_group = jnp.broadcast_to(group[:1, :count], small)
    mine = jnp.broadcast_to(position, small) == iota(small, 0) + capacity * my_group
    found = jnp.sum(jnp.where(mine, jnp.broadcast_to(place + 1, small), 0), axis=1, keepdims=True)
    chosen = jnp.broadcast_to(place, small) == iota(small, 0) + 2 * my_group
    energy = jnp.sum(jnp.where(chosen, jnp.broadcast_to(energy_ref[...], small), 0.0), axis=1, keepdims=True)
    same = jnp.where(group >= jnp.broadcast_to(leaders, wide), 1.0, 0.0)
    info_ref[0] = jnp.where(iota(wide, 0) == 2, same, jnp.broadcast_to(energy, wide))
    info_ref[1] = jnp.broadcast_to(found, wide).astype(F32)
    rows_of = jnp.broadcast_to(virt_ref[...], (virt, virt))
    sums = rows_of + rows_of.T
    on_first = jnp.broadcast_to(core_ref[:1, :1] == 0, (1, 1))
    first, second = info_ref[0, 0:1, 0:1], info_ref[0, 1:2, 0:1]
    alone = jnp.broadcast_to(info_ref[0, 2:3, 0:1] > 0.5, own_ref.shape)
    own = own_ref[...] / (sums - jnp.where(on_first, first, second))
    base_ref[...] = own.T + jnp.where(alone, own, 0.0)
    factor_ref[...] = jnp.where(alone, 0.0, 1.0 / (sums - jnp.where(on_first, second, first)))


def book(group, core, own, partner, owner, pair_energy, virt_energy, capacity):
    count = partner.shape[0]
    virt = virt_energy.shape[0]
    return pl.pallas_call(
        lambda *refs: book_kernel(*refs, capacity=capacity),
        in_specs=[VMEM_SPEC] * 3 + [HBM_SPEC] * 4,
        out_specs=[VMEM_SPEC] * 3,
        out_shape=[
            jax.ShapeDtypeStruct((2, 8, 128), F32),
            jax.ShapeDtypeStruct((virt, virt), F32),
            jax.ShapeDtypeStruct((virt, virt), F32),
        ],
        scratch_shapes=[
            pltpu.VMEM((1, count), jnp.int32),
            pltpu.VMEM((1, count), jnp.int32),
            pltpu.VMEM((1, count), F32),
            pltpu.VMEM((1, virt), F32),
            pltpu.SemaphoreType.DMA((4,)),
        ],
        compiler_params=pltpu.CompilerParams(vmem_limit_bytes=8 << 20),
        cost_estimate=pl.CostEstimate(flops=0, bytes_accessed=1 << 20, transcendentals=0),
        name="book",
    )(
        jnp.full((8, 128), group, jnp.int32),
        jnp.full((8, 128), core, jnp.int32),
        own,
        in_hbm(partner.reshape(1, count)),
        in_hbm(owner.reshape(1, count)),
        in_hbm(pair_energy.reshape(1, count)),
        in_hbm(virt_energy.reshape(1, virt)),
    )


def pack_kernel(pick_ref, own_ref, other_ref, out_ref, *, side):
    tiles = lax.dot_general(pick_ref[0], own_ref[...], NT, preferred_element_type=F32)
    tiles += lax.dot_general(pick_ref[1], other_ref[...], NT, preferred_element_type=F32)
    out_ref[...] = jnp.dot(tiles.astype(BF16), swap_matrix(side), preferred_element_type=F32).astype(BF16)


def pack(pick, own, other, side):
    return pl.pallas_call(
        lambda *refs: pack_kernel(*refs, side=side),
        in_specs=[VMEM_SPEC] * 3,
        out_specs=VMEM_SPEC,
        out_shape=jax.ShapeDtypeStruct((pick.shape[1], own.shape[0]), BF16),
        compiler_params=pltpu.CompilerParams(vmem_limit_bytes=8 << 20),
        name="pack",
    )(pick, own, other)


def ladder_kernel(
    near_ref, core_ref, tiles_ref, own_ref, own_hbm, other_hbm, out_ref, turned, rest_ref, other_ref, sems, *, side
):
    near = near_ref[0] > 0
    naux, virt, _ = other_ref.shape
    skipped = NEAR_HEAD - FAR_HEAD
    tail = pl.ds(skipped, naux - NEAR_HEAD)
    middle = pltpu.make_async_copy(own_hbm.at[pl.ds(FAR_HEAD, skipped)], rest_ref.at[pl.ds(0, skipped)], sems.at[0])
    rest = pltpu.make_async_copy(own_hbm.at[pl.ds(NEAR_HEAD, naux - NEAR_HEAD)], rest_ref.at[tail], sems.at[1])
    fetch = pltpu.make_async_copy(other_hbm, other_ref, sems.at[2])

    @pl.when(jnp.logical_not(near))
    def _():
        middle.start()

    rest.start()
    fetch.start()
    half_lanes = virt // 2
    per_vector = half_lanes // side
    first_core = jnp.broadcast_to(core_ref[:1, :] == 0, (side, half_lanes))

    def piece(z, core, half):
        rows = pl.ds(z * side, side)
        lanes = pl.ds(half * half_lanes, half_lanes)
        own = tiles_ref[0, rows, lanes]
        other = tiles_ref[1, rows, lanes]
        return jnp.where(first_core, own, other) if core == 0 else jnp.where(first_core, other, own)

    order = [(half, high) for half in range(2) for high in range(2)]
    vectors = []
    for low in range(per_vector):
        z_low, core = low // 2, low % 2
        vectors.append(
            jnp.concatenate([piece(high * (per_vector // 2) + z_low, core, half) for half, high in order], axis=0)
        )
    lane_group = iota(vectors[0].shape, 1) // side
    step = 1
    while step < per_vector:
        keep = (lane_group & step) == 0
        shift = step * side
        for i in range(per_vector):
            if i & step:
                continue
            j = i | step
            a, b = vectors[i], vectors[j]
            vectors[i] = jnp.where(keep, a, pltpu.roll(b, shift, 1))
            vectors[j] = jnp.where(keep, pltpu.roll(a, half_lanes - shift, 1), b)
        step *= 2
    for s_low in range(per_vector):
        for k, (half, high) in enumerate(order):
            rows = pl.ds((half * per_vector + s_low) * side, side)
            lanes = pl.ds(high * half_lanes, half_lanes)
            turned[rows, lanes] = vectors[s_low][k * side : (k + 1) * side]
    amp_t = jnp.dot(swap_matrix(side), turned[...], preferred_element_type=F32).astype(BF16)

    def run(blocks):
        total = jnp.zeros((virt, virt), F32)
        for block, copies in blocks:
            for copy in copies:
                copy.wait()
            count = block.shape[0]
            rows = block[...].reshape(count * virt, virt)
            product = jnp.dot(rows, amp_t, preferred_element_type=F32).astype(BF16)
            for q in range(count):
                total += lax.dot_general(
                    product[q * virt : (q + 1) * virt], block[q], NT, preferred_element_type=F32
                )
        out_ref[...] = total

    @pl.when(near)
    def _():
        run(((own_ref, ()), (rest_ref.at[tail], (rest,)), (other_ref, (fetch,))))

    @pl.when(jnp.logical_not(near))
    def _():
        run(((own_ref.at[pl.ds(0, FAR_HEAD)], ()), (rest_ref, (middle, rest)), (other_ref, (fetch,))))


def ladder(near, core, tiles, own, three_index, three_other, side):
    naux, virt, _ = three_index.shape
    return pl.pallas_call(
        lambda *refs: ladder_kernel(*refs, side=side),
        in_specs=[SMEM_SPEC] + [VMEM_SPEC] * 3 + [HBM_SPEC] * 2,
        out_specs=VMEM_SPEC,
        out_shape=jax.ShapeDtypeStruct((virt, virt), F32),
        scratch_shapes=[
            pltpu.VMEM((virt, virt), BF16),
            pltpu.VMEM((naux - FAR_HEAD, virt, virt), BF16),
            pltpu.VMEM((naux, virt, virt), BF16),
            pltpu.SemaphoreType.DMA((3,)),
        ],
        compiler_params=pltpu.CompilerParams(vmem_limit_bytes=40 << 20),
        name="ladder",
    )(
        near,
        jnp.full((8, 128), core, jnp.int32),
        tiles,
        own,
        in_hbm(three_index),
        in_hbm(three_other),
    )


def merge_kernel(base_ref, factor_ref, other_ref, out_ref):
    total = base_ref[...] + other_ref[...] * factor_ref[...]
    out_ref[...] = total.astype(BF16).reshape(out_ref.shape)


def merge(base, factor, other, aux):
    virt = base.shape[0]
    return pl.pallas_call(
        merge_kernel,
        in_specs=[VMEM_SPEC] * 3,
        out_specs=VMEM_SPEC,
        out_shape=jax.ShapeDtypeStruct((aux, virt // aux, virt), BF16),
        compiler_params=pltpu.CompilerParams(vmem_limit_bytes=8 << 20),
        name="merge",
    )(base, factor, other)


def gather_kernel(shares_ref, out_ref):
    for core in range(2):
        total = shares_ref[core].astype(F32)
        for k in range(core + 2, shares_ref.shape[0], 2):
            total += shares_ref[k].astype(F32)
        done = total.astype(BF16)
        for k in range(out_ref.shape[0]):
            out_ref[k, core] = done


def gather(shares, groups):
    return pl.pallas_call(
        gather_kernel,
        in_specs=[VMEM_SPEC],
        out_specs=VMEM_SPEC,
        out_shape=jax.ShapeDtypeStruct((groups, 2) + shares.shape[1:], BF16),
        compiler_params=pltpu.CompilerParams(vmem_limit_bytes=8 << 20),
        name="gather",
    )(shares)


def select_kernel(info_ref, found_ref, out_ref):
    for k in range(out_ref.shape[0]):
        index = info_ref[1, k, 0].astype(jnp.int32)
        block = found_ref[jnp.maximum(index - 1, 0)].astype(F32)
        out_ref[k] = jnp.where(index > 0, block, 0.0)


def select(info, found, capacity):
    return pl.pallas_call(
        select_kernel,
        in_specs=[VMEM_SPEC] * 2,
        out_specs=VMEM_SPEC,
        out_shape=jax.ShapeDtypeStruct((capacity,) + found.shape[1:], F32),
        compiler_params=pltpu.CompilerParams(vmem_limit_bytes=8 << 20),
        name="select",
    )(info, found)


def per_device(amplitudes, three_index, virt_energy, pair_energy, owner, partner):
    aux_axes = ("z", "core")
    swap = [(0, 1), (1, 0)]
    aux = lax.axis_size(aux_axes)
    depth = lax.axis_size("z")
    groups = lax.axis_size("pairs")
    core = lax.axis_index("core")
    pairs_all, side, _ = amplitudes.shape
    virt = three_index.shape[1]
    capacity = 2 * (pairs_all // groups)
    near = (lax.axis_index("z") < depth // 2).astype(jnp.int32).reshape(1)
    amp = jnp.transpose(amplitudes, (1, 2, 0)).reshape(side * side, pairs_all)
    amp_other = lax.ppermute(amp, "core", swap)
    three_other = lax.ppermute(three_index, "core", swap)
    pick, amp_own, own = plan(near, core, amp, partner, three_index)
    tiles = pack(pick, amp_own, amp_other, side)
    outgoing = jnp.broadcast_to(
        tiles.reshape(1, groups, 2, side * side), (depth, groups, 2, side * side)
    ).reshape(depth * groups, 2, side * side)
    arrived = lax.all_to_all(outgoing, ("z", "pairs"), split_axis=0, concat_axis=0, tiled=True)
    arrived = jnp.transpose(arrived, (1, 0, 2))
    turned = ladder(near, core, arrived, own, three_index, three_other, side)
    traded = lax.ppermute(turned, "core", swap)
    info, base, factor = book(lax.axis_index("pairs"), core, turned, partner, owner, pair_energy, virt_energy, capacity)
    partial = merge(base, factor, traded, aux)
    shares = lax.all_to_all(partial, aux_axes, split_axis=0, concat_axis=0, tiled=True)
    spread = gather(shares, groups)
    found = lax.all_to_all(spread, "pairs", split_axis=0, concat_axis=0, tiled=True)
    return select(info, found.reshape(pairs_all, side, virt), capacity)


def solution(mesh):
    groups = mesh.shape["pairs"]
    devices = mesh.devices.reshape(mesh.shape["aux"] // 2, 2, groups)
    split = Mesh(devices, ("z", "core", "pairs"))
    aux = ("z", "core")
    placed = (P(None, aux, "pairs"), P(aux, None, None), P(), P(), P(), P())
    return jax.shard_map(
        per_device, mesh=split, in_specs=placed, out_specs=P("pairs", aux, None), check_vma=False
    )
```

```python
import jax
import jax.numpy as jnp
from jax import lax
from jax.experimental import pallas as pl
from jax.experimental.pallas import tpu as pltpu
from jax.sharding import Mesh
from jax.sharding import PartitionSpec as P


BF16 = jnp.bfloat16
F32 = jnp.float32
NT = (((1,), (1,)), ((), ()))
NEAR_HEAD = 14
FAR_HEAD = 8
VMEM_SPEC = pl.BlockSpec(memory_space=pltpu.VMEM)
HBM_SPEC = pl.BlockSpec(memory_space=pltpu.HBM)
SMEM_SPEC = pl.BlockSpec(memory_space=pltpu.SMEM)


def in_hbm(x):
    return pltpu.with_memory_space_constraint(x, pltpu.HBM)


def iota(shape, dim):
    return lax.broadcasted_iota(jnp.int32, shape, dim)


def swap_matrix(side):
    full = side * side
    turned = (iota((full, full), 0) % side) * side + iota((full, full), 0) // side
    return jnp.where(turned == iota((full, full), 1), 1.0, 0.0).astype(BF16)


def order_of(partner, row, col):
    leads = (partner > col).astype(jnp.int32)
    fixed = (partner == col).astype(jnp.int32)
    low = jnp.minimum(partner, col)
    diagonal = row == col

    def down(x):
        return jnp.sum(jnp.where(diagonal, x, 0), axis=1, keepdims=True)

    lead_rank = jnp.sum(jnp.where(row < low, down(leads), 0), axis=0, keepdims=True)
    fixed_rank = jnp.sum(jnp.where(row < col, down(fixed), 0), axis=0, keepdims=True)
    leaders = jnp.sum(leads[:1], axis=1, keepdims=True)
    late = (col[:1] > partner[:1]).astype(jnp.int32)
    place = jnp.where(fixed[:1] > 0, 2 * leaders + fixed_rank, 2 * lead_rank + late)
    return place, leaders, down


def plan_kernel(
    near_ref, core_ref, amp_hbm, partner_hbm, three_hbm, pick_ref, amp_ref, own_ref, partner_ref, sems
):
    near = near_ref[0] > 0
    kept = own_ref.shape[0]
    copies = [
        pltpu.make_async_copy(partner_hbm, partner_ref, sems.at[0]),
        pltpu.make_async_copy(amp_hbm, amp_ref, sems.at[1]),
    ]
    head = pl.ds(0, FAR_HEAD)
    tail = pl.ds(FAR_HEAD, kept - FAR_HEAD)
    copies.append(pltpu.make_async_copy(three_hbm.at[head], own_ref.at[head], sems.at[2]))
    rest = pltpu.make_async_copy(three_hbm.at[tail], own_ref.at[tail], sems.at[3])
    for copy in copies:
        copy.start()

    @pl.when(near)
    def _():
        rest.start()

    count = partner_ref.shape[1]
    square = (count, count)
    row = iota(square, 0)
    col = iota(square, 1)
    slot = row - row % 2 + jnp.broadcast_to(core_ref[:1, :count], square)
    copies[0].wait()
    partner = jnp.broadcast_to(partner_ref[...], square)
    place, _, _ = order_of(partner, row, col)
    hit = jnp.broadcast_to(place, square) == slot
    for which in range(2):
        pick_ref[which] = jnp.where(hit & (row % 2 == which), 1.0, 0.0).astype(BF16)
    for copy in copies[1:]:
        copy.wait()

    @pl.when(near)
    def _():
        rest.wait()


def plan(near, core, amp, partner, three_index):
    count = partner.shape[0]
    return pl.pallas_call(
        plan_kernel,
        in_specs=[SMEM_SPEC, VMEM_SPEC] + [HBM_SPEC] * 3,
        out_specs=[VMEM_SPEC] * 3,
        out_shape=[
            jax.ShapeDtypeStruct((2, count, count), BF16),
            jax.ShapeDtypeStruct(amp.shape, BF16),
            jax.ShapeDtypeStruct((NEAR_HEAD,) + three_index.shape[1:], BF16),
        ],
        scratch_shapes=[pltpu.VMEM((1, count), jnp.int32), pltpu.SemaphoreType.DMA((4,))],
        compiler_params=pltpu.CompilerParams(vmem_limit_bytes=8 << 20),
        cost_estimate=pl.CostEstimate(flops=0, bytes_accessed=2 << 20, transcendentals=0),
        name="plan",
    )(
        near,
        jnp.full((8, 128), core, jnp.int32),
        in_hbm(amp),
        in_hbm(partner.reshape(1, count)),
        in_hbm(three_index),
    )


def book_kernel(
    group_ref, core_ref, own_ref, partner_hbm, owner_hbm, energy_hbm, virt_hbm, info_ref, base_ref, factor_ref, partner_ref, owner_ref, energy_ref, virt_ref, sems, *, capacity
):
    sources = (partner_hbm, owner_hbm, energy_hbm, virt_hbm)
    targets = (partner_ref, owner_ref, energy_ref, virt_ref)
    copies = [pltpu.make_async_copy(a, b, sems.at[i]) for i, (a, b) in enumerate(zip(sources, targets))]
    for copy in copies:
        copy.start()
    count = partner_ref.shape[1]
    virt = virt_ref.shape[1]
    square = (count, count)
    small = (8, count)
    wide = (8, 128)
    group = group_ref[...]
    row = iota(square, 0)
    col = iota(square, 1)
    for copy in copies:
        copy.wait()
    partner = jnp.broadcast_to(partner_ref[...], square)
    owner = jnp.broadcast_to(owner_ref[...], square)
    place, leaders, down = order_of(partner, row, col)
    slot_rank = jnp.sum(((down(owner) == owner) & (row < col)).astype(jnp.int32), axis=0, keepdims=True)
    position = owner_ref[...] * capacity + slot_rank
    my_group = jnp.broadcast_to(group[:1, :count], small)
    mine = jnp.broadcast_to(position, small) == iota(small, 0) + capacity * my_group
    found = jnp.sum(jnp.where(mine, jnp.broadcast_to(place + 1, small), 0), axis=1, keepdims=True)
    chosen = jnp.broadcast_to(place, small) == iota(small, 0) + 2 * my_group
    energy = jnp.sum(jnp.where(chosen, jnp.broadcast_to(energy_ref[...], small), 0.0), axis=1, keepdims=True)
    same = jnp.where(group >= jnp.broadcast_to(leaders, wide), 1.0, 0.0)
    info_ref[0] = jnp.where(iota(wide, 0) == 2, same, jnp.broadcast_to(energy, wide))
    info_ref[1] = jnp.broadcast_to(found, wide).astype(F32)
    rows_of = jnp.broadcast_to(virt_ref[...], (virt, virt))
    sums = rows_of + rows_of.T
    on_first = jnp.broadcast_to(core_ref[:1, :1] == 0, (1, 1))
    first, second = info_ref[0, 0:1, 0:1], info_ref[0, 1:2, 0:1]
    alone = jnp.broadcast_to(info_ref[0, 2:3, 0:1] > 0.5, own_ref.shape)
    own = own_ref[...] / (sums - jnp.where(on_first, first, second))
    base_ref[...] = own.T + jnp.where(alone, own, 0.0)
    factor_ref[...] = jnp.where(alone, 0.0, 1.0 / (sums - jnp.where(on_first, second, first)))


def book(group, core, own, partner, owner, pair_energy, virt_energy, capacity):
    count = partner.shape[0]
    virt = virt_energy.shape[0]
    return pl.pallas_call(
        lambda *refs: book_kernel(*refs, capacity=capacity),
        in_specs=[VMEM_SPEC] * 3 + [HBM_SPEC] * 4,
        out_specs=[VMEM_SPEC] * 3,
        out_shape=[
            jax.ShapeDtypeStruct((2, 8, 128), F32),
            jax.ShapeDtypeStruct((virt, virt), F32),
            jax.ShapeDtypeStruct((virt, virt), F32),
        ],
        scratch_shapes=[
            pltpu.VMEM((1, count), jnp.int32),
            pltpu.VMEM((1, count), jnp.int32),
            pltpu.VMEM((1, count), F32),
            pltpu.VMEM((1, virt), F32),
            pltpu.SemaphoreType.DMA((4,)),
        ],
        compiler_params=pltpu.CompilerParams(vmem_limit_bytes=8 << 20),
        cost_estimate=pl.CostEstimate(flops=0, bytes_accessed=1 << 20, transcendentals=0),
        name="book",
    )(
        jnp.full((8, 128), group, jnp.int32),
        jnp.full((8, 128), core, jnp.int32),
        own,
        in_hbm(partner.reshape(1, count)),
        in_hbm(owner.reshape(1, count)),
        in_hbm(pair_energy.reshape(1, count)),
        in_hbm(virt_energy.reshape(1, virt)),
    )


def pack_kernel(pick_ref, own_ref, other_ref, out_ref):
    tiles = lax.dot_general(pick_ref[0], own_ref[...], NT, preferred_element_type=F32)
    tiles += lax.dot_general(pick_ref[1], other_ref[...], NT, preferred_element_type=F32)
    out_ref[...] = tiles.astype(BF16)


def pack(pick, own, other):
    return pl.pallas_call(
        pack_kernel,
        in_specs=[VMEM_SPEC] * 3,
        out_specs=VMEM_SPEC,
        out_shape=jax.ShapeDtypeStruct((pick.shape[1], own.shape[0]), BF16),
        compiler_params=pltpu.CompilerParams(vmem_limit_bytes=8 << 20),
        name="pack",
    )(pick, own, other)


def ladder_kernel(
    near_ref, core_ref, raw_ref, own_ref, own_hbm, other_hbm, out_ref, tiles_ref, turned, rest_ref, other_ref, sems, *, side
):
    near = near_ref[0] > 0
    naux, virt, _ = other_ref.shape
    skipped = NEAR_HEAD - FAR_HEAD
    tail = pl.ds(skipped, naux - NEAR_HEAD)
    middle = pltpu.make_async_copy(own_hbm.at[pl.ds(FAR_HEAD, skipped)], rest_ref.at[pl.ds(0, skipped)], sems.at[0])
    rest = pltpu.make_async_copy(own_hbm.at[pl.ds(NEAR_HEAD, naux - NEAR_HEAD)], rest_ref.at[tail], sems.at[1])
    fetch = pltpu.make_async_copy(other_hbm, other_ref, sems.at[2])

    @pl.when(jnp.logical_not(near))
    def _():
        middle.start()

    rest.start()
    fetch.start()
    swap = swap_matrix(side)
    for which in range(2):
        tiles_ref[which] = jnp.dot(raw_ref[which], swap, preferred_element_type=F32).astype(BF16)
    half_lanes = virt // 2
    per_vector = half_lanes // side
    first_core = jnp.broadcast_to(core_ref[:1, :] == 0, (side, half_lanes))

    def piece(z, core, half):
        rows = pl.ds(z * side, side)
        lanes = pl.ds(half * half_lanes, half_lanes)
        own = tiles_ref[0, rows, lanes]
        other = tiles_ref[1, rows, lanes]
        return jnp.where(first_core, own, other) if core == 0 else jnp.where(first_core, other, own)

    order = [(half, high) for half in range(2) for high in range(2)]
    vectors = []
    for low in range(per_vector):
        z_low, core = low // 2, low % 2
        vectors.append(
            jnp.concatenate([piece(high * (per_vector // 2) + z_low, core, half) for half, high in order], axis=0)
        )
    lane_group = iota(vectors[0].shape, 1) // side
    step = 1
    while step < per_vector:
        keep = (lane_group & step) == 0
        shift = step * side
        for i in range(per_vector):
            if i & step:
                continue
            j = i | step
            a, b = vectors[i], vectors[j]
            vectors[i] = jnp.where(keep, a, pltpu.roll(b, shift, 1))
            vectors[j] = jnp.where(keep, pltpu.roll(a, half_lanes - shift, 1), b)
        step *= 2
    for s_low in range(per_vector):
        for k, (half, high) in enumerate(order):
            rows = pl.ds((half * per_vector + s_low) * side, side)
            lanes = pl.ds(high * half_lanes, half_lanes)
            turned[rows, lanes] = vectors[s_low][k * side : (k + 1) * side]
    amp_t = jnp.dot(swap, turned[...], preferred_element_type=F32).astype(BF16)

    def run(blocks):
        total = jnp.zeros((virt, virt), F32)
        for block, copies in blocks:
            for copy in copies:
                copy.wait()
            count = block.shape[0]
            rows = block[...].reshape(count * virt, virt)
            product = jnp.dot(rows, amp_t, preferred_element_type=F32).astype(BF16)
            for q in range(count):
                total += lax.dot_general(
                    product[q * virt : (q + 1) * virt], block[q], NT, preferred_element_type=F32
                )
        out_ref[...] = total

    @pl.when(near)
    def _():
        run(((own_ref, ()), (rest_ref.at[tail], (rest,)), (other_ref, (fetch,))))

    @pl.when(jnp.logical_not(near))
    def _():
        run(((own_ref.at[pl.ds(0, FAR_HEAD)], ()), (rest_ref, (middle, rest)), (other_ref, (fetch,))))


def ladder(near, core, tiles, own, three_index, three_other, side):
    naux, virt, _ = three_index.shape
    return pl.pallas_call(
        lambda *refs: ladder_kernel(*refs, side=side),
        in_specs=[SMEM_SPEC] + [VMEM_SPEC] * 3 + [HBM_SPEC] * 2,
        out_specs=VMEM_SPEC,
        out_shape=jax.ShapeDtypeStruct((virt, virt), F32),
        scratch_shapes=[
            pltpu.VMEM(tiles.shape, BF16),
            pltpu.VMEM((virt, virt), BF16),
            pltpu.VMEM((naux - FAR_HEAD, virt, virt), BF16),
            pltpu.VMEM((naux, virt, virt), BF16),
            pltpu.SemaphoreType.DMA((3,)),
        ],
        compiler_params=pltpu.CompilerParams(vmem_limit_bytes=40 << 20),
        name="ladder",
    )(
        near,
        jnp.full((8, 128), core, jnp.int32),
        tiles,
        own,
        in_hbm(three_index),
        in_hbm(three_other),
    )


def merge_kernel(base_ref, factor_ref, other_ref, out_ref):
    total = base_ref[...] + other_ref[...] * factor_ref[...]
    out_ref[...] = total.astype(BF16).reshape(out_ref.shape)


def merge(base, factor, other, aux):
    virt = base.shape[0]
    return pl.pallas_call(
        merge_kernel,
        in_specs=[VMEM_SPEC] * 3,
        out_specs=VMEM_SPEC,
        out_shape=jax.ShapeDtypeStruct((aux, virt // aux, virt), BF16),
        compiler_params=pltpu.CompilerParams(vmem_limit_bytes=8 << 20),
        name="merge",
    )(base, factor, other)


def gather_kernel(shares_ref, out_ref):
    for core in range(2):
        total = shares_ref[core].astype(F32)
        for k in range(core + 2, shares_ref.shape[0], 2):
            total += shares_ref[k].astype(F32)
        done = total.astype(BF16)
        for k in range(out_ref.shape[0]):
            out_ref[k, core] = done


def gather(shares, groups):
    return pl.pallas_call(
        gather_kernel,
        in_specs=[VMEM_SPEC],
        out_specs=VMEM_SPEC,
        out_shape=jax.ShapeDtypeStruct((groups, 2) + shares.shape[1:], BF16),
        compiler_params=pltpu.CompilerParams(vmem_limit_bytes=8 << 20),
        name="gather",
    )(shares)


def select_kernel(info_ref, found_ref, out_ref):
    for k in range(out_ref.shape[0]):
        index = info_ref[1, k, 0].astype(jnp.int32)
        block = found_ref[jnp.maximum(index - 1, 0)].astype(F32)
        out_ref[k] = jnp.where(index > 0, block, 0.0)


def select(info, found, capacity):
    return pl.pallas_call(
        select_kernel,
        in_specs=[VMEM_SPEC] * 2,
        out_specs=VMEM_SPEC,
        out_shape=jax.ShapeDtypeStruct((capacity,) + found.shape[1:], F32),
        compiler_params=pltpu.CompilerParams(vmem_limit_bytes=8 << 20),
        name="select",
    )(info, found)


def per_device(amplitudes, three_index, virt_energy, pair_energy, owner, partner):
    aux_axes = ("z", "core")
    swap = [(0, 1), (1, 0)]
    aux = lax.axis_size(aux_axes)
    depth = lax.axis_size("z")
    groups = lax.axis_size("pairs")
    core = lax.axis_index("core")
    pairs_all, side, _ = amplitudes.shape
    virt = three_index.shape[1]
    capacity = 2 * (pairs_all // groups)
    near = (lax.axis_index("z") < depth // 2).astype(jnp.int32).reshape(1)
    amp = jnp.transpose(amplitudes, (1, 2, 0)).reshape(side * side, pairs_all)
    amp_other = lax.ppermute(amp, "core", swap)
    three_other = lax.ppermute(three_index, "core", swap)
    pick, amp_own, own = plan(near, core, amp, partner, three_index)
    tiles = pack(pick, amp_own, amp_other)
    outgoing = jnp.broadcast_to(
        tiles.reshape(1, groups, 2, side * side), (depth, groups, 2, side * side)
    ).reshape(depth * groups, 2, side * side)
    arrived = lax.all_to_all(outgoing, ("z", "pairs"), split_axis=0, concat_axis=0, tiled=True)
    arrived = jnp.transpose(arrived, (1, 0, 2))
    turned = ladder(near, core, arrived, own, three_index, three_other, side)
    traded = lax.ppermute(turned, "core", swap)
    info, base, factor = book(lax.axis_index("pairs"), core, turned, partner, owner, pair_energy, virt_energy, capacity)
    partial = merge(base, factor, traded, aux)
    shares = lax.all_to_all(partial, aux_axes, split_axis=0, concat_axis=0, tiled=True)
    spread = gather(shares, groups)
    found = lax.all_to_all(spread, "pairs", split_axis=0, concat_axis=0, tiled=True)
    return select(info, found.reshape(pairs_all, side, virt), capacity)


def solution(mesh):
    groups = mesh.shape["pairs"]
    devices = mesh.devices.reshape(mesh.shape["aux"] // 2, 2, groups)
    split = Mesh(devices, ("z", "core", "pairs"))
    aux = ("z", "core")
    placed = (P(None, aux, "pairs"), P(aux, None, None), P(), P(), P(), P())
    return jax.shard_map(
        per_device, mesh=split, in_specs=placed, out_specs=P("pairs", aux, None), check_vma=False
    )
```

```python
import jax
import jax.numpy as jnp
from jax import lax
from jax.experimental import pallas as pl
from jax.experimental.pallas import tpu as pltpu
from jax.sharding import Mesh
from jax.sharding import PartitionSpec as P


BF16 = jnp.bfloat16
F32 = jnp.float32
NT = (((1,), (1,)), ((), ()))
NEAR_HEAD = 12
FAR_HEAD = 4
VMEM_SPEC = pl.BlockSpec(memory_space=pltpu.VMEM)
HBM_SPEC = pl.BlockSpec(memory_space=pltpu.HBM)
SMEM_SPEC = pl.BlockSpec(memory_space=pltpu.SMEM)


def in_hbm(x):
    return pltpu.with_memory_space_constraint(x, pltpu.HBM)


def iota(shape, dim):
    return lax.broadcasted_iota(jnp.int32, shape, dim)


def swap_matrix(side):
    full = side * side
    turned = (iota((full, full), 0) % side) * side + iota((full, full), 0) // side
    return jnp.where(turned == iota((full, full), 1), 1.0, 0.0).astype(BF16)


def order_of(partner, row, col):
    leads = (partner > col).astype(jnp.int32)
    fixed = (partner == col).astype(jnp.int32)
    low = jnp.minimum(partner, col)
    diagonal = row == col

    def down(x):
        return jnp.sum(jnp.where(diagonal, x, 0), axis=1, keepdims=True)

    lead_rank = jnp.sum(jnp.where(row < low, down(leads), 0), axis=0, keepdims=True)
    fixed_rank = jnp.sum(jnp.where(row < col, down(fixed), 0), axis=0, keepdims=True)
    leaders = jnp.sum(leads[:1], axis=1, keepdims=True)
    late = (col[:1] > partner[:1]).astype(jnp.int32)
    place = jnp.where(fixed[:1] > 0, 2 * leaders + fixed_rank, 2 * lead_rank + late)
    return place, leaders, down


def plan_kernel(
    near_ref, core_ref, amp_hbm, partner_hbm, three_hbm, pick_ref, amp_ref, own_ref, partner_ref, sems
):
    near = near_ref[0] > 0
    kept = own_ref.shape[0]
    copies = [
        pltpu.make_async_copy(partner_hbm, partner_ref, sems.at[0]),
        pltpu.make_async_copy(amp_hbm, amp_ref, sems.at[1]),
    ]
    head = pl.ds(0, FAR_HEAD)
    tail = pl.ds(FAR_HEAD, kept - FAR_HEAD)
    copies.append(pltpu.make_async_copy(three_hbm.at[head], own_ref.at[head], sems.at[2]))
    rest = pltpu.make_async_copy(three_hbm.at[tail], own_ref.at[tail], sems.at[3])
    for copy in copies:
        copy.start()

    @pl.when(near)
    def _():
        rest.start()

    count = partner_ref.shape[1]
    square = (count, count)
    row = iota(square, 0)
    col = iota(square, 1)
    slot = row - row % 2 + jnp.broadcast_to(core_ref[:1, :count], square)
    copies[0].wait()
    partner = jnp.broadcast_to(partner_ref[...], square)
    place, _, _ = order_of(partner, row, col)
    hit = jnp.broadcast_to(place, square) == slot
    for which in range(2):
        pick_ref[which] = jnp.where(hit & (row % 2 == which), 1.0, 0.0).astype(BF16)
    for copy in copies[1:]:
        copy.wait()

    @pl.when(near)
    def _():
        rest.wait()


def plan(near, core, amp, partner, three_index):
    count = partner.shape[0]
    return pl.pallas_call(
        plan_kernel,
        in_specs=[SMEM_SPEC, VMEM_SPEC] + [HBM_SPEC] * 3,
        out_specs=[VMEM_SPEC] * 3,
        out_shape=[
            jax.ShapeDtypeStruct((2, count, count), BF16),
            jax.ShapeDtypeStruct(amp.shape, BF16),
            jax.ShapeDtypeStruct((NEAR_HEAD,) + three_index.shape[1:], BF16),
        ],
        scratch_shapes=[pltpu.VMEM((1, count), jnp.int32), pltpu.SemaphoreType.DMA((4,))],
        compiler_params=pltpu.CompilerParams(vmem_limit_bytes=8 << 20),
        cost_estimate=pl.CostEstimate(flops=0, bytes_accessed=2 << 20, transcendentals=0),
        name="plan",
    )(
        near,
        jnp.full((8, 128), core, jnp.int32),
        in_hbm(amp),
        in_hbm(partner.reshape(1, count)),
        in_hbm(three_index),
    )


def book_kernel(
    group_ref, core_ref, own_ref, partner_hbm, owner_hbm, energy_hbm, virt_hbm, info_ref, base_ref, factor_ref, partner_ref, owner_ref, energy_ref, virt_ref, sems, *, capacity
):
    sources = (partner_hbm, owner_hbm, energy_hbm, virt_hbm)
    targets = (partner_ref, owner_ref, energy_ref, virt_ref)
    copies = [pltpu.make_async_copy(a, b, sems.at[i]) for i, (a, b) in enumerate(zip(sources, targets))]
    for copy in copies:
        copy.start()
    count = partner_ref.shape[1]
    virt = virt_ref.shape[1]
    square = (count, count)
    small = (8, count)
    wide = (8, 128)
    group = group_ref[...]
    row = iota(square, 0)
    col = iota(square, 1)
    for copy in copies:
        copy.wait()
    partner = jnp.broadcast_to(partner_ref[...], square)
    owner = jnp.broadcast_to(owner_ref[...], square)
    place, leaders, down = order_of(partner, row, col)
    slot_rank = jnp.sum(((down(owner) == owner) & (row < col)).astype(jnp.int32), axis=0, keepdims=True)
    position = owner_ref[...] * capacity + slot_rank
    my_group = jnp.broadcast_to(group[:1, :count], small)
    mine = jnp.broadcast_to(position, small) == iota(small, 0) + capacity * my_group
    found = jnp.sum(jnp.where(mine, jnp.broadcast_to(place + 1, small), 0), axis=1, keepdims=True)
    chosen = jnp.broadcast_to(place, small) == iota(small, 0) + 2 * my_group
    energy = jnp.sum(jnp.where(chosen, jnp.broadcast_to(energy_ref[...], small), 0.0), axis=1, keepdims=True)
    same = jnp.where(group >= jnp.broadcast_to(leaders, wide), 1.0, 0.0)
    info_ref[0] = jnp.where(iota(wide, 0) == 2, same, jnp.broadcast_to(energy, wide))
    info_ref[1] = jnp.broadcast_to(found, wide).astype(F32)
    rows_of = jnp.broadcast_to(virt_ref[...], (virt, virt))
    sums = rows_of + rows_of.T
    on_first = jnp.broadcast_to(core_ref[:1, :1] == 0, (1, 1))
    first, second = info_ref[0, 0:1, 0:1], info_ref[0, 1:2, 0:1]
    alone = jnp.broadcast_to(info_ref[0, 2:3, 0:1] > 0.5, own_ref.shape)
    own = own_ref[...] / (sums - jnp.where(on_first, first, second))
    base_ref[...] = own.T + jnp.where(alone, own, 0.0)
    factor_ref[...] = jnp.where(alone, 0.0, 1.0 / (sums - jnp.where(on_first, second, first)))


def book(group, core, own, partner, owner, pair_energy, virt_energy, capacity):
    count = partner.shape[0]
    virt = virt_energy.shape[0]
    return pl.pallas_call(
        lambda *refs: book_kernel(*refs, capacity=capacity),
        in_specs=[VMEM_SPEC] * 3 + [HBM_SPEC] * 4,
        out_specs=[VMEM_SPEC] * 3,
        out_shape=[
            jax.ShapeDtypeStruct((2, 8, 128), F32),
            jax.ShapeDtypeStruct((virt, virt), F32),
            jax.ShapeDtypeStruct((virt, virt), F32),
        ],
        scratch_shapes=[
            pltpu.VMEM((1, count), jnp.int32),
            pltpu.VMEM((1, count), jnp.int32),
            pltpu.VMEM((1, count), F32),
            pltpu.VMEM((1, virt), F32),
            pltpu.SemaphoreType.DMA((4,)),
        ],
        compiler_params=pltpu.CompilerParams(vmem_limit_bytes=8 << 20),
        cost_estimate=pl.CostEstimate(flops=0, bytes_accessed=1 << 20, transcendentals=0),
        name="book",
    )(
        jnp.full((8, 128), group, jnp.int32),
        jnp.full((8, 128), core, jnp.int32),
        own,
        in_hbm(partner.reshape(1, count)),
        in_hbm(owner.reshape(1, count)),
        in_hbm(pair_energy.reshape(1, count)),
        in_hbm(virt_energy.reshape(1, virt)),
    )


def pack_kernel(pick_ref, own_ref, other_ref, out_ref, *, side):
    tiles = lax.dot_general(pick_ref[0], own_ref[...], NT, preferred_element_type=F32)
    tiles += lax.dot_general(pick_ref[1], other_ref[...], NT, preferred_element_type=F32)
    out_ref[...] = jnp.dot(tiles.astype(BF16), swap_matrix(side), preferred_element_type=F32).astype(BF16)


def pack(pick, own, other, side):
    return pl.pallas_call(
        lambda *refs: pack_kernel(*refs, side=side),
        in_specs=[VMEM_SPEC] * 3,
        out_specs=VMEM_SPEC,
        out_shape=jax.ShapeDtypeStruct((pick.shape[1], own.shape[0]), BF16),
        compiler_params=pltpu.CompilerParams(vmem_limit_bytes=8 << 20),
        name="pack",
    )(pick, own, other)


def ladder_kernel(
    near_ref, core_ref, tiles_ref, own_ref, own_hbm, other_hbm, out_ref, turned, rest_ref, other_ref, sems, *, side
):
    near = near_ref[0] > 0
    naux, virt, _ = other_ref.shape
    skipped = NEAR_HEAD - FAR_HEAD
    tail = pl.ds(skipped, naux - NEAR_HEAD)
    middle = pltpu.make_async_copy(own_hbm.at[pl.ds(FAR_HEAD, skipped)], rest_ref.at[pl.ds(0, skipped)], sems.at[0])
    rest = pltpu.make_async_copy(own_hbm.at[pl.ds(NEAR_HEAD, naux - NEAR_HEAD)], rest_ref.at[tail], sems.at[1])
    fetch = pltpu.make_async_copy(other_hbm, other_ref, sems.at[2])

    @pl.when(jnp.logical_not(near))
    def _():
        middle.start()

    rest.start()
    fetch.start()
    half_lanes = virt // 2
    per_vector = half_lanes // side
    first_core = jnp.broadcast_to(core_ref[:1, :] == 0, (side, half_lanes))

    def piece(z, core, half):
        rows = pl.ds(z * side, side)
        lanes = pl.ds(half * half_lanes, half_lanes)
        own = tiles_ref[0, rows, lanes]
        other = tiles_ref[1, rows, lanes]
        return jnp.where(first_core, own, other) if core == 0 else jnp.where(first_core, other, own)

    order = [(half, high) for half in range(2) for high in range(2)]
    vectors = []
    for low in range(per_vector):
        z_low, core = low // 2, low % 2
        vectors.append(
            jnp.concatenate([piece(high * (per_vector // 2) + z_low, core, half) for half, high in order], axis=0)
        )
    lane_group = iota(vectors[0].shape, 1) // side
    step = 1
    while step < per_vector:
        keep = (lane_group & step) == 0
        shift = step * side
        for i in range(per_vector):
            if i & step:
                continue
            j = i | step
            a, b = vectors[i], vectors[j]
            vectors[i] = jnp.where(keep, a, pltpu.roll(b, shift, 1))
            vectors[j] = jnp.where(keep, pltpu.roll(a, half_lanes - shift, 1), b)
        step *= 2
    for s_low in range(per_vector):
        for k, (half, high) in enumerate(order):
            rows = pl.ds((half * per_vector + s_low) * side, side)
            lanes = pl.ds(high * half_lanes, half_lanes)
            turned[rows, lanes] = vectors[s_low][k * side : (k + 1) * side]
    amp_t = jnp.dot(swap_matrix(side), turned[...], preferred_element_type=F32).astype(BF16)

    def run(blocks):
        total = jnp.zeros((virt, virt), F32)
        for block, copies in blocks:
            for copy in copies:
                copy.wait()
            count = block.shape[0]
            rows = block[...].reshape(count * virt, virt)
            product = jnp.dot(rows, amp_t, preferred_element_type=F32).astype(BF16)
            for q in range(count):
                total += lax.dot_general(
                    product[q * virt : (q + 1) * virt], block[q], NT, preferred_element_type=F32
                )
        out_ref[...] = total

    @pl.when(near)
    def _():
        run(((own_ref, ()), (rest_ref.at[tail], (rest,)), (other_ref, (fetch,))))

    @pl.when(jnp.logical_not(near))
    def _():
        run(
            (
                (own_ref.at[pl.ds(0, FAR_HEAD)], ()),
                (rest_ref.at[pl.ds(0, skipped)], (middle,)),
                (rest_ref.at[tail], (rest,)),
                (other_ref, (fetch,)),
            )
        )


def ladder(near, core, tiles, own, three_index, three_other, side):
    naux, virt, _ = three_index.shape
    return pl.pallas_call(
        lambda *refs: ladder_kernel(*refs, side=side),
        in_specs=[SMEM_SPEC] + [VMEM_SPEC] * 3 + [HBM_SPEC] * 2,
        out_specs=VMEM_SPEC,
        out_shape=jax.ShapeDtypeStruct((virt, virt), F32),
        scratch_shapes=[
            pltpu.VMEM((virt, virt), BF16),
            pltpu.VMEM((naux - FAR_HEAD, virt, virt), BF16),
            pltpu.VMEM((naux, virt, virt), BF16),
            pltpu.SemaphoreType.DMA((3,)),
        ],
        compiler_params=pltpu.CompilerParams(vmem_limit_bytes=40 << 20),
        name="ladder",
    )(
        near,
        jnp.full((8, 128), core, jnp.int32),
        tiles,
        own,
        in_hbm(three_index),
        in_hbm(three_other),
    )


def merge_kernel(base_ref, factor_ref, other_ref, out_ref):
    total = base_ref[...] + other_ref[...] * factor_ref[...]
    out_ref[...] = total.astype(BF16).reshape(out_ref.shape)


def merge(base, factor, other, aux):
    virt = base.shape[0]
    return pl.pallas_call(
        merge_kernel,
        in_specs=[VMEM_SPEC] * 3,
        out_specs=VMEM_SPEC,
        out_shape=jax.ShapeDtypeStruct((aux, virt // aux, virt), BF16),
        compiler_params=pltpu.CompilerParams(vmem_limit_bytes=8 << 20),
        name="merge",
    )(base, factor, other)


def gather_kernel(shares_ref, out_ref):
    for core in range(2):
        total = shares_ref[core].astype(F32)
        for k in range(core + 2, shares_ref.shape[0], 2):
            total += shares_ref[k].astype(F32)
        done = total.astype(BF16)
        for k in range(out_ref.shape[0]):
            out_ref[k, core] = done


def gather(shares, groups):
    return pl.pallas_call(
        gather_kernel,
        in_specs=[VMEM_SPEC],
        out_specs=VMEM_SPEC,
        out_shape=jax.ShapeDtypeStruct((groups, 2) + shares.shape[1:], BF16),
        compiler_params=pltpu.CompilerParams(vmem_limit_bytes=8 << 20),
        name="gather",
    )(shares)


def select_kernel(info_ref, found_ref, out_ref):
    for k in range(out_ref.shape[0]):
        index = info_ref[1, k, 0].astype(jnp.int32)
        block = found_ref[jnp.maximum(index - 1, 0)].astype(F32)
        out_ref[k] = jnp.where(index > 0, block, 0.0)


def select(info, found, capacity):
    return pl.pallas_call(
        select_kernel,
        in_specs=[VMEM_SPEC] * 2,
        out_specs=VMEM_SPEC,
        out_shape=jax.ShapeDtypeStruct((capacity,) + found.shape[1:], F32),
        compiler_params=pltpu.CompilerParams(vmem_limit_bytes=8 << 20),
        name="select",
    )(info, found)


def per_device(amplitudes, three_index, virt_energy, pair_energy, owner, partner):
    aux_axes = ("z", "core")
    swap = [(0, 1), (1, 0)]
    aux = lax.axis_size(aux_axes)
    depth = lax.axis_size("z")
    groups = lax.axis_size("pairs")
    core = lax.axis_index("core")
    pairs_all, side, _ = amplitudes.shape
    virt = three_index.shape[1]
    capacity = 2 * (pairs_all // groups)
    near = (lax.axis_index("z") < depth // 2).astype(jnp.int32).reshape(1)
    amp = jnp.transpose(amplitudes, (1, 2, 0)).reshape(side * side, pairs_all)
    amp_other = lax.ppermute(amp, "core", swap)
    three_other = lax.ppermute(three_index, "core", swap)
    pick, amp_own, own = plan(near, core, amp, partner, three_index)
    tiles = pack(pick, amp_own, amp_other, side)
    outgoing = jnp.broadcast_to(
        tiles.reshape(1, groups, 2, side * side), (depth, groups, 2, side * side)
    ).reshape(depth * groups, 2, side * side)
    arrived = lax.all_to_all(outgoing, ("z", "pairs"), split_axis=0, concat_axis=0, tiled=True)
    arrived = jnp.transpose(arrived, (1, 0, 2))
    turned = ladder(near, core, arrived, own, three_index, three_other, side)
    traded = lax.ppermute(turned, "core", swap)
    info, base, factor = book(lax.axis_index("pairs"), core, turned, partner, owner, pair_energy, virt_energy, capacity)
    partial = merge(base, factor, traded, aux)
    shares = lax.all_to_all(partial, aux_axes, split_axis=0, concat_axis=0, tiled=True)
    spread = gather(shares, groups)
    found = lax.all_to_all(spread, "pairs", split_axis=0, concat_axis=0, tiled=True)
    return select(info, found.reshape(pairs_all, side, virt), capacity)


def solution(mesh):
    groups = mesh.shape["pairs"]
    devices = mesh.devices.reshape(mesh.shape["aux"] // 2, 2, groups)
    split = Mesh(devices, ("z", "core", "pairs"))
    aux = ("z", "core")
    placed = (P(None, aux, "pairs"), P(aux, None, None), P(), P(), P(), P())
    return jax.shard_map(
        per_device, mesh=split, in_specs=placed, out_specs=P("pairs", aux, None), check_vma=False
    )
```

```python
import jax
import jax.numpy as jnp
from jax import lax
from jax.experimental import pallas as pl
from jax.experimental.pallas import tpu as pltpu
from jax.sharding import Mesh
from jax.sharding import PartitionSpec as P


BF16 = jnp.bfloat16
F32 = jnp.float32
NT = (((1,), (1,)), ((), ()))
NEAR_HEAD = 14
FAR_HEAD = 4
VMEM_SPEC = pl.BlockSpec(memory_space=pltpu.VMEM)
HBM_SPEC = pl.BlockSpec(memory_space=pltpu.HBM)
SMEM_SPEC = pl.BlockSpec(memory_space=pltpu.SMEM)


def in_hbm(x):
    return pltpu.with_memory_space_constraint(x, pltpu.HBM)


def iota(shape, dim):
    return lax.broadcasted_iota(jnp.int32, shape, dim)


def swap_matrix(side):
    full = side * side
    turned = (iota((full, full), 0) % side) * side + iota((full, full), 0) // side
    return jnp.where(turned == iota((full, full), 1), 1.0, 0.0).astype(BF16)


def order_of(partner, row, col):
    leads = (partner > col).astype(jnp.int32)
    fixed = (partner == col).astype(jnp.int32)
    low = jnp.minimum(partner, col)
    diagonal = row == col

    def down(x):
        return jnp.sum(jnp.where(diagonal, x, 0), axis=1, keepdims=True)

    lead_rank = jnp.sum(jnp.where(row < low, down(leads), 0), axis=0, keepdims=True)
    fixed_rank = jnp.sum(jnp.where(row < col, down(fixed), 0), axis=0, keepdims=True)
    leaders = jnp.sum(leads[:1], axis=1, keepdims=True)
    late = (col[:1] > partner[:1]).astype(jnp.int32)
    place = jnp.where(fixed[:1] > 0, 2 * leaders + fixed_rank, 2 * lead_rank + late)
    return place, leaders, down


def plan_kernel(
    near_ref, core_ref, amp_hbm, partner_hbm, three_hbm, pick_ref, amp_ref, own_ref, swap_ref, partner_ref, sems, *, side
):
    near = near_ref[0] > 0
    kept = own_ref.shape[0]
    copies = [
        pltpu.make_async_copy(partner_hbm, partner_ref, sems.at[0]),
        pltpu.make_async_copy(amp_hbm, amp_ref, sems.at[1]),
    ]
    head = pl.ds(0, FAR_HEAD)
    tail = pl.ds(FAR_HEAD, kept - FAR_HEAD)
    copies.append(pltpu.make_async_copy(three_hbm.at[head], own_ref.at[head], sems.at[2]))
    rest = pltpu.make_async_copy(three_hbm.at[tail], own_ref.at[tail], sems.at[3])
    for copy in copies:
        copy.start()

    @pl.when(near)
    def _():
        rest.start()

    swap_ref[...] = swap_matrix(side)
    count = partner_ref.shape[1]
    square = (count, count)
    row = iota(square, 0)
    col = iota(square, 1)
    slot = row - row % 2 + jnp.broadcast_to(core_ref[:1, :count], square)
    copies[0].wait()
    partner = jnp.broadcast_to(partner_ref[...], square)
    place, _, _ = order_of(partner, row, col)
    hit = jnp.broadcast_to(place, square) == slot
    for which in range(2):
        pick_ref[which] = jnp.where(hit & (row % 2 == which), 1.0, 0.0).astype(BF16)
    for copy in copies[1:]:
        copy.wait()

    @pl.when(near)
    def _():
        rest.wait()


def plan(near, core, amp, partner, three_index, side):
    count = partner.shape[0]
    return pl.pallas_call(
        lambda *refs: plan_kernel(*refs, side=side),
        in_specs=[SMEM_SPEC, VMEM_SPEC] + [HBM_SPEC] * 3,
        out_specs=[VMEM_SPEC] * 4,
        out_shape=[
            jax.ShapeDtypeStruct((2, count, count), BF16),
            jax.ShapeDtypeStruct(amp.shape, BF16),
            jax.ShapeDtypeStruct((NEAR_HEAD,) + three_index.shape[1:], BF16),
            jax.ShapeDtypeStruct((side * side, side * side), BF16),
        ],
        scratch_shapes=[pltpu.VMEM((1, count), jnp.int32), pltpu.SemaphoreType.DMA((4,))],
        compiler_params=pltpu.CompilerParams(vmem_limit_bytes=8 << 20),
        cost_estimate=pl.CostEstimate(flops=0, bytes_accessed=2 << 20, transcendentals=0),
        name="plan",
    )(
        near,
        jnp.full((8, 128), core, jnp.int32),
        in_hbm(amp),
        in_hbm(partner.reshape(1, count)),
        in_hbm(three_index),
    )


def book_kernel(
    group_ref, core_ref, own_ref, partner_hbm, owner_hbm, energy_hbm, virt_hbm, info_ref, base_ref, factor_ref, partner_ref, owner_ref, energy_ref, virt_ref, sems, *, capacity
):
    sources = (partner_hbm, owner_hbm, energy_hbm, virt_hbm)
    targets = (partner_ref, owner_ref, energy_ref, virt_ref)
    copies = [pltpu.make_async_copy(a, b, sems.at[i]) for i, (a, b) in enumerate(zip(sources, targets))]
    for copy in copies:
        copy.start()
    count = partner_ref.shape[1]
    virt = virt_ref.shape[1]
    square = (count, count)
    small = (8, count)
    wide = (8, 128)
    group = group_ref[...]
    row = iota(square, 0)
    col = iota(square, 1)
    for copy in copies:
        copy.wait()
    partner = jnp.broadcast_to(partner_ref[...], square)
    owner = jnp.broadcast_to(owner_ref[...], square)
    place, leaders, down = order_of(partner, row, col)
    slot_rank = jnp.sum(((down(owner) == owner) & (row < col)).astype(jnp.int32), axis=0, keepdims=True)
    position = owner_ref[...] * capacity + slot_rank
    my_group = jnp.broadcast_to(group[:1, :count], small)
    mine = jnp.broadcast_to(position, small) == iota(small, 0) + capacity * my_group
    found = jnp.sum(jnp.where(mine, jnp.broadcast_to(place + 1, small), 0), axis=1, keepdims=True)
    chosen = jnp.broadcast_to(place, small) == iota(small, 0) + 2 * my_group
    energy = jnp.sum(jnp.where(chosen, jnp.broadcast_to(energy_ref[...], small), 0.0), axis=1, keepdims=True)
    same = jnp.where(group >= jnp.broadcast_to(leaders, wide), 1.0, 0.0)
    info_ref[0] = jnp.where(iota(wide, 0) == 2, same, jnp.broadcast_to(energy, wide))
    info_ref[1] = jnp.broadcast_to(found, wide).astype(F32)
    rows_of = jnp.broadcast_to(virt_ref[...], (virt, virt))
    sums = rows_of + rows_of.T
    on_first = jnp.broadcast_to(core_ref[:1, :1] == 0, (1, 1))
    first, second = info_ref[0, 0:1, 0:1], info_ref[0, 1:2, 0:1]
    alone = jnp.broadcast_to(info_ref[0, 2:3, 0:1] > 0.5, own_ref.shape)
    own = own_ref[...] / (sums - jnp.where(on_first, first, second))
    base_ref[...] = own.T + jnp.where(alone, own, 0.0)
    factor_ref[...] = jnp.where(alone, 0.0, 1.0 / (sums - jnp.where(on_first, second, first)))


def book(group, core, own, partner, owner, pair_energy, virt_energy, capacity):
    count = partner.shape[0]
    virt = virt_energy.shape[0]
    return pl.pallas_call(
        lambda *refs: book_kernel(*refs, capacity=capacity),
        in_specs=[VMEM_SPEC] * 3 + [HBM_SPEC] * 4,
        out_specs=[VMEM_SPEC] * 3,
        out_shape=[
            jax.ShapeDtypeStruct((2, 8, 128), F32),
            jax.ShapeDtypeStruct((virt, virt), F32),
            jax.ShapeDtypeStruct((virt, virt), F32),
        ],
        scratch_shapes=[
            pltpu.VMEM((1, count), jnp.int32),
            pltpu.VMEM((1, count), jnp.int32),
            pltpu.VMEM((1, count), F32),
            pltpu.VMEM((1, virt), F32),
            pltpu.SemaphoreType.DMA((4,)),
        ],
        compiler_params=pltpu.CompilerParams(vmem_limit_bytes=8 << 20),
        cost_estimate=pl.CostEstimate(flops=0, bytes_accessed=1 << 20, transcendentals=0),
        name="book",
    )(
        jnp.full((8, 128), group, jnp.int32),
        jnp.full((8, 128), core, jnp.int32),
        own,
        in_hbm(partner.reshape(1, count)),
        in_hbm(owner.reshape(1, count)),
        in_hbm(pair_energy.reshape(1, count)),
        in_hbm(virt_energy.reshape(1, virt)),
    )


def pack_kernel(pick_ref, own_ref, other_ref, swap_ref, out_ref):
    tiles = lax.dot_general(pick_ref[0], own_ref[...], NT, preferred_element_type=F32)
    tiles += lax.dot_general(pick_ref[1], other_ref[...], NT, preferred_element_type=F32)
    out_ref[...] = jnp.dot(tiles.astype(BF16), swap_ref[...], preferred_element_type=F32).astype(BF16)


def pack(pick, own, other, lanes):
    return pl.pallas_call(
        pack_kernel,
        in_specs=[VMEM_SPEC] * 4,
        out_specs=VMEM_SPEC,
        out_shape=jax.ShapeDtypeStruct((pick.shape[1], own.shape[0]), BF16),
        compiler_params=pltpu.CompilerParams(vmem_limit_bytes=8 << 20),
        name="pack",
    )(pick, own, other, lanes)


def ladder_kernel(
    near_ref, core_ref, tiles_ref, own_ref, swap_ref, own_hbm, other_hbm, out_ref, turned, rest_ref, other_ref, sems, *, side
):
    near = near_ref[0] > 0
    naux, virt, _ = other_ref.shape
    skipped = NEAR_HEAD - FAR_HEAD
    tail = pl.ds(skipped, naux - NEAR_HEAD)
    middle = pltpu.make_async_copy(own_hbm.at[pl.ds(FAR_HEAD, skipped)], rest_ref.at[pl.ds(0, skipped)], sems.at[0])
    rest = pltpu.make_async_copy(own_hbm.at[pl.ds(NEAR_HEAD, naux - NEAR_HEAD)], rest_ref.at[tail], sems.at[1])
    fetch = pltpu.make_async_copy(other_hbm, other_ref, sems.at[2])

    @pl.when(jnp.logical_not(near))
    def _():
        middle.start()

    rest.start()
    fetch.start()
    half_lanes = virt // 2
    per_vector = half_lanes // side
    first_core = jnp.broadcast_to(core_ref[:1, :] == 0, (side, half_lanes))

    def piece(z, core, half):
        rows = pl.ds(z * side, side)
        lanes = pl.ds(half * half_lanes, half_lanes)
        own = tiles_ref[0, rows, lanes]
        other = tiles_ref[1, rows, lanes]
        return jnp.where(first_core, own, other) if core == 0 else jnp.where(first_core, other, own)

    order = [(half, high) for half in range(2) for high in range(2)]
    vectors = []
    for low in range(per_vector):
        z_low, core = low // 2, low % 2
        vectors.append(
            jnp.concatenate([piece(high * (per_vector // 2) + z_low, core, half) for half, high in order], axis=0)
        )
    lane_group = iota(vectors[0].shape, 1) // side
    step = 1
    while step < per_vector:
        keep = (lane_group & step) == 0
        shift = step * side
        for i in range(per_vector):
            if i & step:
                continue
            j = i | step
            a, b = vectors[i], vectors[j]
            vectors[i] = jnp.where(keep, a, pltpu.roll(b, shift, 1))
            vectors[j] = jnp.where(keep, pltpu.roll(a, half_lanes - shift, 1), b)
        step *= 2
    for s_low in range(per_vector):
        for k, (half, high) in enumerate(order):
            rows = pl.ds((half * per_vector + s_low) * side, side)
            lanes = pl.ds(high * half_lanes, half_lanes)
            turned[rows, lanes] = vectors[s_low][k * side : (k + 1) * side]
    amp_t = jnp.dot(swap_ref[...], turned[...], preferred_element_type=F32).astype(BF16)

    def run(blocks):
        total = jnp.zeros((virt, virt), F32)
        for block, copies in blocks:
            for copy in copies:
                copy.wait()
            count = block.shape[0]
            rows = block[...].reshape(count * virt, virt)
            product = jnp.dot(rows, amp_t, preferred_element_type=F32).astype(BF16)
            for q in range(count):
                total += lax.dot_general(
                    product[q * virt : (q + 1) * virt], block[q], NT, preferred_element_type=F32
                )
        out_ref[...] = total

    @pl.when(near)
    def _():
        run(((own_ref, ()), (rest_ref.at[tail], (rest,)), (other_ref, (fetch,))))

    @pl.when(jnp.logical_not(near))
    def _():
        run(
            (
                (own_ref.at[pl.ds(0, FAR_HEAD)], ()),
                (rest_ref.at[pl.ds(0, skipped)], (middle,)),
                (rest_ref.at[tail], (rest,)),
                (other_ref, (fetch,)),
            )
        )


def ladder(near, core, tiles, own, lanes, three_index, three_other, side):
    naux, virt, _ = three_index.shape
    return pl.pallas_call(
        lambda *refs: ladder_kernel(*refs, side=side),
        in_specs=[SMEM_SPEC] + [VMEM_SPEC] * 4 + [HBM_SPEC] * 2,
        out_specs=VMEM_SPEC,
        out_shape=jax.ShapeDtypeStruct((virt, virt), F32),
        scratch_shapes=[
            pltpu.VMEM((virt, virt), BF16),
            pltpu.VMEM((naux - FAR_HEAD, virt, virt), BF16),
            pltpu.VMEM((naux, virt, virt), BF16),
            pltpu.SemaphoreType.DMA((3,)),
        ],
        compiler_params=pltpu.CompilerParams(vmem_limit_bytes=40 << 20),
        name="ladder",
    )(
        near,
        jnp.full((8, 128), core, jnp.int32),
        tiles,
        own,
        lanes,
        in_hbm(three_index),
        in_hbm(three_other),
    )


def merge_kernel(base_ref, factor_ref, other_ref, out_ref):
    total = base_ref[...] + other_ref[...] * factor_ref[...]
    out_ref[...] = total.astype(BF16).reshape(out_ref.shape)


def merge(base, factor, other, aux):
    virt = base.shape[0]
    return pl.pallas_call(
        merge_kernel,
        in_specs=[VMEM_SPEC] * 3,
        out_specs=VMEM_SPEC,
        out_shape=jax.ShapeDtypeStruct((aux, virt // aux, virt), BF16),
        compiler_params=pltpu.CompilerParams(vmem_limit_bytes=8 << 20),
        name="merge",
    )(base, factor, other)


def gather_kernel(shares_ref, out_ref):
    for core in range(2):
        total = shares_ref[core].astype(F32)
        for k in range(core + 2, shares_ref.shape[0], 2):
            total += shares_ref[k].astype(F32)
        done = total.astype(BF16)
        for k in range(out_ref.shape[0]):
            out_ref[k, core] = done


def gather(shares, groups):
    return pl.pallas_call(
        gather_kernel,
        in_specs=[VMEM_SPEC],
        out_specs=VMEM_SPEC,
        out_shape=jax.ShapeDtypeStruct((groups, 2) + shares.shape[1:], BF16),
        compiler_params=pltpu.CompilerParams(vmem_limit_bytes=8 << 20),
        name="gather",
    )(shares)


def select_kernel(info_ref, found_ref, out_ref):
    for k in range(out_ref.shape[0]):
        index = info_ref[1, k, 0].astype(jnp.int32)
        block = found_ref[jnp.maximum(index - 1, 0)].astype(F32)
        out_ref[k] = jnp.where(index > 0, block, 0.0)


def select(info, found, capacity):
    return pl.pallas_call(
        select_kernel,
        in_specs=[VMEM_SPEC] * 2,
        out_specs=VMEM_SPEC,
        out_shape=jax.ShapeDtypeStruct((capacity,) + found.shape[1:], F32),
        compiler_params=pltpu.CompilerParams(vmem_limit_bytes=8 << 20),
        name="select",
    )(info, found)


def per_device(amplitudes, three_index, virt_energy, pair_energy, owner, partner):
    aux_axes = ("z", "core")
    swap = [(0, 1), (1, 0)]
    aux = lax.axis_size(aux_axes)
    depth = lax.axis_size("z")
    groups = lax.axis_size("pairs")
    core = lax.axis_index("core")
    pairs_all, side, _ = amplitudes.shape
    virt = three_index.shape[1]
    capacity = 2 * (pairs_all // groups)
    near = (lax.axis_index("z") < depth // 2).astype(jnp.int32).reshape(1)
    amp = jnp.transpose(amplitudes, (1, 2, 0)).reshape(side * side, pairs_all)
    amp_other = lax.ppermute(amp, "core", swap)
    three_other = lax.ppermute(three_index, "core", swap)
    pick, amp_own, own, lanes = plan(near, core, amp, partner, three_index, side)
    tiles = pack(pick, amp_own, amp_other, lanes)
    outgoing = jnp.broadcast_to(
        tiles.reshape(1, groups, 2, side * side), (depth, groups, 2, side * side)
    ).reshape(depth * groups, 2, side * side)
    arrived = lax.all_to_all(outgoing, ("z", "pairs"), split_axis=0, concat_axis=0, tiled=True)
    arrived = jnp.transpose(arrived, (1, 0, 2))
    turned = ladder(near, core, arrived, own, lanes, three_index, three_other, side)
    traded = lax.ppermute(turned, "core", swap)
    info, base, factor = book(lax.axis_index("pairs"), core, turned, partner, owner, pair_energy, virt_energy, capacity)
    partial = merge(base, factor, traded, aux)
    shares = lax.all_to_all(partial, aux_axes, split_axis=0, concat_axis=0, tiled=True)
    spread = gather(shares, groups)
    found = lax.all_to_all(spread, "pairs", split_axis=0, concat_axis=0, tiled=True)
    return select(info, found.reshape(pairs_all, side, virt), capacity)


def solution(mesh):
    groups = mesh.shape["pairs"]
    devices = mesh.devices.reshape(mesh.shape["aux"] // 2, 2, groups)
    split = Mesh(devices, ("z", "core", "pairs"))
    aux = ("z", "core")
    placed = (P(None, aux, "pairs"), P(aux, None, None), P(), P(), P(), P())
    return jax.shard_map(
        per_device, mesh=split, in_specs=placed, out_specs=P("pairs", aux, None), check_vma=False
    )
```
